32 devices in a mesh: utt: 8 (over z, y), sp: 4 (over x, core).
Axes of the slice: x: 2, y: 2, z: 4, core: 2. Of those that a mesh axis runs over, the one named last changes fastest.
Arguments:
- frames: bfloat16 [8192, 1024], P(('utt', 'sp')), may hold values from -6 to 6
- skip_frames: bfloat16 [8192, 1024], P(('utt', 'sp')), may hold values from -6 to 6
- lengths: int32 [8, 3], P('utt'), may hold values from 1 to 768, 1024 in all within a row
- flow_time: float32 [8, 3], P('utt'), may hold values from 0 to 1
- skip_weight: bfloat16 [2048, 1024], P(('utt', 'sp')), may hold values from -0.125 to 0.125
- adaln_weight: bfloat16 [1024, 6144], P(('utt', 'sp')), may hold values from -0.1875 to 0.1875
- adaln_bias: bfloat16 [6144], P(('utt', 'sp')), may hold values from -3 to 3
- qkv_weight: bfloat16 [1024, 3072], P(('utt', 'sp')), may hold values from -0.1875 to 0.1875
- qkv_bias: bfloat16 [3072], P(('utt', 'sp')), may hold values from -3 to 3
- output_weight: bfloat16 [1024, 1024], P(('utt', 'sp')), may hold values from -1.5 to 1.5
- output_bias: bfloat16 [1024], P(('utt', 'sp')), may hold values from -3 to 3
- up_weight: bfloat16 [1024, 4096], P(('utt', 'sp')), may hold values from -0.1875 to 0.1875
- up_bias: bfloat16 [4096], P(('utt', 'sp')), may hold values from -3 to 3
- down_weight: bfloat16 [4096, 1024], P(('utt', 'sp')), may hold values from -0.09375 to 0.09375
- down_bias: bfloat16 [1024], P(('utt', 'sp')), may hold values from -3 to 3
- out_grad: bfloat16 [8192, 1024], P(('utt', 'sp')), may hold values from -6 to 6
Outputs:
- mixed_out: bfloat16 [8192, 1024], P(('utt', 'sp'))
- frames_grad: float32 [8192, 1024], P(('utt', 'sp'))
- skip_grad: float32 [8192, 1024], P(('utt', 'sp'))
- skip_weight_grad: float32 [2048, 1024], P(('utt', 'sp'))
- adaln_weight_grad: float32 [1024, 6144], P(('utt', 'sp'))
- adaln_bias_grad: float32 [6144], P(('utt', 'sp'))
- qkv_weight_grad: float32 [1024, 3072], P(('utt', 'sp'))
- qkv_bias_grad: float32 [3072], P(('utt', 'sp'))
- output_weight_grad: float32 [1024, 1024], P(('utt', 'sp'))
- output_bias_grad: float32 [1024], P(('utt', 'sp'))
- up_weight_grad: float32 [1024, 4096], P(('utt', 'sp'))
- up_bias_grad: float32 [4096], P(('utt', 'sp'))
- down_weight_grad: float32 [4096, 1024], P(('utt', 'sp'))
- down_bias_grad: float32 [1024], P(('utt', 'sp'))
The draws below stay inside these ranges and needn't reach their ends.
Inputs may be any that keep to these rules, and one draw needn't show every extreme that they name: lengths[g] holds the frame counts of the 3 utterances packed in order into group g's 1024 rows; they sum to 1024, and the largest of every row is exactly 768.
All inputs are finite; a program needn't handle non-finite values.
Results may differ from the reference program's by a relative error of at most 0.015.
Values may be sent and summed in bfloat16 or wider, within the bound.
No kernel may reach another device: no remote copies, remote signals or barrier semaphores. Data moves between devices by JAX's collectives and lax.ppermute only.
A program may use at most 256 MiB of HBM per device.

```python
import math
import jax
import jax.numpy as jnp
import numpy as np
from jax import lax

D = 1024
FF = 4096
HD = 64
UPG = 3
GROUP_FR = 1024
LONGEST = 768
GROUPS = 8
TOKENS = 8192


def steps_of(key, shape, cuts, least, largest):
    level = 1.0
    for dim, blocks in cuts:
        draws = jax.random.uniform(jax.random.fold_in(jax.random.fold_in(key, 6), dim), (blocks,), jnp.float32, least / len(cuts), largest / len(cuts))
        level = level * jnp.repeat(jnp.exp(draws), shape[dim] // blocks).reshape((-1,) + (1,) * (len(shape) - 1 - dim))
    return level


def split_up(amount, total, bound, lean):
    loads = [(1 << 20) // math.isqrt(standing ** lean) + 1 for standing in range(2, amount + 1)]
    surplus, counts = total - bound - (amount - 1), [1] * (amount - 1)
    while surplus > 0:
        candidates = [i for i in range(amount - 1) if counts[i] < bound]
        mass, left = sum([loads[i] for i in candidates]), surplus
        for i in candidates:
            addition = min(bound - counts[i], max(1, left * loads[i] // mass), surplus)
            counts[i] = counts[i] + addition
            surplus = surplus - addition
    return np.array([bound] + counts)


def ragged_sizes(own_key, number_of, total, bound, skew):
    if number_of == 2:
        one = jax.random.randint(own_key, (), max(1, total - bound), min(bound, total - 1) + 1)
        return jnp.stack([one, total - one])
    sizes = jnp.asarray(split_up(number_of, total, bound, skew), jnp.int32)
    twos = (number_of - 1) // 2
    source_of, receiver = sizes[1:1 + 2 * twos:2], sizes[2:2 + 2 * twos:2]
    slack = jnp.minimum(source_of - 1, bound - receiver)
    moved = jax.random.randint(jax.random.fold_in(own_key, 1), (twos,), 0, 1 << 20) % (slack + 1)
    sizes = sizes.at[1:1 + 2 * twos:2].set(source_of - moved).at[2:2 + 2 * twos:2].set(receiver + moved)
    return sizes[jax.random.permutation(jax.random.fold_in(own_key, 2), number_of)]


def centred(rng, extent, scale, limit, cuts=(), held_as=jnp.bfloat16):
    values = scale * jax.random.normal(rng, extent, jnp.float32)
    if cuts:
        values = values * steps_of(rng, extent, cuts, -0.22, 0.18)
    return jnp.clip(values, -limit, limit).astype(held_as)


def setup_inputs(seed: int = 0) -> dict:
    seeds = jax.random.split(jax.random.key(seed), 17)
    frames = centred(seeds[0], (TOKENS, D), 1.0, 6.0, ((0, 32),))
    skip_frames = centred(seeds[1], (TOKENS, D), 1.0, 6.0, ((0, 32),))
    lengths = jax.vmap(lambda own: ragged_sizes(own, UPG, GROUP_FR, LONGEST, 2))(jax.random.split(seeds[2], GROUPS)).reshape((GROUPS, UPG)).astype(jnp.int32)
    flow_time = jnp.clip(1.0 * jax.random.uniform(seeds[3], (GROUPS, UPG), jnp.float32) ** steps_of(seeds[3], (GROUPS, UPG), ((0, 8),), -0.2, 0.2), 0.0, 1.0)
    skip_weight = centred(seeds[4], (2 * D, D), (2 * D) ** -0.5, 0.125, ((0, 32),))
    adaln_weight = centred(seeds[5], (D, 6 * D), D ** -0.5, 0.1875, ((0, 32),))
    adaln_bias = centred(seeds[6], (6 * D,), 0.5, 3.0, ((0, 32),))
    qkv_weight = centred(seeds[7], (D, 3 * D), D ** -0.5, 0.1875, ((0, 32),))
    qkv_bias = centred(seeds[8], (3 * D,), 0.5, 3.0, ((0, 32),))
    output_weight = centred(seeds[9], (D, D), (D // 64) ** -0.5, 1.5, ((0, 32),))
    output_bias = centred(seeds[10], (D,), 0.5, 3.0, ((0, 32),))
    up_weight = centred(seeds[11], (D, FF), D ** -0.5, 0.1875, ((0, 32),))
    up_bias = centred(seeds[12], (FF,), 0.5, 3.0, ((0, 32),))
    down_weight = centred(seeds[13], (FF, D), FF ** -0.5, 0.09375, ((0, 32),))
    down_bias = centred(seeds[14], (D,), 0.5, 3.0, ((0, 32),))
    out_grad = centred(seeds[15], (TOKENS, D), 1.0, 6.0, ((0, 32),))
    return dict(frames=frames, skip_frames=skip_frames, lengths=lengths, flow_time=flow_time, skip_weight=skip_weight, adaln_weight=adaln_weight, adaln_bias=adaln_bias, qkv_weight=qkv_weight, qkv_bias=qkv_bias, output_weight=output_weight, output_bias=output_bias, up_weight=up_weight, up_bias=up_bias, down_weight=down_weight, down_bias=down_bias, out_grad=out_grad)


highest_precision = lax.Precision.HIGHEST
mask_value = -1e+30

@jax.custom_vjp
def low(v):
    return lax.optimization_barrier(v.astype(jnp.bfloat16)).astype(jnp.float32)

@jax.custom_vjp
def low_back(v):
    return v

def low_keep(v):
    return (low(v), None)

def low_pass(kept, grad):
    return (grad,)

def back_keep(v):
    return (v, None)

def back_low(kept, grad):
    return (low(grad),)
low.defvjp(low_keep, low_pass)
low_back.defvjp(back_keep, back_low)

def dot_high(left, right):
    return jnp.dot(left, right, precision=highest_precision, preferred_element_type=jnp.float32)

def layer_norm(values):
    mean_row = lax.optimization_barrier(jnp.mean(values, axis=-1, keepdims=True))
    centered = values - mean_row
    variance = lax.optimization_barrier(jnp.mean(centered * centered, axis=-1, keepdims=True))
    return centered * lax.rsqrt(variance + 1e-06)

def time_features(flow_row, model_width):
    half_width = model_width // 2
    steps_row = jnp.arange(half_width, dtype=jnp.float32)
    frequency = jnp.exp(steps_row * (-math.log(10000.0) / (half_width - 1)))
    phase_arg = 1000.0 * flow_row[:, None] * frequency[None, :]
    return jnp.concatenate([jnp.sin(phase_arg), jnp.cos(phase_arg)], axis=1)

def rotary(values, position, head_size, direction):
    row_count = values.shape[0]
    col_count = values.shape[1]
    half_head = head_size // 2
    head_count = col_count // head_size
    inverse = jnp.exp(jnp.arange(half_head, dtype=jnp.float32) * (-2.0 * math.log(10000.0) / head_size))
    angle_arg = position.astype(jnp.float32)[:, None] * inverse[None, :]
    cosine = jnp.cos(angle_arg)
    sine_row = jnp.sin(angle_arg) * direction
    cos_full = jnp.tile(jnp.concatenate([cosine, cosine], axis=1), (1, head_count))
    sin_full = jnp.tile(jnp.concatenate([-sine_row, sine_row], axis=1), (1, head_count))
    halves = values.reshape(row_count, head_count, 2, half_head)
    swapped = jnp.concatenate([halves[:, :, 1:], halves[:, :, :1]], axis=2).reshape(row_count, col_count)
    return values * cos_full + swapped * sin_full

def utterance_layout(lengths_row, first_row, row_count):
    ends_at = jnp.cumsum(lengths_row).astype(jnp.int32)
    starts_at = (ends_at - lengths_row).astype(jnp.int32)
    frame_ids = (first_row + jnp.arange(row_count, dtype=jnp.int32)).astype(jnp.int32)
    inside = (frame_ids[:, None] >= starts_at[None, :]) & (frame_ids[:, None] < ends_at[None, :])
    segment = lax.optimization_barrier(jnp.sum(jnp.where(frame_ids[:, None] >= ends_at[None, :], 1, 0), axis=1)).astype(jnp.int32)
    position = (frame_ids - lax.optimization_barrier(jnp.sum(jnp.where(inside, starts_at[None, :], 0), axis=1))).astype(jnp.int32)
    return (inside, segment, position)

def block_rows(total_rows):
    return 512 if total_rows % 512 == 0 else total_rows

def attention(query_rows, key_rows, value_rows, segment):
    row_count = query_rows.shape[0]
    block_size = block_rows(row_count)
    head_count = query_rows.shape[1] // HD
    keys_all = key_rows.reshape(row_count, head_count, HD)
    values_all = value_rows.reshape(row_count, head_count, HD)
    score_scale = HD ** (-0.5)

    def one_block(query_block, segment_block):
        scores = low_back(jnp.einsum('qhd,khd->hqk', query_block, keys_all, precision=highest_precision) * score_scale)
        same_seg = segment_block[:, None] == segment[None, :]
        masked = jnp.where(same_seg[None], scores, mask_value)
        shifted = masked - lax.optimization_barrier(jnp.max(masked, axis=-1, keepdims=True))
        exp_rows = jnp.exp(shifted)
        prob_rows = exp_rows / lax.optimization_barrier(jnp.sum(exp_rows, axis=-1, keepdims=True))
        return jnp.einsum('hqk,khd->qhd', low(prob_rows), values_all, precision=highest_precision)
    checked = jax.checkpoint(one_block)
    blocks = lax.map(lambda pieces: checked(pieces[0], pieces[1]), (query_rows.reshape(row_count // block_size, block_size, head_count, HD), segment.reshape(row_count // block_size, block_size)))
    return blocks.reshape(row_count, head_count * HD)

def group_forward(frames_group, skip_group, lengths_row, flow_row, weights):
    skip_weight, adaln_weight, adaln_bias, qkv_weight, qkv_bias, output_weight, output_bias, up_weight, up_bias, down_weight, down_bias = weights
    row_count = frames_group.shape[0]
    inside, segment, position = utterance_layout(lengths_row, 0, row_count)
    onehot = inside.astype(jnp.float32)
    silu_time = low(jax.nn.silu(time_features(flow_row, D)))
    mod_table = dot_high(silu_time, adaln_weight) + adaln_bias[None, :]
    modulation = dot_high(onehot, mod_table)
    shift_attn, scale_attn, gate_attn, shift_ffn, scale_ffn, gate_ffn = jnp.split(modulation, 6, axis=1)
    joined = jnp.concatenate([frames_group, skip_group], axis=1)
    base_rows = low_back(dot_high(joined, skip_weight))
    normed = low(layer_norm(base_rows) * (1.0 + scale_attn) + shift_attn)
    projected = low_back(dot_high(normed, qkv_weight) + qkv_bias[None, :])
    query_rows = low(low_back(rotary(projected[:, :D], position, HD, 1.0)))
    key_rows = low(low_back(rotary(projected[:, D:2 * D], position, HD, 1.0)))
    value_rows = low(low_back(projected[:, 2 * D:]))
    attended = low(low_back(attention(query_rows, key_rows, value_rows, segment)))
    branch = low_back(dot_high(attended, output_weight) + output_bias[None, :])
    middle = base_rows + gate_attn * branch
    normed_ffn = low(layer_norm(middle) * (1.0 + scale_ffn) + shift_ffn)
    hidden = low_back(dot_high(normed_ffn, up_weight) + up_bias[None, :])
    active = low(jax.nn.gelu(hidden, approximate=True))
    result = low_back(dot_high(active, down_weight) + down_bias[None, :])
    return middle + gate_ffn * result

def reference(frames, skip_frames, lengths, flow_time, skip_weight, adaln_weight, adaln_bias, qkv_weight, qkv_bias, output_weight, output_bias, up_weight, up_bias, down_weight, down_bias, out_grad):
    widened = [array_in.astype(jnp.float32) for array_in in (frames, skip_frames, skip_weight, adaln_weight, adaln_bias, qkv_weight, qkv_bias, output_weight, output_bias, up_weight, up_bias, down_weight, down_bias)]

    def forward(frames_wide, skip_wide, *weights):

        def one_group(pieces):
            return jax.checkpoint(group_forward)(pieces[0], pieces[1], pieces[2], pieces[3], weights)
        outputs = lax.map(one_group, (frames_wide.reshape(GROUPS, GROUP_FR, D), skip_wide.reshape(GROUPS, GROUP_FR, D), lengths, flow_time))
        return outputs.reshape(TOKENS, D)
    mixed_wide, pull_back = jax.vjp(forward, *widened)
    gradients = pull_back(out_grad.astype(jnp.float32))
    return (mixed_wide.astype(jnp.bfloat16), gradients[0], gradients[1], gradients[2], gradients[3], gradients[4], gradients[5], gradients[6], gradients[7], gradients[8], gradients[9], gradients[10], gradients[11], gradients[12])
```

```python
import math

import jax
import jax.numpy as jnp
from jax import lax
from jax.sharding import PartitionSpec as P

HD = 64
LANES = 128
BF = jnp.bfloat16
F32 = jnp.float32
highest_precision = lax.Precision.HIGHEST
mask_value = -1e30


def dot32(left, right):
    return jnp.dot(left, right, preferred_element_type=F32)


def dot_nt(left, right):
    return lax.dot_general(left, right, (((1,), (1,)), ((), ())), preferred_element_type=F32)


def dot_tn(left, right):
    return lax.dot_general(left, right, (((0,), (0,)), ((), ())), preferred_element_type=F32)


def xor_sp(values, distance):
    size = lax.axis_size("sp")
    return lax.ppermute(values, "sp", [(i, i ^ distance) for i in range(size)])


def gather_sp(own):
    size = lax.axis_size("sp")
    blocks = {0: own}
    step = size // 2
    while step >= 1:
        for d in list(blocks):
            blocks[d ^ step] = xor_sp(blocks[d], step)
        step //= 2
    return [blocks[d] for d in range(size)]


def reduce_sp(parts):
    size = lax.axis_size("sp")
    sums = {d: parts[d] for d in range(size)}
    step = 1
    while step < size:
        kept = {}
        for d in sums:
            if d & step == 0:
                arrived = xor_sp(sums[d ^ step].astype(BF), step).astype(F32)
                kept[d] = sums[d] + arrived
        sums = kept
        step *= 2
    return sums[0]


def exchange_sp(parts):
    return [parts[0]] + [xor_sp(parts[d], d) for d in range(1, len(parts))]


def in_device_order(blocks):
    stacked = jnp.stack(blocks)
    me = lax.axis_index("sp")
    return [
        lax.dynamic_index_in_dim(stacked, me ^ a, 0, keepdims=False) for a in range(len(blocks))
    ]


def sum_sp(values):
    size = lax.axis_size("sp")
    step = size // 2
    while step >= 1:
        values = values + xor_sp(values, step)
        step //= 2
    return values


def high_groups():
    high = lax.axis_size("utt") // 2
    return [[z * 2 + y for z in range(high)] for y in range(2)]


def low_partner():
    return [(i, i ^ 1) for i in range(lax.axis_size("utt"))]


def gather_utt(own):
    size = lax.axis_size("utt")
    high = size // 2
    tiled = jnp.broadcast_to(own[None], (high,) + own.shape)
    line = lax.all_to_all(
        tiled, "utt", 0, 0, axis_index_groups=high_groups(), tiled=True
    )
    other = lax.ppermute(line, "utt", low_partner())
    first = lax.axis_index("utt") % 2 == 0
    both = jnp.stack([jnp.where(first, line, other), jnp.where(first, other, line)], axis=1)
    return both.reshape((size,) + own.shape)


def scatter_utt(parts):
    size = lax.axis_size("utt")
    high = size // 2
    low = lax.axis_index("utt") % 2
    pairs = parts.reshape((high, 2) + parts.shape[1:])
    keep = lax.dynamic_index_in_dim(pairs, low, 1, keepdims=False)
    send = lax.dynamic_index_in_dim(pairs, 1 - low, 1, keepdims=False)
    arrived = lax.ppermute(send.astype(BF), "utt", low_partner())
    half = (keep.astype(F32) + arrived.astype(F32)).astype(BF)
    pieces = lax.all_to_all(half, "utt", 0, 0, axis_index_groups=high_groups(), tiled=True)
    return jnp.sum(pieces.astype(F32), axis=0)


def to_owner(values):
    n_u, n_s = lax.axis_size("utt"), lax.axis_size("sp")
    routes = []
    for p in range(n_u):
        for s in range(n_s):
            routes.append((p * n_s + s, s * n_u + p))
    return lax.ppermute(values, ("utt", "sp"), routes)


def owned(values):
    n = lax.axis_size("utt") * lax.axis_size("sp")
    j = lax.axis_index("utt") * lax.axis_size("sp") + lax.axis_index("sp")
    size = values.shape[-1] // n
    return lax.dynamic_slice_in_dim(values, j * size, size, values.ndim - 1)


def norm_parts(values):
    mean_row = jnp.mean(values, axis=-1, keepdims=True)
    centered = values - mean_row
    variance = jnp.mean(centered * centered, axis=-1, keepdims=True)
    scale = lax.rsqrt(variance + 1e-06)
    return centered * scale, scale


def norm_back(normal, scale, grads):
    mean_grad = jnp.mean(grads, axis=-1, keepdims=True)
    mean_both = jnp.mean(grads * normal, axis=-1, keepdims=True)
    return (grads - mean_grad - normal * mean_both) * scale


def gelu_tanh(values):
    return jax.nn.gelu(values, approximate=True)


def rotary(values, position, direction):
    row_count, col_count = values.shape
    half_head = HD // 2
    head_count = col_count // HD
    inverse = jnp.exp(jnp.arange(half_head, dtype=F32) * (-2.0 * math.log(10000.0) / HD))
    angle_arg = position.astype(F32)[:, None] * inverse[None, :]
    cosine = jnp.cos(angle_arg)
    sine_row = jnp.sin(angle_arg) * direction
    cos_full = jnp.tile(jnp.concatenate([cosine, cosine], axis=1), (1, head_count))
    sin_full = jnp.tile(jnp.concatenate([-sine_row, sine_row], axis=1), (1, head_count))
    first = (jnp.arange(col_count) % HD < half_head)[None, :]
    swapped = jnp.where(
        first, jnp.roll(values, -half_head, axis=1), jnp.roll(values, half_head, axis=1)
    )
    return values * cos_full + swapped * sin_full


def utterance_layout(lengths_row, frame_ids):
    ends_at = jnp.cumsum(lengths_row)
    starts_at = ends_at - lengths_row
    inside = (frame_ids[:, None] >= starts_at[None, :]) & (frame_ids[:, None] < ends_at[None, :])
    segment = jnp.sum(jnp.where(frame_ids[:, None] >= ends_at[None, :], 1, 0), axis=1).astype(
        jnp.int32
    )
    position = frame_ids - jnp.sum(jnp.where(inside, starts_at[None, :], 0), axis=1)
    return inside, segment, position


def block_rows():
    return 512


def head_scores(query_block, keys_all, segment_block, segment_all, score_scale):
    scores = jnp.einsum("qhd,khd->hqk", query_block, keys_all, preferred_element_type=F32)
    same_seg = segment_block[:, None] == segment_all[None, :]
    return jnp.where(same_seg[None], scores * score_scale, mask_value)


def attend(query_heads, key_heads, value_heads, segment_all):
    total_rows, col_count = query_heads.shape
    head_count = col_count // HD
    block_size = block_rows()
    block_count = total_rows // block_size
    keys_all = key_heads.reshape(total_rows, head_count, HD)
    values_all = value_heads.reshape(total_rows, head_count, HD)
    score_scale = HD ** (-0.5)

    def one_block(pieces):
        query_block, segment_block = pieces
        masked = head_scores(query_block, keys_all, segment_block, segment_all, score_scale)
        row_max = jnp.max(masked, axis=-1, keepdims=True)
        exp_rows = jnp.exp(masked - row_max)
        totals = jnp.sum(exp_rows, axis=-1, keepdims=True)
        prob_rows = (exp_rows / totals).astype(BF)
        block_out = jnp.einsum("hqk,khd->qhd", prob_rows, values_all, preferred_element_type=F32)
        return (
            block_out.astype(BF).reshape(block_size, col_count),
            (row_max + jnp.log(totals))[..., 0],
        )

    outputs, log_totals = lax.map(
        one_block,
        (
            query_heads.reshape(block_count, block_size, head_count, HD),
            segment_all.reshape(block_count, block_size),
        ),
    )
    return outputs.reshape(total_rows, col_count), log_totals


def attend_back(query_heads, key_heads, value_heads, grad_heads, log_totals, segment_all):
    total_rows, col_count = query_heads.shape
    head_count = col_count // HD
    block_size = block_rows()
    block_count = total_rows // block_size
    keys_all = key_heads.reshape(total_rows, head_count, HD)
    values_all = value_heads.reshape(total_rows, head_count, HD)
    score_scale = HD ** (-0.5)

    def one_block(carried, pieces):
        key_sum, value_sum = carried
        query_block, grad_block, log_block, segment_block = pieces
        masked = head_scores(query_block, keys_all, segment_block, segment_all, score_scale)
        prob_rows = jnp.exp(masked - log_block[:, :, None])
        grad_probs = jnp.einsum("qhd,khd->hqk", grad_block, values_all, preferred_element_type=F32)
        inner_sum = jnp.sum(prob_rows * grad_probs, axis=-1, keepdims=True)
        grad_scores = (prob_rows * (grad_probs - inner_sum)).astype(BF)
        grad_query = (
            jnp.einsum("hqk,khd->qhd", grad_scores, keys_all, preferred_element_type=F32)
            * score_scale
        )
        key_sum = (
            key_sum
            + jnp.einsum("hqk,qhd->khd", grad_scores, query_block, preferred_element_type=F32)
            * score_scale
        )
        value_sum = value_sum + jnp.einsum(
            "hqk,qhd->khd", prob_rows.astype(BF), grad_block, preferred_element_type=F32
        )
        return (key_sum, value_sum), grad_query.astype(BF).reshape(block_size, col_count)

    zero_sums = jnp.zeros((total_rows, head_count, HD), F32)
    (key_sum, value_sum), query_grads = lax.scan(
        one_block,
        (zero_sums, zero_sums),
        (
            query_heads.reshape(block_count, block_size, head_count, HD),
            grad_heads.reshape(block_count, block_size, head_count, HD),
            log_totals,
            segment_all.reshape(block_count, block_size),
        ),
    )
    return (
        query_grads.reshape(total_rows, col_count),
        key_sum.astype(BF).reshape(total_rows, col_count),
        value_sum.astype(BF).reshape(total_rows, col_count),
    )


def own_time_features(times, first_col, col_count, model_width):
    half_width = model_width // 2
    cols = first_col + jnp.arange(col_count, dtype=jnp.int32)
    is_sine = cols < half_width
    steps_row = jnp.where(is_sine, cols, cols - half_width).astype(F32)
    frequency = jnp.exp(steps_row * (-math.log(10000.0) / (half_width - 1)))
    phase_arg = 1000.0 * times[:, None] * frequency[None, :]
    features = jnp.where(is_sine[None, :], jnp.sin(phase_arg), jnp.cos(phase_arg))
    return jax.nn.silu(features).astype(BF)


def pad_rows(vector):
    rows = -(-vector.shape[-1] // LANES)
    return jnp.pad(vector, (0, rows * LANES - vector.shape[-1])).reshape(rows, LANES)


def body(
    frames,
    skip_frames,
    lengths,
    flow_time,
    skip_weight,
    adaln_weight,
    adaln_bias,
    qkv_weight,
    qkv_bias,
    output_weight,
    output_bias,
    up_weight,
    up_bias,
    down_weight,
    down_bias,
    out_grad,
):
    n_u, n_s = lax.axis_size("utt"), lax.axis_size("sp")
    u, s = lax.axis_index("utt"), lax.axis_index("sp")
    n_all = n_u * n_s
    me = u * n_s + s
    rows, width = frames.shape
    per_group = lengths.shape[1]
    ff = up_weight.shape[1]
    part_width = width // n_s
    part_ff = ff // n_s
    lengths_row = lengths[0]

    own_ids = s * rows + jnp.arange(rows, dtype=jnp.int32)
    inside, segment_own, _ = utterance_layout(lengths_row, own_ids)
    all_ids = jnp.concatenate(
        [(s ^ d) * rows + jnp.arange(rows, dtype=jnp.int32) for d in range(n_s)]
    )
    _, segment_all, position_all = utterance_layout(lengths_row, all_ids)

    skip_lines = gather_utt(skip_weight)
    skip_parts = in_device_order(gather_sp(skip_lines))
    full_skip = jnp.stack(skip_parts, axis=1).reshape(-1, width)

    cols = qkv_weight.shape[0]
    qkv_split = qkv_weight.reshape(cols, 3, n_s, part_width).transpose(2, 0, 1, 3)
    up_split = up_weight.reshape(cols, n_u, n_s, ff // n_all).transpose(2, 0, 1, 3)
    both_split = jnp.concatenate(
        [qkv_split.reshape(n_s, cols, 3 * part_width), up_split.reshape(n_s, cols, part_ff)], axis=2
    )
    both_mine = lax.all_to_all(both_split, "sp", 0, 0, tiled=True).reshape(n_s * cols, -1)
    my_qkv = lax.all_gather(both_mine[:, : 3 * part_width], "utt", axis=0, tiled=True)
    out_lines = gather_utt(output_weight)
    out_parts = in_device_order(gather_sp(out_lines))
    full_output = jnp.stack(out_parts, axis=1).reshape(-1, width)
    ff_bundle = jnp.concatenate([both_mine[:, 3 * part_width :], down_weight], axis=0)
    ff_lines = lax.all_gather(ff_bundle, "utt", axis=0)
    my_up = ff_lines[:, : n_s * cols].reshape(width, part_ff)
    my_down = ff_lines[:, n_s * cols :].reshape(part_ff, width)

    flow_row = jnp.pad(flow_time, ((0, 0), (0, LANES - per_group)))
    flow_tiled = jnp.broadcast_to(flow_row[None], (n_u, 1, LANES))
    all_flow = lax.all_to_all(flow_tiled, "utt", 0, 0, tiled=True)
    times = all_flow[:, 0, :per_group].reshape(n_u * per_group)
    feature_rows = adaln_weight.shape[0]
    silu_own = own_time_features(times, me * feature_rows, feature_rows, width)
    table_width = adaln_weight.shape[1]
    mod_terms = dot32(silu_own, adaln_weight)
    bias_row = lax.dynamic_update_slice(
        jnp.zeros((table_width,), F32), adaln_bias.astype(F32), (me * adaln_bias.shape[0],)
    )
    mod_terms = mod_terms + bias_row[None, :]
    table_rows = per_group * table_width // LANES
    bias_sizes = [qkv_bias.shape[0], output_bias.shape[0], up_bias.shape[0], down_bias.shape[0]]
    bias_own = pad_rows(
        jnp.concatenate([qkv_bias, output_bias, up_bias, down_bias]).astype(F32)
    )
    bias_rows = bias_own.shape[0]
    small = jnp.concatenate(
        [
            mod_terms.reshape(n_u, table_rows, LANES),
            jnp.broadcast_to(bias_own[None], (n_u, bias_rows, LANES)),
        ],
        axis=1,
    )
    small = lax.all_to_all(small, "utt", 0, 0, tiled=True)
    mod_part = jnp.sum(small[:, :table_rows], axis=0)
    bias_part = small[:, table_rows:].reshape(n_u * bias_rows, LANES)
    slots = jnp.where((jnp.arange(n_s) == s)[:, None, None], bias_part[None], 0.0)
    message = jnp.concatenate([mod_part, slots.reshape(-1, LANES)], axis=0)
    message = sum_sp(message)
    mod_table = message[:table_rows].reshape(per_group, table_width)
    bias_all = message[table_rows:].reshape(n_s, n_u, bias_rows * LANES).transpose(1, 0, 2)
    offsets = [0]
    for size in bias_sizes:
        offsets.append(offsets[-1] + size)
    full_qkv_bias, full_output_bias, full_up_bias, full_down_bias = [
        bias_all[:, :, offsets[i] : offsets[i + 1]].reshape(-1) for i in range(4)
    ]
    my_qkv_bias = lax.dynamic_slice_in_dim(
        full_qkv_bias.reshape(3, width), s * part_width, part_width, 1
    ).reshape(-1)
    my_up_bias = lax.dynamic_index_in_dim(
        full_up_bias.reshape(n_u, n_s, -1), s, 1, keepdims=False
    ).reshape(-1)

    def expand(block):
        table = mod_table[:, block * width : (block + 1) * width]
        result = table[per_group - 1][None, :]
        for k in range(per_group - 2, -1, -1):
            result = jnp.where(segment_own[:, None] == k, table[k][None, :], result)
        return result

    def segment_sums(values):
        return jnp.stack(
            [jnp.sum(jnp.where(inside[:, k][:, None], values, 0.0), axis=0) for k in range(per_group)]
        )

    shift_attn, scale_attn, gate_attn, shift_ffn, scale_ffn, gate_ffn = [expand(i) for i in range(6)]

    grad_out = out_grad.astype(F32)
    grad_result = (gate_ffn * grad_out).astype(BF)
    grad_result_all = jnp.concatenate(gather_sp(grad_result), axis=0)

    base_rows = dot32(frames, full_skip[:width]) + dot32(skip_frames, full_skip[width:])
    base_norm, base_scale = norm_parts(base_rows)
    normed = (base_norm * (1.0 + scale_attn) + shift_attn).astype(BF)
    normed_all = jnp.concatenate(gather_sp(normed), axis=0)
    projected = dot32(normed_all, my_qkv) + my_qkv_bias[None, :]
    query_rows = rotary(projected[:, :part_width], position_all, 1.0).astype(BF)
    key_rows = rotary(projected[:, part_width : 2 * part_width], position_all, 1.0).astype(BF)
    value_rows = projected[:, 2 * part_width :].astype(BF)
    attended_heads, log_totals = attend(query_rows, key_rows, value_rows, segment_all)
    arrived = exchange_sp([attended_heads[d * rows : (d + 1) * rows] for d in range(n_s)])
    attended = jnp.concatenate(in_device_order(arrived), axis=1)
    branch = dot32(attended, full_output) + full_output_bias[None, :]
    middle = base_rows + gate_attn * branch
    middle_norm, middle_scale = norm_parts(middle)
    normed_ffn = (middle_norm * (1.0 + scale_ffn) + shift_ffn).astype(BF)
    normed_ffn_all = jnp.concatenate(gather_sp(normed_ffn), axis=0)
    hidden = dot32(normed_ffn_all, my_up) + my_up_bias[None, :]
    active_wide, gelu_pull = jax.vjp(gelu_tanh, hidden)
    active = active_wide.astype(BF)

    grad_active = dot_nt(grad_result_all, my_down)
    grad_hidden = gelu_pull(grad_active)[0].astype(BF)
    grad_nffn_part = dot_nt(grad_hidden, my_up)
    grad_normed_ffn = reduce_sp([grad_nffn_part[d * rows : (d + 1) * rows] for d in range(n_s)])

    result_part = dot32(active, my_down)
    result = reduce_sp([result_part[d * rows : (d + 1) * rows] for d in range(n_s)])
    result = result + full_down_bias[None, :]
    mixed_out = (middle + gate_ffn * result).astype(BF)
    grad_gate_ffn = grad_out * result

    grad_down = dot_tn(active, grad_result_all)
    grad_up = dot_tn(normed_ffn_all, grad_hidden)
    grad_up_bias = jnp.sum(grad_hidden.astype(F32), axis=0)
    grad_down_bias = jnp.sum(grad_result.astype(F32), axis=0)
    down_sum = lax.psum_scatter(
        grad_down.astype(BF), "utt", scatter_dimension=0, tiled=True
    ).astype(F32)
    up_mine = lax.psum_scatter(grad_up.astype(BF), "utt", scatter_dimension=0, tiled=True)
    up_back = lax.all_to_all(up_mine.reshape(n_s, cols, part_ff), "sp", 0, 0, tiled=True)
    up_sum = (
        up_back.reshape(n_s, cols, n_u, ff // n_all).transpose(1, 2, 0, 3).reshape(cols, ff)
    ).astype(F32)

    grad_scale_ffn = grad_normed_ffn * middle_norm
    grad_middle = grad_out + norm_back(
        middle_norm, middle_scale, grad_normed_ffn * (1.0 + scale_ffn)
    )
    grad_gate_attn = grad_middle * branch
    grad_branch = (gate_attn * grad_middle).astype(BF)
    grad_output_bias = jnp.sum(grad_branch.astype(F32), axis=0)
    grad_branch_all = jnp.concatenate(gather_sp(grad_branch), axis=0)
    my_output = lax.dynamic_slice_in_dim(full_output, s * part_width, part_width, 0)
    grad_heads = dot_nt(grad_branch_all, my_output).astype(BF)
    grad_output = dot_tn(attended_heads, grad_branch_all)
    out_sum = to_owner(scatter_utt(grad_output.reshape(n_u, -1, width)).astype(F32))

    grad_query, grad_key, grad_value = attend_back(
        query_rows, key_rows, value_rows, grad_heads, log_totals, segment_all
    )
    grad_projected = jnp.concatenate(
        [
            rotary(grad_query.astype(F32), position_all, -1.0).astype(BF),
            rotary(grad_key.astype(F32), position_all, -1.0).astype(BF),
            grad_value,
        ],
        axis=1,
    )
    grad_normed_part = dot_nt(grad_projected, my_qkv)
    grad_normed = reduce_sp([grad_normed_part[d * rows : (d + 1) * rows] for d in range(n_s)])
    grad_qkv = dot_tn(normed_all, grad_projected)
    my_qkv_bias_grad = jnp.sum(grad_projected.astype(F32), axis=0)
    qkv_mine = scatter_utt(grad_qkv.reshape(n_u, n_s * cols, 3 * part_width))
    qkv_back = lax.all_to_all(
        qkv_mine.astype(BF).reshape(n_s, cols, 3 * part_width), "sp", 0, 0, tiled=True
    )
    qkv_sum = (
        qkv_back.reshape(n_s, cols, 3, part_width).transpose(1, 2, 0, 3).reshape(cols, 3 * width)
    ).astype(F32)

    grad_scale_attn = grad_normed * base_norm
    grad_base = (
        grad_middle + norm_back(base_norm, base_scale, grad_normed * (1.0 + scale_attn))
    ).astype(BF)
    grad_base_all = jnp.concatenate(gather_sp(grad_base), axis=0)
    part_joined = 2 * width // n_s
    joined = jnp.concatenate([frames, skip_frames], axis=1)
    joined_mine = jnp.concatenate(
        exchange_sp(
            [
                lax.dynamic_slice_in_dim(joined, (s ^ d) * part_joined, part_joined, 1)
                for d in range(n_s)
            ]
        ),
        axis=0,
    )
    grad_skip = dot_tn(joined_mine, grad_base_all)
    skip_sum = to_owner(scatter_utt(grad_skip.reshape(n_u, -1, width)).astype(F32))
    frames_grad = dot_nt(grad_base, full_skip[:width])
    skip_grad = dot_nt(grad_base, full_skip[width:])

    grad_table = jnp.concatenate(
        [
            segment_sums(v)
            for v in (
                grad_normed,
                grad_scale_attn,
                grad_gate_attn,
                grad_normed_ffn,
                grad_scale_ffn,
                grad_gate_ffn,
            )
        ],
        axis=1,
    )
    qkv_bias_slots = lax.dynamic_update_slice(
        jnp.zeros((3, width), F32), my_qkv_bias_grad.reshape(3, part_width), (0, s * part_width)
    ).reshape(-1)
    up_bias_slots = lax.dynamic_update_slice(
        jnp.zeros((n_u, n_s, ff // n_all), F32),
        grad_up_bias.reshape(n_u, 1, ff // n_all),
        (0, s, 0),
    ).reshape(-1)
    bias_vec = jnp.concatenate(
        [
            v.reshape(n_u, -1)
            for v in (qkv_bias_slots, grad_output_bias, up_bias_slots, grad_down_bias)
        ],
        axis=1,
    )
    vec_rows = -(-bias_vec.shape[1] // LANES)
    bias_vec = jnp.pad(bias_vec, ((0, 0), (0, vec_rows * LANES - bias_vec.shape[1])))
    tail = jnp.concatenate(
        [grad_table.reshape(table_rows, LANES), bias_vec.reshape(n_u * vec_rows, LANES)], axis=0
    )
    tail = sum_sp(tail)
    tail = jnp.concatenate(
        [
            jnp.broadcast_to(tail[None, :table_rows], (n_u, table_rows, LANES)),
            tail[table_rows:].reshape(n_u, vec_rows, LANES),
        ],
        axis=1,
    )
    tail = lax.all_to_all(tail, "utt", 0, 0, tiled=True)
    table_all = tail[:, :table_rows].reshape(n_u * per_group, table_width)
    adaln_sum = lax.dot_general(
        silu_own.astype(F32),
        table_all,
        (((0,), (0,)), ((), ())),
        precision=highest_precision,
        preferred_element_type=F32,
    )
    adaln_bias_sum = jnp.sum(owned(table_all), axis=0)
    vec = jnp.sum(tail[:, table_rows:], axis=0).reshape(-1)
    bias_sums, start = [], 0
    for size in bias_sizes:
        bias_sums.append(lax.dynamic_slice_in_dim(vec, start + s * size, size, 0))
        start += size * n_s

    return (
        mixed_out,
        frames_grad,
        skip_grad,
        skip_sum,
        adaln_sum,
        adaln_bias_sum,
        qkv_sum,
        bias_sums[0],
        out_sum,
        bias_sums[1],
        up_sum,
        bias_sums[2],
        down_sum,
        bias_sums[3],
    )


def solution(mesh):
    both = ("utt", "sp")
    matrix, vector, group = P(both, None), P(both), P("utt", None)
    return jax.shard_map(
        body,
        mesh=mesh,
        in_specs=(
            matrix,
            matrix,
            group,
            group,
            matrix,
            matrix,
            vector,
            matrix,
            vector,
            matrix,
            vector,
            matrix,
            vector,
            matrix,
            vector,
            matrix,
        ),
        out_specs=(
            matrix,
            matrix,
            matrix,
            matrix,
            matrix,
            vector,
            matrix,
            vector,
            matrix,
            vector,
            matrix,
            vector,
            matrix,
            vector,
        ),
        check_vma=False,
    )
```

```python
import math

import jax
import jax.numpy as jnp
from jax import lax
from jax.experimental import pallas as pl
from jax.experimental.pallas import tpu as pltpu
from jax.sharding import PartitionSpec as P

HD = 64
LANES = 128
BIAS_ROWS = 16
BF = jnp.bfloat16
F32 = jnp.float32
highest_precision = lax.Precision.HIGHEST
mask_value = -1e30


def product(left, right, left_dim, right_dim):
    return lax.dot_general(
        left, right, (((left_dim,), (right_dim,)), ((), ())), preferred_element_type=F32
    )


def dot32(left, right):
    return jnp.dot(left, right, preferred_element_type=F32)


def dot_nt(left, right):
    return lax.dot_general(left, right, (((1,), (1,)), ((), ())), preferred_element_type=F32)


def dot_tn(left, right):
    return lax.dot_general(left, right, (((0,), (0,)), ((), ())), preferred_element_type=F32)


fence = lax.optimization_barrier


def after(value, *others):
    return fence((value, others))[0]


def block_order(count):
    order, step = [0], count // 2
    while step >= 1:
        order = order + [d ^ step for d in order]
        step //= 2
    return order


def xor_sp(values, distance):
    size = lax.axis_size("sp")
    return lax.ppermute(values, "sp", [(i, i ^ distance) for i in range(size)])


def swap_utt(values):
    return lax.ppermute(values, "utt", [(i, i ^ 1) for i in range(lax.axis_size("utt"))])


def gather_sp(own):
    blocks, step = [own], lax.axis_size("sp") // 2
    while step >= 1:
        blocks = blocks + [xor_sp(b, step) for b in blocks]
        step //= 2
    return blocks


def exchange_sp(parts):
    order = block_order(len(parts))
    return [parts[0]] + [xor_sp(parts[i], order[i]) for i in range(1, len(parts))]


def in_device_order(blocks):
    order = block_order(len(blocks))
    stacked = jnp.stack([blocks[order.index(d)] for d in range(len(blocks))])
    me = lax.axis_index("sp")
    return [
        lax.dynamic_index_in_dim(stacked, me ^ a, 0, keepdims=False) for a in range(len(blocks))
    ]


def sum_sp(values):
    step = lax.axis_size("sp") // 2
    while step >= 1:
        values = values + xor_sp(values, step)
        step //= 2
    return values


def turn_utt(values, k):
    size = lax.axis_size("utt")
    high = size // 2
    routes = [(z * 2 + y, (z + k) % high * 2 + y) for z in range(high) for y in range(2)]
    return lax.ppermute(values, "utt", routes)


def line_blocks(own):
    return [own] + [turn_utt(own, k) for k in range(1, lax.axis_size("utt") // 2)]


def gather_line(own):
    return jnp.concatenate(line_blocks(own), axis=0)


def split_pair(parts, axis):
    low = lax.axis_index("utt") % 2
    keep = lax.dynamic_index_in_dim(parts, low, axis, keepdims=False)
    return keep, lax.dynamic_index_in_dim(parts, 1 - low, axis, keepdims=False)


def scatter_fast(parts):
    keep, send = split_pair(parts.reshape((-1, 2) + parts.shape[1:]), 1)
    return (keep.astype(F32) + swap_utt(send.astype(BF)).astype(F32)).astype(BF)


def scatter_slow(half):
    high = lax.axis_size("utt") // 2
    z = lax.axis_index("utt") // 2
    terms = [lax.dynamic_index_in_dim(half, z, 0, keepdims=False)]
    for k in range(1, high):
        piece = lax.dynamic_index_in_dim(half, (z + k) % high, 0, keepdims=False)
        terms.append(turn_utt(piece, k))
    return terms


def add_terms(terms):
    total = terms[0].astype(F32)
    for term in terms[1:]:
        total = total + term.astype(F32)
    return total


def entry(values, index):
    return lax.dynamic_index_in_dim(values, index, 0, keepdims=False)


def far_entries(values):
    me, far = lax.axis_index("sp"), lax.axis_size("sp") // 2
    return jnp.stack([entry(values, me ^ far), entry(values, me ^ far ^ 1)])


def exchange_far(values):
    return xor_sp(far_entries(values), lax.axis_size("sp") // 2)


def exchange_near(values, arrived):
    me = lax.axis_index("sp")
    last = xor_sp(jnp.stack([entry(values, me ^ 1), arrived[1]]), 1)
    return [entry(values, me), arrived[0], last[0], last[1]]


def split_exchange_sp(values):
    return jnp.stack(in_device_order(exchange_near(values, exchange_far(values))))


class Pieces:
    def __init__(self):
        self.arrays, self.starts, self.sizes = [], [], []

    def add(self, array, first_rows, size):
        self.arrays.append(array)
        self.starts.append(first_rows)
        self.sizes.append(size)

    def offsets(self):
        return jnp.stack([start for starts in self.starts for start in starts]).astype(jnp.int32)

    def count(self):
        return sum(len(starts) for starts in self.starts)

    def copies(self, offset_ref, refs, whole_ref, sems):
        made, n = [], 0
        for ref, starts, size in zip(refs, self.starts, self.sizes):
            for i in range(len(starts)):
                first = pl.multiple_of(offset_ref[n], size)
                made.append(
                    pltpu.make_async_copy(
                        ref.at[pl.ds(i * size, size)], whole_ref.at[pl.ds(first, size)], sems.at[n]
                    )
                )
                n += 1
        return made


def line_indices(flip):
    size = lax.axis_size("utt")
    high = size // 2
    u = lax.axis_index("utt")
    z, y = u // 2, u % 2
    return [(z - k + high) % high * 2 + (1 - y if flip else y) for k in range(high)]


def whole_pieces(arrays, rows):
    n_s, me = lax.axis_size("sp"), lax.axis_index("sp")
    pieces = Pieces()
    for array, d, owners, shift, size in arrays:
        pieces.add(array, [(i * n_s + (me ^ d)) * rows + shift for i in owners], size)
    return pieces


def to_owner(values):
    n_u, n_s = lax.axis_size("utt"), lax.axis_size("sp")
    routes = []
    for p in range(n_u):
        for s in range(n_s):
            routes.append((p * n_s + s, s * n_u + p))
    return lax.ppermute(values, ("utt", "sp"), routes)


def owned(values):
    n = lax.axis_size("utt") * lax.axis_size("sp")
    j = lax.axis_index("utt") * lax.axis_size("sp") + lax.axis_index("sp")
    size = values.shape[-1] // n
    return lax.dynamic_slice_in_dim(values, j * size, size, values.ndim - 1)


def norm_parts(values):
    mean_row = jnp.mean(values, axis=-1, keepdims=True)
    centered = values - mean_row
    variance = jnp.mean(centered * centered, axis=-1, keepdims=True)
    scale = lax.rsqrt(variance + 1e-06)
    return centered * scale, scale


def norm_back(normal, scale, grads):
    mean_grad = jnp.mean(grads, axis=-1, keepdims=True)
    mean_both = jnp.mean(grads * normal, axis=-1, keepdims=True)
    return (grads - mean_grad - normal * mean_both) * scale


def rotary_tables(position):
    half_head = HD // 2
    inverse = jnp.exp(jnp.arange(half_head, dtype=F32) * (-2.0 * math.log(10000.0) / HD))
    angle_arg = position.astype(F32)[:, None] * inverse[None, :]
    cosine, sine = jnp.cos(angle_arg), jnp.sin(angle_arg)
    return (
        jnp.concatenate([cosine] * 4, axis=1),
        jnp.concatenate([-sine, sine, -sine, sine], axis=1),
    )


def utterance_layout(lengths_row, frame_ids):
    ends_at = jnp.cumsum(lengths_row)
    starts_at = ends_at - lengths_row
    inside = (frame_ids[:, None] >= starts_at[None, :]) & (frame_ids[:, None] < ends_at[None, :])
    segment = jnp.sum(jnp.where(frame_ids[:, None] >= ends_at[None, :], 1, 0), axis=1).astype(
        jnp.int32
    )
    position = frame_ids - jnp.sum(jnp.where(inside, starts_at[None, :], 0), axis=1)
    return inside, segment, position


QUERY_ROWS = 512


def any_refs(count):
    return [pl.BlockSpec(memory_space=pltpu.HBM)] * count


def smem_ref():
    return pl.BlockSpec(memory_space=pltpu.SMEM)


def vmem_ref():
    return pl.BlockSpec(memory_space=pltpu.VMEM)


def placed_product(lefts, pieces, depth):
    n, count = len(pieces.arrays), pieces.count()
    rows = lefts[0].shape[0]
    width = pieces.arrays[0].shape[1]

    def kernel(offset_ref, *refs):
        piece_refs, left_refs = refs[:n], refs[n : n + len(lefts)]
        whole_ref, base_ref, sems = refs[n + len(lefts) :]
        copies = pieces.copies(offset_ref, piece_refs, whole_ref, sems)
        for copy in copies:
            copy.start()
        for copy in copies:
            copy.wait()
        total, first = None, 0
        for left_ref in left_refs:
            last = first + left_ref.shape[1]
            term = product(left_ref[...], whole_ref[first:last, :], 1, 0)
            total = term if total is None else total + term
            first = last
        base_ref[...] = total

    return pl.pallas_call(
        kernel,
        out_shape=(
            jax.ShapeDtypeStruct((depth, width), BF),
            jax.ShapeDtypeStruct((rows, width), F32),
        ),
        in_specs=[smem_ref()] + any_refs(n) + [vmem_ref()] * len(lefts),
        out_specs=(vmem_ref(),) * 2,
        scratch_shapes=[pltpu.SemaphoreType.DMA((count,))],

        cost_estimate=pl.CostEstimate(
            flops=2 * rows * depth * width,
            bytes_accessed=4 * depth * width + 2 * rows * (depth + 2 * width),
            transcendentals=0,
        ),
        name="placed_product",
    )(pieces.offsets(), *pieces.arrays, *lefts)


def turn_halves(values, cosine, sine):
    half, cols = HD // 2, values.shape[1]
    first = lax.broadcasted_iota(jnp.int32, values.shape, 1) % HD < half
    swapped = jnp.where(
        first, pltpu.roll(values, cols - half, 1), pltpu.roll(values, half, 1)
    )
    repeats = cols // cosine.shape[1]
    wide = lambda t: jnp.concatenate([t] * repeats, axis=1) if repeats > 1 else t
    return values * wide(cosine) + swapped * wide(sine)


def attend(normed_blocks, weight, bias, cosine, sine, segment):
    blocks, width = len(normed_blocks), normed_blocks[0].shape[1]
    rows = normed_blocks[0].shape[0]
    total = blocks * rows
    cols = weight.shape[1] // 3
    heads = cols // HD
    block = min(QUERY_ROWS, total)

    def kernel(*refs):
        block_refs = refs[:blocks]
        (
            weight_ref,
            cos_from,
            sin_from,
            b_ref,
            segc_ref,
            segr_ref,
            x_ref,
            q_ref,
            k_ref,
            v_ref,
            o_ref,
            lse_ref,
            vt_ref,
            bias_ref,
            w_ref,
            cos_ref,
            sin_ref,
            sems,
        ) = refs[blocks:]
        sources = [weight_ref, cos_from, sin_from, *block_refs]
        targets = [w_ref, cos_ref, sin_ref] + [
            x_ref.at[pl.ds(i * rows, rows)] for i in range(blocks)
        ]
        copies = [
            pltpu.make_async_copy(sources[i], targets[i], sems.at[i]) for i in range(3 + blocks)
        ]
        for copy in copies:
            copy.start()

        for copy in copies:
            copy.wait()

        def project(i, carried):
            at = pl.ds(pl.multiple_of(i * block, block), block)
            three = product(x_ref[at, :], w_ref[...], 1, 0) + b_ref[...]
            cosine, sine = cos_ref[at, :], sin_ref[at, :]
            q_ref[at, :] = turn_halves(three[:, :cols], cosine, sine).astype(BF)
            k_ref[at, :] = turn_halves(three[:, cols : 2 * cols], cosine, sine).astype(BF)
            v_ref[at, :] = three[:, 2 * cols :].astype(BF)
            return carried

        lax.fori_loop(0, total // block, project, 0)
        vt_ref[...] = v_ref[...].T

        def one(i, carried):
            row = pl.multiple_of(i * block, block)
            same = segc_ref[...] == segr_ref[:, pl.ds(row, block)]
            bias_ref[...] = jnp.where(same, 0.0, mask_value)
            outs = []
            for h in range(heads):
                c = slice(h * HD, (h + 1) * HD)
                scores = product(k_ref[:, c], q_ref[pl.ds(row, block), c], 1, 1)
                scores = scores * (HD**-0.5) + bias_ref[...]
                top = jnp.max(scores, axis=0, keepdims=True)
                exps = jnp.exp(scores - top)
                totals = jnp.sum(exps, axis=0, keepdims=True)
                outs.append(product(vt_ref[c, :], exps.astype(BF), 1, 0) * (1.0 / totals))
                lse_ref[h : h + 1, pl.ds(row, block)] = top + jnp.log(totals)
            o_ref[pl.ds(row, block), :] = jnp.concatenate(outs, axis=0).T.astype(BF)
            return carried

        lax.fori_loop(0, total // block, one, 0)

    return pl.pallas_call(
        kernel,
        out_shape=(
            jax.ShapeDtypeStruct((total, width), BF),
            jax.ShapeDtypeStruct((total, cols), BF),
            jax.ShapeDtypeStruct((total, cols), BF),
            jax.ShapeDtypeStruct((total, cols), BF),
            jax.ShapeDtypeStruct((total, cols), BF),
            jax.ShapeDtypeStruct((heads, total), F32),
        ),
        in_specs=any_refs(blocks + 3) + [vmem_ref()] * 3,
        out_specs=(vmem_ref(),) * 6,
        scratch_shapes=[
            pltpu.VMEM((cols, total), BF),
            pltpu.VMEM((total, block), F32),
            pltpu.VMEM(weight.shape, BF),
            pltpu.VMEM(cosine.shape, F32),
            pltpu.VMEM(cosine.shape, F32),
            pltpu.SemaphoreType.DMA((blocks + 3,)),
        ],

        cost_estimate=pl.CostEstimate(
            flops=4 * total * total * cols + 6 * total * width * cols,
            bytes_accessed=8 * total * cols + 2 * total * width + 6 * width * cols,
            transcendentals=heads * total * total,
        ),
        name="attend_forward",
    )(
        *normed_blocks,
        weight,
        cosine,
        sine,
        bias[None, :],
        segment[:, None],
        segment[None, :],
    )


def attend_back(queries, keys, values, grad_blocks, log_totals, cosine, sine, segment):
    total, cols = queries.shape
    heads = cols // HD
    block = min(QUERY_ROWS, total)
    blocks, rows = len(grad_blocks), grad_blocks[0].shape[0]

    def kernel(*refs):
        big_refs, block_refs = refs[:5], refs[5 : 5 + blocks]
        (
            lse_ref,
            segc_ref,
            segr_ref,
            d_ref,
            q_ref,
            k_ref,
            v_ref,
            cos_ref,
            sin_ref,
            g_ref,
            kt_ref,
            bias_ref,
            dk_sum,
            dv_sum,
            sems,
        ) = refs[5 + blocks :]
        held = (q_ref, k_ref, v_ref, cos_ref, sin_ref)
        copies = [pltpu.make_async_copy(big_refs[i], held[i], sems.at[i]) for i in range(5)] + [
            pltpu.make_async_copy(block_refs[i], g_ref.at[pl.ds(i * rows, rows)], sems.at[5 + i])
            for i in range(blocks)
        ]
        for copy in copies:
            copy.start()
        dk_sum[...] = jnp.zeros_like(dk_sum)
        dv_sum[...] = jnp.zeros_like(dv_sum)
        for copy in copies:
            copy.wait()
        kt_ref[...] = k_ref[...].T

        def one(i, carried):
            row = pl.multiple_of(i * block, block)
            at = pl.ds(row, block)
            same = segc_ref[...] == segr_ref[:, at]
            bias_ref[...] = jnp.where(same, 0.0, mask_value)
            outs = []
            for h in range(heads):
                c = slice(h * HD, (h + 1) * HD)
                query, grad = q_ref[at, c], g_ref[at, c]
                scores = product(k_ref[:, c], query, 1, 1) * (HD**-0.5) + bias_ref[...]
                probs = jnp.exp(scores - lse_ref[h : h + 1, at])
                both = probs * product(v_ref[:, c], grad, 1, 1)
                inner = jnp.sum(both, axis=0, keepdims=True)
                grad_scores = (both - probs * inner).astype(BF)
                dv_sum[:, c] += product(probs.astype(BF), grad, 1, 0)
                dk_sum[:, c] += product(grad_scores, query, 1, 0)
                outs.append(product(kt_ref[c, :], grad_scores, 1, 0))
            grad_query = (jnp.concatenate(outs, axis=0) * (HD**-0.5)).T.astype(BF).astype(F32)
            d_ref[at, :cols] = turn_halves(grad_query, cos_ref[at, :], -sin_ref[at, :]).astype(BF)
            return carried

        lax.fori_loop(0, total // block, one, 0)
        grad_key = (dk_sum[...] * (HD**-0.5)).astype(BF).astype(F32)
        d_ref[:, cols : 2 * cols] = turn_halves(grad_key, cos_ref[...], -sin_ref[...]).astype(BF)
        d_ref[:, 2 * cols :] = dv_sum[...].astype(BF)

    return pl.pallas_call(
        kernel,
        out_shape=jax.ShapeDtypeStruct((total, 3 * cols), BF),
        in_specs=any_refs(5 + blocks) + [vmem_ref()] * 3,
        out_specs=vmem_ref(),
        scratch_shapes=[pltpu.VMEM((total, cols), BF)] * 3
        + [pltpu.VMEM(cosine.shape, F32)] * 2
        + [
            pltpu.VMEM((total, cols), BF),
            pltpu.VMEM((cols, total), BF),
            pltpu.VMEM((total, block), F32),
            pltpu.VMEM((total, cols), F32),
            pltpu.VMEM((total, cols), F32),
            pltpu.SemaphoreType.DMA((5 + blocks,)),
        ],

        cost_estimate=pl.CostEstimate(
            flops=10 * total * total * cols,
            bytes_accessed=14 * total * cols,
            transcendentals=heads * total * total,
        ),
        name="attend_backward",
    )(
        queries,
        keys,
        values,
        cosine,
        sine,
        *grad_blocks,
        log_totals,
        segment[:, None],
        segment[None, :],
    )


def gelu_both(values):
    root = math.sqrt(2.0 / math.pi)
    square = values * values
    tanh = jnp.tanh(root * (values + 0.044715 * (values * square)))
    half = 0.5 * (1.0 + tanh)
    slope = root * (1.0 + 3 * 0.044715 * square)
    return values * half, half + 0.5 * values * (1.0 - tanh * tanh) * slope


def feed_forward(normed_blocks, grad_blocks, weights, up_bias, up_rows):
    sources = list(normed_blocks) + list(grad_blocks)
    count, width = len(sources), normed_blocks[0].shape[1]
    total = sum(block.shape[0] for block in normed_blocks)
    parts, both_rows, ff = weights.shape
    down_rows = both_rows - up_rows
    group = max(1, 256 // down_rows)
    block, half = group * down_rows, total // 2
    steps = ff // block

    def kernel(*refs):
        (
            weight_from,
            b_ref,
            act_ref,
            gh_ref,
            sum_ref,
            keep_ref,
            send_ref,
            x_ref,
            g_ref,
            acc_ref,
            w_ref,
            hidden_ref,
            active_ref,
            sems,
        ) = refs[count:]
        step = pl.program_id(0)
        copies, first = [], 0
        for i, ref in enumerate(refs[:count]):
            whole = x_ref if i < len(normed_blocks) else g_ref
            at = pl.ds(first % total, ref.shape[0])
            copies.append(pltpu.make_async_copy(ref, whole.at[at], sems.at[i]))
            first += ref.shape[0]
        copies.append(pltpu.make_async_copy(weight_from, w_ref, sems.at[count]))

        @pl.when(step == 0)
        def _():
            for copy in copies:
                copy.start()
            for copy in copies:
                copy.wait()

        def up_of(i):
            at = pl.ds(pl.multiple_of(i * block, block), block)
            return w_ref[:, :up_rows, at].reshape(width, block)

        now, before = jnp.minimum(step, steps - 1), jnp.maximum(step - 1, 0)
        slot, other = step % 2, (step + 1) % 2
        hidden_ref[slot] = product(x_ref[...], up_of(now), 1, 0) + b_ref[now]
        down = w_ref[pl.ds(now * group, group), up_rows:, :].reshape(block, width)
        active_ref[slot] = product(g_ref[...], down, 1, 1)

        active, slope = gelu_both(hidden_ref[other])
        act_ref[...] = active.astype(BF)
        grad_hidden = (active_ref[other] * slope).astype(BF)
        gh_ref[...] = grad_hidden
        sum_ref[...] = jnp.sum(grad_hidden.astype(F32), axis=0, keepdims=True)
        part = product(grad_hidden, up_of(before), 1, 1)

        @pl.when(step <= 1)
        def _():
            acc_ref[...] = part

        @pl.when(step > 1)
        def _():
            acc_ref[...] += part

        @pl.when(step == steps)
        def _():
            keep_ref[...] = acc_ref[:half, :]
            send_ref[...] = acc_ref[half:, :].astype(BF)

    fixed = lambda i: (0, 0)
    behind = lambda i: (0, jnp.maximum(i - 1, 0))
    return pl.pallas_call(
        kernel,
        grid=(steps + 1,),
        out_shape=(
            jax.ShapeDtypeStruct((total, ff), BF),
            jax.ShapeDtypeStruct((total, ff), BF),
            jax.ShapeDtypeStruct((1, ff), F32),
            jax.ShapeDtypeStruct((half, width), F32),
            jax.ShapeDtypeStruct((half, width), BF),
        ),
        in_specs=any_refs(count + 1) + [pl.BlockSpec((steps, 1, block), lambda i: (0, 0, 0))],
        out_specs=(
            pl.BlockSpec((total, block), behind),
            pl.BlockSpec((total, block), behind),
            pl.BlockSpec((1, block), behind),
            pl.BlockSpec((half, width), fixed),
            pl.BlockSpec((half, width), fixed),
        ),
        scratch_shapes=[
            pltpu.VMEM((total, width), BF),
            pltpu.VMEM((total, width), BF),
            pltpu.VMEM((total, width), F32),
            pltpu.VMEM(weights.shape, BF),
            pltpu.VMEM((2, total, block), F32),
            pltpu.VMEM((2, total, block), F32),
            pltpu.SemaphoreType.DMA((count + 1,)),
        ],

        cost_estimate=pl.CostEstimate(
            flops=6 * total * width * ff,
            bytes_accessed=2 * (4 * total * width + 2 * total * ff + 2 * width * ff),
            transcendentals=total * ff,
        ),
        name="feed_forward",
    )(*sources, weights, up_bias.reshape(steps, 1, block))


def feed_forward_weights(normed_blocks, grad_hidden, active, grad_blocks, weights, up_rows):
    sources = list(normed_blocks) + list(grad_blocks)
    count, width = len(sources), normed_blocks[0].shape[1]
    total, ff = active.shape
    parts = weights.shape[0]
    down_rows = ff // parts
    group = max(1, min(parts, 256 // up_rows))
    steps = parts // group
    tall, near = total // steps, steps // 2

    def kernel(*refs):
        (
            gh_from,
            weight_from,
            a_ref,
            r_ref,
            o_ref,
            keep_ref,
            send_ref,
            x_ref,
            g_ref,
            gh_ref,
            down_ref,
            sems,
        ) = refs[count:]
        step = pl.program_id(0)
        copies, first = [], 0
        for i, ref in enumerate(refs[:count]):
            whole = x_ref if i < len(normed_blocks) else g_ref
            at = pl.ds(first % total, ref.shape[0])
            copies.append(pltpu.make_async_copy(ref, whole.at[at], sems.at[i]))
            first += ref.shape[0]
        copies.append(pltpu.make_async_copy(gh_from, gh_ref, sems.at[count]))
        copies.append(
            pltpu.make_async_copy(weight_from.at[:, up_rows:, :], down_ref, sems.at[count + 1])
        )

        @pl.when(step == 0)
        def _():
            for copy in copies:
                copy.start()
            for copy in copies:
                copy.wait()

        at = pl.ds(pl.multiple_of(step * (group * up_rows), group * up_rows), group * up_rows)
        up = product(x_ref[:, at], gh_ref[...], 0, 0).astype(BF)
        down = product(a_ref[...], g_ref[...], 0, 0).astype(BF)
        for i in range(group):
            o_ref[i, :up_rows, :] = up[i * up_rows : (i + 1) * up_rows]
            o_ref[i, up_rows:, :] = down[i * down_rows : (i + 1) * down_rows]
        result = product(r_ref[...], down_ref[...].reshape(ff, width), 1, 0)

        @pl.when(step < near)
        def _():
            keep_ref[...] = result

        @pl.when(step >= near)
        def _():
            send_ref[...] = result.astype(BF)

    return pl.pallas_call(
        kernel,
        grid=(steps,),
        out_shape=(
            jax.ShapeDtypeStruct((parts, up_rows + down_rows, width), BF),
            jax.ShapeDtypeStruct((total // 2, width), F32),
            jax.ShapeDtypeStruct((total // 2, width), BF),
        ),
        in_specs=any_refs(count + 2)
        + [
            pl.BlockSpec((total, group * down_rows), lambda i: (0, i)),
            pl.BlockSpec((tall, ff), lambda i: (i, 0)),
        ],
        out_specs=(
            pl.BlockSpec((group, up_rows + down_rows, width), lambda i: (i, 0, 0)),
            pl.BlockSpec((tall, width), lambda i: (jnp.minimum(i, near - 1), 0)),
            pl.BlockSpec((tall, width), lambda i: (jnp.maximum(i - near, 0), 0)),
        ),
        scratch_shapes=[
            pltpu.VMEM((total, width), BF),
            pltpu.VMEM((total, width), BF),
            pltpu.VMEM((total, ff), BF),
            pltpu.VMEM((parts, down_rows, width), BF),
            pltpu.SemaphoreType.DMA((count + 2,)),
        ],
        cost_estimate=pl.CostEstimate(
            flops=6 * total * width * ff,
            bytes_accessed=2 * (2 * total * (width + ff) + 2 * width * ff),
            transcendentals=0,
        ),
        name="feed_forward_weights",
    )(*sources, grad_hidden, weights, active, active)


def own_time_features(times, first_col, col_count, model_width):
    half_width = model_width // 2
    cols = first_col + jnp.arange(col_count, dtype=jnp.int32)
    is_sine = cols < half_width
    steps_row = jnp.where(is_sine, cols, cols - half_width).astype(F32)
    frequency = jnp.exp(steps_row * (-math.log(10000.0) / (half_width - 1)))
    phase_arg = 1000.0 * times[:, None] * frequency[None, :]
    features = jnp.where(is_sine[None, :], jnp.sin(phase_arg), jnp.cos(phase_arg))
    return jax.nn.silu(features).astype(BF)


def pad_rows(vector):
    rows = -(-vector.shape[-1] // LANES)
    return jnp.pad(vector, (0, rows * LANES - vector.shape[-1])).reshape(rows, LANES)


def body(
    frames,
    skip_frames,
    lengths,
    flow_time,
    skip_weight,
    adaln_weight,
    adaln_bias,
    qkv_weight,
    qkv_bias,
    output_weight,
    output_bias,
    up_weight,
    up_bias,
    down_weight,
    down_bias,
    out_grad,
):
    n_u, n_s = lax.axis_size("utt"), lax.axis_size("sp")
    u, s = lax.axis_index("utt"), lax.axis_index("sp")
    n_all = n_u * n_s
    me = u * n_s + s
    rows, width = frames.shape
    per_group = lengths.shape[1]
    ff = up_weight.shape[1]
    part_width = width // n_s
    part_ff = ff // n_s
    lengths_row = lengths[0]

    all_ids = jnp.concatenate(
        [(s ^ d) * rows + jnp.arange(rows, dtype=jnp.int32) for d in block_order(n_s)]
    )
    inside_all, segment_all, position_all = utterance_layout(lengths_row, all_ids)
    inside = inside_all[:rows]

    cols = qkv_weight.shape[0]
    slot, out_slot = skip_weight.shape[0], output_weight.shape[0]
    far = n_s // 2
    bias_sizes = [qkv_bias.shape[0], output_bias.shape[0], up_bias.shape[0], down_bias.shape[0]]
    bias_own = pad_rows(
        jnp.concatenate([qkv_bias, output_bias, up_bias, down_bias]).astype(F32)
    )
    qkv_split = qkv_weight.reshape(cols, 3, n_s, part_width).transpose(2, 0, 1, 3)
    up_split = up_weight.reshape(cols, n_u, n_s, ff // n_all).transpose(2, 0, 1, 3)
    both_split = jnp.concatenate(
        [qkv_split.reshape(n_s, cols, 3 * part_width), up_split.reshape(n_s, cols, part_ff)], axis=2
    )
    skip_blocks = line_blocks(skip_weight)
    flow_row = jnp.pad(flow_time, ((0, 0), (0, LANES - per_group)))
    first_rows = jnp.concatenate([flow_row, bias_own], axis=0)
    first_rows = lax.all_to_all(
        jnp.broadcast_to(first_rows[None], (n_u,) + first_rows.shape), "utt", 0, 0, tiled=True
    )
    both_mine = lax.all_to_all(after(both_split, first_rows), "sp", 0, 0, tiled=True)
    part = n_u * slot
    chosen = jnp.arange(2 * width, dtype=jnp.int32)
    chosen = chosen % part // slot * (slot * n_s) + chosen // part * slot + chosen % slot
    selection = (jnp.arange(2 * width, dtype=jnp.int32)[:, None] == chosen[None, :]).astype(BF)
    joined_split = dot32(jnp.concatenate([frames, skip_frames], axis=1), selection).astype(BF)
    joined_split = joined_split.reshape(rows, n_s, part).transpose(1, 0, 2)
    joined_sent = far_entries(joined_split)
    skip_blocks, both_mine, first_rows, joined_split, joined_sent = fence(
        (skip_blocks, both_mine, first_rows, joined_split, joined_sent)
    )
    skip_line = jnp.concatenate(skip_blocks, axis=0)
    both_mine = both_mine.reshape(n_s * cols, -1)
    my_qkv = lax.all_gather(both_mine[:, : 3 * part_width], "utt", axis=0, tiled=True)
    ff_lines = lax.all_gather(
        jnp.concatenate([both_mine[:, 3 * part_width :], down_weight], axis=0), "utt", axis=0
    )

    times = first_rows[:, 0, :per_group].reshape(n_u * per_group)
    feature_rows = adaln_weight.shape[0]
    silu_own = own_time_features(times, me * feature_rows, feature_rows, width)
    table_width = adaln_weight.shape[1]
    mod_terms = dot32(silu_own, adaln_weight)
    bias_cols = lax.dynamic_update_slice(
        jnp.zeros((table_width,), F32), adaln_bias.astype(F32), (me * adaln_bias.shape[0],)
    )
    mod_terms = (mod_terms + bias_cols[None, :]).reshape(n_u, per_group, 6, width)
    mod_terms = mod_terms.transpose(0, 2, 1, 3).reshape(n_u, 6 * per_group, width)

    high, half = skip_line.shape[0] // slot, slot // 2
    rows_of = lambda x: x.reshape(high, slot, width)
    over_sp, over_utt = xor_sp(skip_line, far), swap_utt(skip_line)
    joined_far = xor_sp(joined_sent, far)
    near_line = xor_sp(skip_line, 1)
    mod_terms = lax.all_to_all(mod_terms, "utt", 0, 0, tiled=True)
    cosine, sine = rotary_tables(position_all)
    over_sp, over_utt, joined_far, near_line, mod_terms, cosine, sine = fence(
        (over_sp, over_utt, joined_far, near_line, mod_terms, cosine, sine)
    )
    top = xor_sp(rows_of(over_utt)[:, :half].reshape(high * half, width), far)
    bottom = swap_utt(rows_of(over_sp)[:, half:].reshape(high * half, width))
    near_sp, near_utt = xor_sp(over_sp, 1), xor_sp(over_utt, 1)
    table_rows = 6 * per_group
    bias_own = first_rows[:, 1:].reshape(-1, width)
    message = jnp.concatenate([jnp.sum(mod_terms, axis=0), bias_own], axis=0)
    message_far = xor_sp(message, far)
    output_blocks = lax.all_to_all(
        jnp.broadcast_to(after(output_weight, over_sp)[None], (n_u, out_slot, width)),
        "utt",
        0,
        0,
        tiled=True,
    ).reshape(n_u * out_slot, width)
    top, bottom, near_sp, near_utt, message_far, my_qkv = fence(
        (top, bottom, near_sp, near_utt, message_far, my_qkv)
    )
    corner = jnp.concatenate([top, bottom], axis=0)
    message = jnp.concatenate(
        [message[:table_rows] + message_far[:table_rows], bias_own, message_far[table_rows:]], axis=0
    )
    corner, message = fence((corner, message))
    near_corner, message_near = fence((xor_sp(corner, 1), xor_sp(message, 1)))
    mod_table = message[:table_rows] + message_near[:table_rows]
    bias_blocks = [
        m.reshape(2, n_u, -1)[i]
        for m in (message[table_rows:], message_near[table_rows:])
        for i in range(2)
    ]
    here, there = line_indices(False), line_indices(True)
    skip_pieces = Pieces()
    whole_row = lambda i, distance: (i * n_s + (s ^ distance)) * slot
    for array, owners, distance in (
        (skip_line, here, 0),
        (over_sp, here, far),
        (over_utt, there, 0),
        (near_line, here, 1),
        (near_sp, here, far ^ 1),
        (near_utt, there, 1),
    ):
        skip_pieces.add(array, [whole_row(i, distance) for i in owners], slot)
    for array, distance in ((corner, far), (near_corner, far ^ 1)):
        skip_pieces.add(
            array,
            [whole_row(i, distance) for i in there]
            + [whole_row(i, distance) + half for i in there],
            half,
        )

    def expand(block, segment):
        table = mod_table[block * per_group : (block + 1) * per_group]
        result = table[per_group - 1][None, :]
        for k in range(per_group - 2, -1, -1):
            result = jnp.where(segment[:, None] == k, table[k][None, :], result)
        return result

    def segment_sums(values):
        return jnp.stack(
            [jnp.sum(jnp.where(inside[:, k][:, None], values, 0.0), axis=0) for k in range(per_group)]
        )

    segment_own = segment_all[:rows]
    scale_attn, gate_attn, shift_ffn, scale_ffn, gate_ffn = [
        expand(i, segment_own) for i in range(1, 6)
    ]

    grad_out = out_grad.astype(F32)
    grad_result = (gate_ffn * grad_out).astype(BF)
    grad_result_far = xor_sp(grad_result, far)
    full_skip, base_rows = placed_product([frames, skip_frames], skip_pieces, 2 * width)
    base_rows, my_qkv, grad_result_far = fence((base_rows, my_qkv, grad_result_far))
    base_norm, base_scale = norm_parts(base_rows)
    normed = (base_norm * (1.0 + scale_attn) + expand(0, segment_own)).astype(BF)
    far_normed = xor_sp(normed, far)
    far_normed, output_blocks = fence((far_normed, output_blocks))
    two_normed = jnp.concatenate([normed, far_normed], axis=0)
    near_normed = xor_sp(two_normed, 1)
    joined_mine = exchange_near(joined_split, joined_far)
    near_normed, joined_mine = fence((near_normed, joined_mine))
    output_far = xor_sp(output_blocks, far)
    bias_all = jnp.stack(in_device_order(bias_blocks), axis=1).reshape(n_u, n_s, -1)
    offsets = [0]
    for size in bias_sizes:
        offsets.append(offsets[-1] + size)
    full_qkv_bias, full_output_bias, full_up_bias, full_down_bias = [
        bias_all[:, :, offsets[i] : offsets[i + 1]].reshape(-1) for i in range(4)
    ]
    my_qkv_bias = lax.dynamic_slice_in_dim(
        full_qkv_bias.reshape(3, width), s * part_width, part_width, 1
    ).reshape(-1)
    my_up_bias = lax.dynamic_index_in_dim(
        full_up_bias.reshape(n_u, n_s, -1), s, 1, keepdims=False
    ).reshape(-1)

    normed_all, query_rows, key_rows, value_rows, attended_heads, log_totals = attend(
        [two_normed, near_normed], my_qkv, my_qkv_bias, cosine, sine, segment_all
    )
    attended_heads, output_far = fence((attended_heads, output_far))
    arrived = exchange_sp([attended_heads[i * rows : (i + 1) * rows] for i in range(n_s)])
    output_near = xor_sp(jnp.concatenate([output_blocks, output_far], axis=0), 1)
    grad_result_near = xor_sp(jnp.concatenate([grad_result, grad_result_far], axis=0), 1)
    arrived, output_near, grad_result_near = fence((arrived, output_near, grad_result_near))
    output_pieces = whole_pieces(
        [
            (output_blocks, 0, range(n_u), 0, out_slot),
            (output_far, far, range(n_u), 0, out_slot),
        ],
        out_slot,
    )
    output_pieces.add(
        output_near,
        [(i * n_s + (s ^ 1)) * out_slot for i in range(n_u)]
        + [(i * n_s + (s ^ 1 ^ far)) * out_slot for i in range(n_u)],
        out_slot,
    )
    attended = jnp.concatenate(in_device_order(arrived), axis=1)
    full_output, branch = placed_product([attended], output_pieces, width)
    branch = branch + full_output_bias[None, :]
    middle = base_rows + gate_attn * branch
    middle_norm, middle_scale = norm_parts(middle)
    normed_ffn = (middle_norm * (1.0 + scale_ffn) + shift_ffn).astype(BF)

    half_rows = n_s * rows // 2
    far_ffn = xor_sp(normed_ffn, far)
    two_ffn = jnp.concatenate([normed_ffn, far_ffn], axis=0)
    near_ffn = xor_sp(two_ffn, 1)
    ffn_blocks = [two_ffn, near_ffn]
    grad_result_blocks = [grad_result, grad_result_far, grad_result_near]
    active, grad_hidden, grad_up_bias, kept, sent = feed_forward(
        ffn_blocks, grad_result_blocks, ff_lines, my_up_bias, n_s * cols
    )
    arrived = xor_sp(sent, 1)
    far_sent = (kept[rows:] + arrived[rows:].astype(F32)).astype(BF)
    far_sent, active, grad_hidden = fence((far_sent, active, grad_hidden))
    far_sum = xor_sp(far_sent, n_s // 2)

    ff_grads, result_kept, sent = feed_forward_weights(
        ffn_blocks, grad_hidden, active, grad_result_blocks, ff_lines, n_s * cols
    )
    far_sum, result_kept, sent, ff_grads = fence((far_sum, result_kept, sent, ff_grads))
    grad_normed_ffn = kept[:rows] + arrived[:rows].astype(F32) + far_sum.astype(F32)
    ff_mine = lax.psum_scatter(ff_grads, "utt", scatter_dimension=0, tiled=True)[0]
    grad_middle = grad_out + norm_back(
        middle_norm, middle_scale, grad_normed_ffn * (1.0 + scale_ffn)
    )
    grad_branch = (gate_attn * grad_middle).astype(BF)
    grad_attended = dot_nt(grad_branch, full_output).astype(BF)
    grad_heads = exchange_sp(
        [
            lax.dynamic_slice_in_dim(grad_attended, (s ^ d) * part_width, part_width, 1)
            for d in block_order(n_s)
        ]
    )
    result_arrived = xor_sp(after(sent, grad_attended), 1)
    grad_heads, result_arrived, grad_branch = fence((grad_heads, result_arrived, grad_branch))
    far_branch = xor_sp(grad_branch, far)
    result_sent = (result_kept[rows:] + result_arrived[rows:].astype(F32)).astype(BF)

    grad_projected = attend_back(
        query_rows, key_rows, value_rows, grad_heads, log_totals, cosine, sine, segment_all
    )
    grad_projected, far_branch = fence((grad_projected, far_branch))
    sent = product(grad_projected[half_rows:], my_qkv, 1, 1).astype(BF)
    kept = product(grad_projected[:half_rows], my_qkv, 1, 1)
    arrived = xor_sp(sent, 1)
    far_sent = (kept[rows:] + arrived[rows:].astype(F32)).astype(BF)
    far_sent, projected_late, far_branch, middle_late, nffn_late = fence(
        (far_sent, grad_projected, far_branch, grad_middle, grad_normed_ffn)
    )
    far_sum = xor_sp(far_sent, far)

    grad_qkv = dot_tn(normed_all, projected_late).astype(BF)
    my_qkv_bias_grad = jnp.sum(projected_late.astype(F32), axis=0)
    qkv_keep, qkv_send = split_pair(grad_qkv.reshape(-1, 2, n_s * cols, 3 * part_width), 1)
    qkv_arrived = swap_utt(qkv_send)
    branch_blocks, step = [grad_branch, far_branch], n_s // 4
    while step >= 1:
        branch_blocks = branch_blocks + [xor_sp(b, step) for b in branch_blocks]
        step //= 2
    grad_output = dot_tn(attended_heads, jnp.concatenate(branch_blocks, axis=0)).astype(BF)
    grad_output_bias = jnp.sum((gate_attn * middle_late).astype(BF).astype(F32), axis=0)
    early_tables = [
        segment_sums(v) for v in (middle_late * branch, nffn_late, nffn_late * middle_norm)
    ]
    far_sum, early_tables, qkv_keep, qkv_arrived, grad_output = fence(
        (far_sum, early_tables, qkv_keep, qkv_arrived, grad_output)
    )
    grad_normed = kept[:rows] + arrived[:rows].astype(F32) + far_sum.astype(F32)

    grad_base = (
        grad_middle + norm_back(base_norm, base_scale, grad_normed * (1.0 + scale_attn))
    ).astype(BF)
    far_base = xor_sp(grad_base, far)
    far_base, normed_late = fence((far_base, grad_normed))
    two_base = jnp.concatenate([grad_base, far_base], axis=0)
    near_base = xor_sp(two_base, 1)
    grad_skip = dot_tn(
        jnp.concatenate(joined_mine, axis=0), jnp.concatenate([two_base, near_base], axis=0)
    ).astype(BF)
    skip_keep, skip_send = split_pair(grad_skip.reshape((-1, 2) + (slot, width)), 1)
    skip_send, grad_output, base_late, normed_late, result_sent, late_grad = fence(
        (skip_send, grad_output, grad_base, normed_late, result_sent, out_grad)
    )

    skip_arrived, far_result = swap_utt(skip_send), xor_sp(result_sent, far)
    frames_grad = dot_nt(base_late, full_skip[:width])
    skip_grad = dot_nt(base_late, full_skip[width:])
    late_tables = [segment_sums(v) for v in (normed_late, normed_late * base_norm)]
    skip_arrived, far_result, late_tables, frames_grad, skip_grad, qkv_keep, ff_mine = fence(
        (skip_arrived, far_result, late_tables, frames_grad, skip_grad, qkv_keep, ff_mine)
    )
    qkv_half = (qkv_keep.astype(F32) + qkv_arrived.astype(F32)).astype(BF)
    grad_out = late_grad.astype(F32)
    result = (
        result_kept[:rows]
        + result_arrived[:rows].astype(F32)
        + far_result.astype(F32)
        + full_down_bias[None, :]
    )
    skip_half = (skip_keep.astype(F32) + skip_arrived.astype(F32)).astype(BF)
    out_keep, out_send = split_pair(grad_output.reshape(-1, 2, out_slot, width), 1)
    skip_half, qkv_half, out_send = fence((skip_half, qkv_half, out_send))

    skip_terms, qkv_terms = scatter_slow(skip_half), scatter_slow(qkv_half)
    out_arrived = swap_utt(out_send)
    mixed_out = (middle + gate_ffn * result).astype(BF)
    grad_down_bias = jnp.sum((gate_ffn * grad_out).astype(BF).astype(F32), axis=0)
    gate_table = segment_sums(grad_out * result)
    skip_sum = add_terms(skip_terms)
    out_half = (out_keep.astype(F32) + out_arrived.astype(F32)).astype(BF)
    qkv_mine = add_terms(qkv_terms).astype(BF)
    qkv_mine = qkv_mine.reshape(n_s, cols, 3 * part_width)
    out_sum = to_owner(add_terms(scatter_slow(out_half)))
    qkv_back = split_exchange_sp(qkv_mine)
    qkv_sum = (
        qkv_back.reshape(n_s, cols, 3, part_width).transpose(1, 2, 0, 3).reshape(cols, 3 * width)
    ).astype(F32)
    up_back = split_exchange_sp(ff_mine[: n_s * cols].reshape(n_s, cols, part_ff))
    up_sum = (
        up_back.reshape(n_s, cols, n_u, ff // n_all).transpose(1, 2, 0, 3).reshape(cols, ff)
    ).astype(F32)
    down_sum = ff_mine[n_s * cols :].astype(F32)

    grad_table = jnp.concatenate(late_tables + early_tables + [gate_table], axis=1)
    qkv_bias_slots = lax.dynamic_update_slice(
        jnp.zeros((3, width), F32), my_qkv_bias_grad.reshape(3, part_width), (0, s * part_width)
    ).reshape(-1)
    up_bias_slots = lax.dynamic_update_slice(
        jnp.zeros((n_u, n_s, ff // n_all), F32),
        grad_up_bias.reshape(n_u, 1, ff // n_all),
        (0, s, 0),
    ).reshape(-1)
    bias_vec = jnp.concatenate(
        [
            v.reshape(n_u, -1)
            for v in (qkv_bias_slots, grad_output_bias, up_bias_slots, grad_down_bias)
        ],
        axis=1,
    )
    vec_rows = -(-bias_vec.shape[1] // LANES)
    bias_vec = jnp.pad(bias_vec, ((0, 0), (0, vec_rows * LANES - bias_vec.shape[1])))
    table_rows = per_group * table_width // LANES
    tail = jnp.concatenate(
        [grad_table.reshape(table_rows, LANES), bias_vec.reshape(n_u * vec_rows, LANES)], axis=0
    )
    tail = sum_sp(tail)
    tail = jnp.concatenate(
        [
            jnp.broadcast_to(tail[None, :table_rows], (n_u, table_rows, LANES)),
            tail[table_rows:].reshape(n_u, vec_rows, LANES),
        ],
        axis=1,
    )
    tail = tail.astype(BF)
    tail = lax.all_to_all(tail, "utt", 0, 0, tiled=True).astype(F32)
    table_all = tail[:, :table_rows].reshape(n_u * per_group, table_width)
    adaln_sum = lax.dot_general(
        silu_own.astype(F32),
        table_all,
        (((0,), (0,)), ((), ())),
        precision=highest_precision,
        preferred_element_type=F32,
    )
    adaln_bias_sum = jnp.sum(owned(table_all), axis=0)
    vec = jnp.sum(tail[:, table_rows:], axis=0).reshape(-1)
    bias_sums, start = [], 0
    for size in bias_sizes:
        bias_sums.append(lax.dynamic_slice_in_dim(vec, start + s * size, size, 0))
        start += size * n_s

    return (
        mixed_out,
        frames_grad,
        skip_grad,
        skip_sum,
        adaln_sum,
        adaln_bias_sum,
        qkv_sum,
        bias_sums[0],
        out_sum,
        bias_sums[1],
        up_sum,
        bias_sums[2],
        down_sum,
        bias_sums[3],
    )


def solution(mesh):
    both = ("utt", "sp")
    matrix, vector, group = P(both, None), P(both), P("utt", None)
    return jax.shard_map(
        body,
        mesh=mesh,
        in_specs=(
            matrix,
            matrix,
            group,
            group,
            matrix,
            matrix,
            vector,
            matrix,
            vector,
            matrix,
            vector,
            matrix,
            vector,
            matrix,
            vector,
            matrix,
        ),
        out_specs=(
            matrix,
            matrix,
            matrix,
            matrix,
            matrix,
            vector,
            matrix,
            vector,
            matrix,
            vector,
            matrix,
            vector,
            matrix,
            vector,
        ),
        check_vma=False,
    )
```

```python
import math

import jax
import jax.numpy as jnp
from jax import lax
from jax.experimental import pallas as pl
from jax.experimental.pallas import tpu as pltpu
from jax.sharding import PartitionSpec as P

HD = 64
LANES = 128
BIAS_ROWS = 16
BF = jnp.bfloat16
F32 = jnp.float32
highest_precision = lax.Precision.HIGHEST
mask_value = -1e30


def product(left, right, left_dim, right_dim):
    return lax.dot_general(
        left, right, (((left_dim,), (right_dim,)), ((), ())), preferred_element_type=F32
    )


def dot32(left, right):
    return jnp.dot(left, right, preferred_element_type=F32)


def dot_nt(left, right):
    return lax.dot_general(left, right, (((1,), (1,)), ((), ())), preferred_element_type=F32)


def dot_tn(left, right):
    return lax.dot_general(left, right, (((0,), (0,)), ((), ())), preferred_element_type=F32)


fence = lax.optimization_barrier


def after(value, *others):
    return fence((value, others))[0]


def block_order(count):
    order, step = [0], count // 2
    while step >= 1:
        order = order + [d ^ step for d in order]
        step //= 2
    return order


def xor_sp(values, distance):
    size = lax.axis_size("sp")
    return lax.ppermute(values, "sp", [(i, i ^ distance) for i in range(size)])


def swap_utt(values):
    return lax.ppermute(values, "utt", [(i, i ^ 1) for i in range(lax.axis_size("utt"))])


def gather_sp(own):
    blocks, step = [own], lax.axis_size("sp") // 2
    while step >= 1:
        blocks = blocks + [xor_sp(b, step) for b in blocks]
        step //= 2
    return blocks


def exchange_sp(parts):
    order = block_order(len(parts))
    return [parts[0]] + [xor_sp(parts[i], order[i]) for i in range(1, len(parts))]


def in_device_order(blocks):
    order = block_order(len(blocks))
    stacked = jnp.stack([blocks[order.index(d)] for d in range(len(blocks))])
    me = lax.axis_index("sp")
    return [
        lax.dynamic_index_in_dim(stacked, me ^ a, 0, keepdims=False) for a in range(len(blocks))
    ]


def sum_sp(values):
    step = lax.axis_size("sp") // 2
    while step >= 1:
        values = values + xor_sp(values, step)
        step //= 2
    return values


def turn_utt(values, k):
    size = lax.axis_size("utt")
    high = size // 2
    routes = [(z * 2 + y, (z + k) % high * 2 + y) for z in range(high) for y in range(2)]
    return lax.ppermute(values, "utt", routes)


def line_blocks(own):
    return [own] + [turn_utt(own, k) for k in range(1, lax.axis_size("utt") // 2)]


def gather_line(own):
    return jnp.concatenate(line_blocks(own), axis=0)


def split_pair(parts, axis):
    low = lax.axis_index("utt") % 2
    keep = lax.dynamic_index_in_dim(parts, low, axis, keepdims=False)
    return keep, lax.dynamic_index_in_dim(parts, 1 - low, axis, keepdims=False)


def scatter_fast(parts):
    keep, send = split_pair(parts.reshape((-1, 2) + parts.shape[1:]), 1)
    return (keep.astype(F32) + swap_utt(send.astype(BF)).astype(F32)).astype(BF)


def scatter_slow(half):
    high = lax.axis_size("utt") // 2
    z = lax.axis_index("utt") // 2
    terms = [lax.dynamic_index_in_dim(half, z, 0, keepdims=False)]
    for k in range(1, high):
        piece = lax.dynamic_index_in_dim(half, (z + k) % high, 0, keepdims=False)
        terms.append(turn_utt(piece, k))
    return terms


def add_terms(terms):
    total = terms[0].astype(F32)
    for term in terms[1:]:
        total = total + term.astype(F32)
    return total


def entry(values, index):
    return lax.dynamic_index_in_dim(values, index, 0, keepdims=False)


def far_entries(values):
    me, far = lax.axis_index("sp"), lax.axis_size("sp") // 2
    return jnp.stack([entry(values, me ^ far), entry(values, me ^ far ^ 1)])


def exchange_far(values):
    return xor_sp(far_entries(values), lax.axis_size("sp") // 2)


def exchange_near(values, arrived):
    me = lax.axis_index("sp")
    last = xor_sp(jnp.stack([entry(values, me ^ 1), arrived[1]]), 1)
    return [entry(values, me), arrived[0], last[0], last[1]]


def split_exchange_sp(values):
    return jnp.stack(in_device_order(exchange_near(values, exchange_far(values))))


class Pieces:
    def __init__(self):
        self.arrays, self.starts, self.sizes = [], [], []

    def add(self, array, first_rows, size):
        self.arrays.append(array)
        self.starts.append(first_rows)
        self.sizes.append(size)

    def offsets(self):
        return jnp.stack([start for starts in self.starts for start in starts]).astype(jnp.int32)

    def count(self):
        return sum(len(starts) for starts in self.starts)

    def copies(self, offset_ref, refs, whole_ref, sems):
        made, n = [], 0
        for ref, starts, size in zip(refs, self.starts, self.sizes):
            for i in range(len(starts)):
                first = pl.multiple_of(offset_ref[n], size)
                made.append(
                    pltpu.make_async_copy(
                        ref.at[pl.ds(i * size, size)], whole_ref.at[pl.ds(first, size)], sems.at[n]
                    )
                )
                n += 1
        return made


def line_indices(flip):
    size = lax.axis_size("utt")
    high = size // 2
    u = lax.axis_index("utt")
    z, y = u // 2, u % 2
    return [(z - k + high) % high * 2 + (1 - y if flip else y) for k in range(high)]


def whole_pieces(arrays, rows):
    n_s, me = lax.axis_size("sp"), lax.axis_index("sp")
    pieces = Pieces()
    for array, d, owners, shift, size in arrays:
        pieces.add(array, [(i * n_s + (me ^ d)) * rows + shift for i in owners], size)
    return pieces


def to_owner(values):
    n_u, n_s = lax.axis_size("utt"), lax.axis_size("sp")
    routes = []
    for p in range(n_u):
        for s in range(n_s):
            routes.append((p * n_s + s, s * n_u + p))
    return lax.ppermute(values, ("utt", "sp"), routes)


def owned(values):
    n = lax.axis_size("utt") * lax.axis_size("sp")
    j = lax.axis_index("utt") * lax.axis_size("sp") + lax.axis_index("sp")
    size = values.shape[-1] // n
    return lax.dynamic_slice_in_dim(values, j * size, size, values.ndim - 1)


def norm_parts(values):
    mean_row = jnp.mean(values, axis=-1, keepdims=True)
    centered = values - mean_row
    variance = jnp.mean(centered * centered, axis=-1, keepdims=True)
    scale = lax.rsqrt(variance + 1e-06)
    return centered * scale, scale


def norm_back(normal, scale, grads):
    mean_grad = jnp.mean(grads, axis=-1, keepdims=True)
    mean_both = jnp.mean(grads * normal, axis=-1, keepdims=True)
    return (grads - mean_grad - normal * mean_both) * scale


def rotary_tables(position):
    half_head = HD // 2
    inverse = jnp.exp(jnp.arange(half_head, dtype=F32) * (-2.0 * math.log(10000.0) / HD))
    angle_arg = position.astype(F32)[:, None] * inverse[None, :]
    cosine, sine = jnp.cos(angle_arg), jnp.sin(angle_arg)
    return (
        jnp.concatenate([cosine] * 4, axis=1),
        jnp.concatenate([-sine, sine, -sine, sine], axis=1),
    )


def utterance_layout(lengths_row, frame_ids):
    ends_at = jnp.cumsum(lengths_row)
    starts_at = ends_at - lengths_row
    inside = (frame_ids[:, None] >= starts_at[None, :]) & (frame_ids[:, None] < ends_at[None, :])
    segment = jnp.sum(jnp.where(frame_ids[:, None] >= ends_at[None, :], 1, 0), axis=1).astype(
        jnp.int32
    )
    position = frame_ids - jnp.sum(jnp.where(inside, starts_at[None, :], 0), axis=1)
    return inside, segment, position


QUERY_ROWS = 512


def any_refs(count):
    return [pl.BlockSpec(memory_space=pltpu.HBM)] * count


def smem_ref():
    return pl.BlockSpec(memory_space=pltpu.SMEM)


def vmem_ref():
    return pl.BlockSpec(memory_space=pltpu.VMEM)


def placed_product(lefts, pieces, depth):
    n, count = len(pieces.arrays), pieces.count()
    rows = lefts[0].shape[0]
    width = pieces.arrays[0].shape[1]

    def kernel(offset_ref, *refs):
        piece_refs, left_refs = refs[:n], refs[n : n + len(lefts)]
        whole_ref, base_ref, sems = refs[n + len(lefts) :]
        copies = pieces.copies(offset_ref, piece_refs, whole_ref, sems)
        for copy in copies:
            copy.start()
        for copy in copies:
            copy.wait()
        total, first = None, 0
        for left_ref in left_refs:
            last = first + left_ref.shape[1]
            term = product(left_ref[...], whole_ref[first:last, :], 1, 0)
            total = term if total is None else total + term
            first = last
        base_ref[...] = total

    return pl.pallas_call(
        kernel,
        out_shape=(
            jax.ShapeDtypeStruct((depth, width), BF),
            jax.ShapeDtypeStruct((rows, width), F32),
        ),
        in_specs=[smem_ref()] + any_refs(n) + [vmem_ref()] * len(lefts),
        out_specs=(vmem_ref(),) * 2,
        scratch_shapes=[pltpu.SemaphoreType.DMA((count,))],

        cost_estimate=pl.CostEstimate(
            flops=2 * rows * depth * width,
            bytes_accessed=4 * depth * width + 2 * rows * (depth + 2 * width),
            transcendentals=0,
        ),
        name="placed_product",
    )(pieces.offsets(), *pieces.arrays, *lefts)


def turn_halves(values, cosine, sine):
    half, cols = HD // 2, values.shape[1]
    first = lax.broadcasted_iota(jnp.int32, values.shape, 1) % HD < half
    swapped = jnp.where(
        first, pltpu.roll(values, cols - half, 1), pltpu.roll(values, half, 1)
    )
    repeats = cols // cosine.shape[1]
    wide = lambda t: jnp.concatenate([t] * repeats, axis=1) if repeats > 1 else t
    return values * wide(cosine) + swapped * wide(sine)


def attend(normed_blocks, weight, bias, cosine, sine, segment):
    blocks, width = len(normed_blocks), normed_blocks[0].shape[1]
    rows = normed_blocks[0].shape[0]
    total = blocks * rows
    cols = weight.shape[1] // 3
    heads = cols // HD
    block = min(QUERY_ROWS, total)

    def kernel(*refs):
        block_refs = refs[:blocks]
        (
            weight_ref,
            cos_from,
            sin_from,
            b_ref,
            segc_ref,
            segr_ref,
            x_ref,
            q_ref,
            k_ref,
            v_ref,
            o_ref,
            lse_ref,
            vt_ref,
            bias_ref,
            w_ref,
            cos_ref,
            sin_ref,
            sems,
        ) = refs[blocks:]
        sources = [weight_ref, cos_from, sin_from, *block_refs]
        targets = [w_ref, cos_ref, sin_ref] + [
            x_ref.at[pl.ds(i * rows, rows)] for i in range(blocks)
        ]
        copies = [
            pltpu.make_async_copy(sources[i], targets[i], sems.at[i]) for i in range(3 + blocks)
        ]
        for copy in copies:
            copy.start()

        for copy in copies:
            copy.wait()

        def project(i, carried):
            at = pl.ds(pl.multiple_of(i * block, block), block)
            three = product(x_ref[at, :], w_ref[...], 1, 0) + b_ref[...]
            cosine, sine = cos_ref[at, :], sin_ref[at, :]
            q_ref[at, :] = turn_halves(three[:, :cols], cosine, sine).astype(BF)
            k_ref[at, :] = turn_halves(three[:, cols : 2 * cols], cosine, sine).astype(BF)
            v_ref[at, :] = three[:, 2 * cols :].astype(BF)
            return carried

        lax.fori_loop(0, total // block, project, 0)
        vt_ref[...] = v_ref[...].T

        def one(i, carried):
            row = pl.multiple_of(i * block, block)
            same = segc_ref[...] == segr_ref[:, pl.ds(row, block)]
            bias_ref[...] = jnp.where(same, 0.0, mask_value)
            outs = []
            for h in range(heads):
                c = slice(h * HD, (h + 1) * HD)
                scores = product(k_ref[:, c], q_ref[pl.ds(row, block), c], 1, 1)
                scores = scores * (HD**-0.5) + bias_ref[...]
                top = jnp.max(scores, axis=0, keepdims=True)
                exps = jnp.exp(scores - top)
                totals = jnp.sum(exps, axis=0, keepdims=True)
                outs.append(product(vt_ref[c, :], exps.astype(BF), 1, 0) * (1.0 / totals))
                lse_ref[h : h + 1, pl.ds(row, block)] = top + jnp.log(totals)
            o_ref[pl.ds(row, block), :] = jnp.concatenate(outs, axis=0).T.astype(BF)
            return carried

        lax.fori_loop(0, total // block, one, 0)

    return pl.pallas_call(
        kernel,
        out_shape=(
            jax.ShapeDtypeStruct((total, width), BF),
            jax.ShapeDtypeStruct((total, cols), BF),
            jax.ShapeDtypeStruct((total, cols), BF),
            jax.ShapeDtypeStruct((total, cols), BF),
            jax.ShapeDtypeStruct((total, cols), BF),
            jax.ShapeDtypeStruct((heads, total), F32),
        ),
        in_specs=any_refs(blocks + 3) + [vmem_ref()] * 3,
        out_specs=(vmem_ref(),) * 6,
        scratch_shapes=[
            pltpu.VMEM((cols, total), BF),
            pltpu.VMEM((total, block), F32),
            pltpu.VMEM(weight.shape, BF),
            pltpu.VMEM(cosine.shape, F32),
            pltpu.VMEM(cosine.shape, F32),
            pltpu.SemaphoreType.DMA((blocks + 3,)),
        ],

        cost_estimate=pl.CostEstimate(
            flops=4 * total * total * cols + 6 * total * width * cols,
            bytes_accessed=8 * total * cols + 2 * total * width + 6 * width * cols,
            transcendentals=heads * total * total,
        ),
        name="attend_forward",
    )(
        *normed_blocks,
        weight,
        cosine,
        sine,
        bias[None, :],
        segment[:, None],
        segment[None, :],
    )


def attend_back(queries, keys, values, grad_blocks, log_totals, cosine, sine, segment):
    total, cols = queries.shape
    heads = cols // HD
    block = min(QUERY_ROWS, total)
    blocks, rows = len(grad_blocks), grad_blocks[0].shape[0]

    def kernel(*refs):
        big_refs, block_refs = refs[:5], refs[5 : 5 + blocks]
        (
            lse_ref,
            segc_ref,
            segr_ref,
            d_ref,
            q_ref,
            k_ref,
            v_ref,
            cos_ref,
            sin_ref,
            g_ref,
            kt_ref,
            bias_ref,
            dk_sum,
            dv_sum,
            sems,
        ) = refs[5 + blocks :]
        held = (q_ref, k_ref, v_ref, cos_ref, sin_ref)
        copies = [pltpu.make_async_copy(big_refs[i], held[i], sems.at[i]) for i in range(5)] + [
            pltpu.make_async_copy(block_refs[i], g_ref.at[pl.ds(i * rows, rows)], sems.at[5 + i])
            for i in range(blocks)
        ]
        for copy in copies:
            copy.start()
        dk_sum[...] = jnp.zeros_like(dk_sum)
        dv_sum[...] = jnp.zeros_like(dv_sum)
        for copy in copies:
            copy.wait()
        kt_ref[...] = k_ref[...].T

        def one(i, carried):
            row = pl.multiple_of(i * block, block)
            at = pl.ds(row, block)
            same = segc_ref[...] == segr_ref[:, at]
            bias_ref[...] = jnp.where(same, 0.0, mask_value)
            outs = []
            for h in range(heads):
                c = slice(h * HD, (h + 1) * HD)
                query, grad = q_ref[at, c], g_ref[at, c]
                scores = product(k_ref[:, c], query, 1, 1) * (HD**-0.5) + bias_ref[...]
                probs = jnp.exp(scores - lse_ref[h : h + 1, at])
                both = probs * product(v_ref[:, c], grad, 1, 1)
                inner = jnp.sum(both, axis=0, keepdims=True)
                grad_scores = (both - probs * inner).astype(BF)
                dv_sum[:, c] += product(probs.astype(BF), grad, 1, 0)
                dk_sum[:, c] += product(grad_scores, query, 1, 0)
                outs.append(product(kt_ref[c, :], grad_scores, 1, 0))
            grad_query = (jnp.concatenate(outs, axis=0) * (HD**-0.5)).T.astype(BF).astype(F32)
            d_ref[at, :cols] = turn_halves(grad_query, cos_ref[at, :], -sin_ref[at, :]).astype(BF)
            return carried

        lax.fori_loop(0, total // block, one, 0)
        grad_key = (dk_sum[...] * (HD**-0.5)).astype(BF).astype(F32)
        d_ref[:, cols : 2 * cols] = turn_halves(grad_key, cos_ref[...], -sin_ref[...]).astype(BF)
        d_ref[:, 2 * cols :] = dv_sum[...].astype(BF)

    return pl.pallas_call(
        kernel,
        out_shape=jax.ShapeDtypeStruct((total, 3 * cols), BF),
        in_specs=any_refs(5 + blocks) + [vmem_ref()] * 3,
        out_specs=vmem_ref(),
        scratch_shapes=[pltpu.VMEM((total, cols), BF)] * 3
        + [pltpu.VMEM(cosine.shape, F32)] * 2
        + [
            pltpu.VMEM((total, cols), BF),
            pltpu.VMEM((cols, total), BF),
            pltpu.VMEM((total, block), F32),
            pltpu.VMEM((total, cols), F32),
            pltpu.VMEM((total, cols), F32),
            pltpu.SemaphoreType.DMA((5 + blocks,)),
        ],

        cost_estimate=pl.CostEstimate(
            flops=10 * total * total * cols,
            bytes_accessed=14 * total * cols,
            transcendentals=heads * total * total,
        ),
        name="attend_backward",
    )(
        queries,
        keys,
        values,
        cosine,
        sine,
        *grad_blocks,
        log_totals,
        segment[:, None],
        segment[None, :],
    )


def gelu_both(values):
    root = math.sqrt(2.0 / math.pi)
    square = values * values
    tanh = jnp.tanh(root * (values + 0.044715 * (values * square)))
    half = 0.5 * (1.0 + tanh)
    slope = root * (1.0 + 3 * 0.044715 * square)
    return values * half, half + 0.5 * values * (1.0 - tanh * tanh) * slope


def feed_forward(normed_blocks, grad_blocks, weights, up_bias, up_rows):
    sources = list(normed_blocks) + list(grad_blocks)
    count, width = len(sources), normed_blocks[0].shape[1]
    total = sum(block.shape[0] for block in normed_blocks)
    parts, both_rows, ff = weights.shape
    down_rows = both_rows - up_rows
    group = max(1, 256 // down_rows)
    block, half = group * down_rows, total // 2
    steps = ff // block

    def kernel(*refs):
        (
            weight_from,
            b_ref,
            act_ref,
            gh_ref,
            sum_ref,
            keep_ref,
            send_ref,
            x_ref,
            g_ref,
            acc_ref,
            w_ref,
            hidden_ref,
            active_ref,
            old_hidden_ref,
            old_active_ref,
            sems,
        ) = refs[count:]
        step = pl.program_id(0)
        copies, first = [], 0
        for i, ref in enumerate(refs[:count]):
            whole = x_ref if i < len(normed_blocks) else g_ref
            at = pl.ds(first % total, ref.shape[0])
            copies.append(pltpu.make_async_copy(ref, whole.at[at], sems.at[i]))
            first += ref.shape[0]
        copies.append(pltpu.make_async_copy(weight_from, w_ref, sems.at[count]))

        @pl.when(step == 0)
        def _():
            for copy in copies:
                copy.start()
            for copy in copies:
                copy.wait()

        def up_of(i):
            at = pl.ds(pl.multiple_of(i * block, block), block)
            return w_ref[:, :up_rows, at].reshape(width, block)

        now, before = jnp.minimum(step, steps - 1), jnp.maximum(step - 1, 0)
        old_hidden_ref[...] = hidden_ref[...]
        old_active_ref[...] = active_ref[...]
        hidden_ref[...] = product(x_ref[...], up_of(now), 1, 0) + b_ref[now]
        down = w_ref[pl.ds(now * group, group), up_rows:, :].reshape(block, width)
        active_ref[...] = product(g_ref[...], down, 1, 1)

        active, slope = gelu_both(old_hidden_ref[...])
        act_ref[...] = active.astype(BF)
        grad_hidden = (old_active_ref[...] * slope).astype(BF)
        gh_ref[...] = grad_hidden
        sum_ref[...] = jnp.sum(grad_hidden.astype(F32), axis=0, keepdims=True)
        part = product(grad_hidden, up_of(before), 1, 1)

        @pl.when(step <= 1)
        def _():
            acc_ref[...] = part

        @pl.when(step > 1)
        def _():
            acc_ref[...] += part

        @pl.when(step == steps)
        def _():
            keep_ref[...] = acc_ref[:half, :]
            send_ref[...] = acc_ref[half:, :].astype(BF)

    fixed = lambda i: (0, 0)
    behind = lambda i: (0, jnp.maximum(i - 1, 0))
    return pl.pallas_call(
        kernel,
        grid=(steps + 1,),
        out_shape=(
            jax.ShapeDtypeStruct((total, ff), BF),
            jax.ShapeDtypeStruct((total, ff), BF),
            jax.ShapeDtypeStruct((1, ff), F32),
            jax.ShapeDtypeStruct((half, width), F32),
            jax.ShapeDtypeStruct((half, width), BF),
        ),
        in_specs=any_refs(count + 1) + [pl.BlockSpec((steps, 1, block), lambda i: (0, 0, 0))],
        out_specs=(
            pl.BlockSpec((total, block), behind),
            pl.BlockSpec((total, block), behind),
            pl.BlockSpec((1, block), behind),
            pl.BlockSpec((half, width), fixed),
            pl.BlockSpec((half, width), fixed),
        ),
        scratch_shapes=[
            pltpu.VMEM((total, width), BF),
            pltpu.VMEM((total, width), BF),
            pltpu.VMEM((total, width), F32),
            pltpu.VMEM(weights.shape, BF),
            pltpu.VMEM((total, block), F32),
            pltpu.VMEM((total, block), F32),
            pltpu.VMEM((total, block), F32),
            pltpu.VMEM((total, block), F32),
            pltpu.SemaphoreType.DMA((count + 1,)),
        ],

        cost_estimate=pl.CostEstimate(
            flops=6 * total * width * ff,
            bytes_accessed=2 * (4 * total * width + 2 * total * ff + 2 * width * ff),
            transcendentals=total * ff,
        ),
        name="feed_forward",
    )(*sources, weights, up_bias.reshape(steps, 1, block))


def feed_forward_weights(normed_blocks, grad_hidden, active, grad_blocks, weights, up_rows):
    sources = list(normed_blocks) + list(grad_blocks)
    count, width = len(sources), normed_blocks[0].shape[1]
    total, ff = active.shape
    parts = weights.shape[0]
    down_rows = ff // parts
    group = max(1, min(parts, 256 // up_rows))
    steps = parts // group
    tall, near = total // steps, steps // 2

    def kernel(*refs):
        (
            gh_from,
            weight_from,
            a_ref,
            r_ref,
            o_ref,
            keep_ref,
            send_ref,
            x_ref,
            g_ref,
            gh_ref,
            down_ref,
            sems,
        ) = refs[count:]
        step = pl.program_id(0)
        copies, first = [], 0
        for i, ref in enumerate(refs[:count]):
            whole = x_ref if i < len(normed_blocks) else g_ref
            at = pl.ds(first % total, ref.shape[0])
            copies.append(pltpu.make_async_copy(ref, whole.at[at], sems.at[i]))
            first += ref.shape[0]
        copies.append(pltpu.make_async_copy(gh_from, gh_ref, sems.at[count]))
        copies.append(
            pltpu.make_async_copy(weight_from.at[:, up_rows:, :], down_ref, sems.at[count + 1])
        )

        left, right = len(normed_blocks), count
        order = copies[:left] + copies[right : right + 1] + copies[left:right] + copies[right + 1 :]

        @pl.when(step == 0)
        def _():
            for copy in order:
                copy.start()
            for copy in order[: left + 1]:
                copy.wait()

        at = pl.ds(pl.multiple_of(step * (group * up_rows), group * up_rows), group * up_rows)
        up = product(x_ref[:, at], gh_ref[...], 0, 0).astype(BF)
        for i in range(group):
            o_ref[i, :up_rows, :] = up[i * up_rows : (i + 1) * up_rows]

        @pl.when(step == 0)
        def _():
            for copy in order[left + 1 :]:
                copy.wait()

        down = product(a_ref[...], g_ref[...], 0, 0).astype(BF)
        for i in range(group):
            o_ref[i, up_rows:, :] = down[i * down_rows : (i + 1) * down_rows]
        result = product(r_ref[...], down_ref[...].reshape(ff, width), 1, 0)

        @pl.when(step < near)
        def _():
            keep_ref[...] = result

        @pl.when(step >= near)
        def _():
            send_ref[...] = result.astype(BF)

    return pl.pallas_call(
        kernel,
        grid=(steps,),
        out_shape=(
            jax.ShapeDtypeStruct((parts, up_rows + down_rows, width), BF),
            jax.ShapeDtypeStruct((total // 2, width), F32),
            jax.ShapeDtypeStruct((total // 2, width), BF),
        ),
        in_specs=any_refs(count + 2)
        + [
            pl.BlockSpec((total, group * down_rows), lambda i: (0, i)),
            pl.BlockSpec((tall, ff), lambda i: (i, 0)),
        ],
        out_specs=(
            pl.BlockSpec((group, up_rows + down_rows, width), lambda i: (i, 0, 0)),
            pl.BlockSpec((tall, width), lambda i: (jnp.minimum(i, near - 1), 0)),
            pl.BlockSpec((tall, width), lambda i: (jnp.maximum(i - near, 0), 0)),
        ),
        scratch_shapes=[
            pltpu.VMEM((total, width), BF),
            pltpu.VMEM((total, width), BF),
            pltpu.VMEM((total, ff), BF),
            pltpu.VMEM((parts, down_rows, width), BF),
            pltpu.SemaphoreType.DMA((count + 2,)),
        ],
        cost_estimate=pl.CostEstimate(
            flops=6 * total * width * ff,
            bytes_accessed=2 * (2 * total * (width + ff) + 2 * width * ff),
            transcendentals=0,
        ),
        name="feed_forward_weights",
    )(*sources, grad_hidden, weights, active, active)


def own_time_features(times, first_col, col_count, model_width):
    half_width = model_width // 2
    cols = first_col + jnp.arange(col_count, dtype=jnp.int32)
    is_sine = cols < half_width
    steps_row = jnp.where(is_sine, cols, cols - half_width).astype(F32)
    frequency = jnp.exp(steps_row * (-math.log(10000.0) / (half_width - 1)))
    phase_arg = 1000.0 * times[:, None] * frequency[None, :]
    features = jnp.where(is_sine[None, :], jnp.sin(phase_arg), jnp.cos(phase_arg))
    return jax.nn.silu(features).astype(BF)


def pad_rows(vector):
    rows = -(-vector.shape[-1] // LANES)
    return jnp.pad(vector, (0, rows * LANES - vector.shape[-1])).reshape(rows, LANES)


def body(
    frames,
    skip_frames,
    lengths,
    flow_time,
    skip_weight,
    adaln_weight,
    adaln_bias,
    qkv_weight,
    qkv_bias,
    output_weight,
    output_bias,
    up_weight,
    up_bias,
    down_weight,
    down_bias,
    out_grad,
):
    n_u, n_s = lax.axis_size("utt"), lax.axis_size("sp")
    u, s = lax.axis_index("utt"), lax.axis_index("sp")
    n_all = n_u * n_s
    me = u * n_s + s
    rows, width = frames.shape
    per_group = lengths.shape[1]
    ff = up_weight.shape[1]
    part_width = width // n_s
    part_ff = ff // n_s
    lengths_row = lengths[0]

    all_ids = jnp.concatenate(
        [(s ^ d) * rows + jnp.arange(rows, dtype=jnp.int32) for d in block_order(n_s)]
    )
    inside_all, segment_all, position_all = utterance_layout(lengths_row, all_ids)
    inside = inside_all[:rows]

    cols = qkv_weight.shape[0]
    slot, out_slot = skip_weight.shape[0], output_weight.shape[0]
    far = n_s // 2
    bias_sizes = [qkv_bias.shape[0], output_bias.shape[0], up_bias.shape[0], down_bias.shape[0]]
    bias_own = pad_rows(
        jnp.concatenate([qkv_bias, output_bias, up_bias, down_bias]).astype(F32)
    )
    qkv_split = qkv_weight.reshape(cols, 3, n_s, part_width).transpose(2, 0, 1, 3)
    up_split = up_weight.reshape(cols, n_u, n_s, ff // n_all).transpose(2, 0, 1, 3)
    both_split = jnp.concatenate(
        [qkv_split.reshape(n_s, cols, 3 * part_width), up_split.reshape(n_s, cols, part_ff)], axis=2
    )
    skip_blocks = line_blocks(skip_weight)
    flow_row = jnp.pad(flow_time, ((0, 0), (0, LANES - per_group)))
    first_rows = jnp.concatenate([flow_row, bias_own], axis=0)
    both_mine = lax.all_to_all(both_split, "sp", 0, 0, tiled=True)
    first_rows = lax.all_to_all(
        jnp.broadcast_to(after(first_rows, both_mine)[None], (n_u,) + first_rows.shape),
        "utt",
        0,
        0,
        tiled=True,
    )
    part = n_u * slot
    chosen = jnp.arange(2 * width, dtype=jnp.int32)
    chosen = chosen % part // slot * (slot * n_s) + chosen // part * slot + chosen % slot
    selection = (jnp.arange(2 * width, dtype=jnp.int32)[:, None] == chosen[None, :]).astype(BF)
    joined_split = dot32(jnp.concatenate([frames, skip_frames], axis=1), selection).astype(BF)
    joined_split = joined_split.reshape(rows, n_s, part).transpose(1, 0, 2)
    joined_sent = far_entries(joined_split)
    skip_blocks, both_mine, joined_split, joined_sent = fence(
        (skip_blocks, both_mine, joined_split, joined_sent)
    )
    skip_line = jnp.concatenate(skip_blocks, axis=0)
    both_mine = both_mine.reshape(n_s * cols, -1)
    my_qkv = lax.all_gather(both_mine[:, : 3 * part_width], "utt", axis=0, tiled=True)
    ff_lines = lax.all_gather(
        jnp.concatenate([both_mine[:, 3 * part_width :], down_weight], axis=0), "utt", axis=0
    )

    times = first_rows[:, 0, :per_group].reshape(n_u * per_group)
    feature_rows = adaln_weight.shape[0]
    silu_own = own_time_features(times, me * feature_rows, feature_rows, width)
    table_width = adaln_weight.shape[1]
    mod_terms = dot32(silu_own, adaln_weight)
    bias_cols = lax.dynamic_update_slice(
        jnp.zeros((table_width,), F32), adaln_bias.astype(F32), (me * adaln_bias.shape[0],)
    )
    mod_terms = (mod_terms + bias_cols[None, :]).reshape(n_u, per_group, 6, width)
    mod_terms = mod_terms.transpose(0, 2, 1, 3).reshape(n_u, 6 * per_group, width)

    high, half = skip_line.shape[0] // slot, slot // 2
    rows_of = lambda x: x.reshape(high, slot, width)
    over_sp, over_utt = xor_sp(skip_line, far), swap_utt(skip_line)
    near_line = xor_sp(skip_line, 1)
    mod_terms = lax.all_to_all(mod_terms, "utt", 0, 0, tiled=True)
    cosine, sine = rotary_tables(position_all)
    over_sp, over_utt, near_line, cosine, sine = fence(
        (over_sp, over_utt, near_line, cosine, sine)
    )
    top = xor_sp(rows_of(over_utt)[:, :half].reshape(high * half, width), far)
    bottom = swap_utt(rows_of(over_sp)[:, half:].reshape(high * half, width))
    near_sp, near_utt = xor_sp(over_sp, 1), xor_sp(over_utt, 1)
    table_rows = 6 * per_group
    bias_own = first_rows[:, 1:].reshape(-1, width)
    top, bottom, near_sp, near_utt, mod_terms = fence((top, bottom, near_sp, near_utt, mod_terms))
    corner = jnp.concatenate([top, bottom], axis=0)
    message = jnp.concatenate([jnp.sum(mod_terms, axis=0), bias_own], axis=0)
    corner, message, joined_sent = fence((corner, message, joined_sent))
    output_blocks = lax.all_to_all(
        jnp.broadcast_to(after(output_weight, corner)[None], (n_u, out_slot, width)),
        "utt",
        0,
        0,
        tiled=True,
    ).reshape(n_u * out_slot, width)
    near_corner, message_far = fence((xor_sp(corner, 1), xor_sp(message, far)))
    joined_far = xor_sp(joined_sent, far)
    message = jnp.concatenate(
        [message[:table_rows] + message_far[:table_rows], bias_own, message_far[table_rows:]], axis=0
    )
    message_near = xor_sp(message, 1)
    mod_table = message[:table_rows] + message_near[:table_rows]
    bias_blocks = [
        m.reshape(2, n_u, -1)[i]
        for m in (message[table_rows:], message_near[table_rows:])
        for i in range(2)
    ]
    here, there = line_indices(False), line_indices(True)
    skip_pieces = Pieces()
    whole_row = lambda i, distance: (i * n_s + (s ^ distance)) * slot
    for array, owners, distance in (
        (skip_line, here, 0),
        (over_sp, here, far),
        (over_utt, there, 0),
        (near_line, here, 1),
        (near_sp, here, far ^ 1),
        (near_utt, there, 1),
    ):
        skip_pieces.add(array, [whole_row(i, distance) for i in owners], slot)
    for array, distance in ((corner, far), (near_corner, far ^ 1)):
        skip_pieces.add(
            array,
            [whole_row(i, distance) for i in there]
            + [whole_row(i, distance) + half for i in there],
            half,
        )

    def segment_sums(values):
        return jnp.stack(
            [jnp.sum(jnp.where(inside[:, k][:, None], values, 0.0), axis=0) for k in range(per_group)]
        )

    full_skip, base_rows = placed_product([frames, skip_frames], skip_pieces, 2 * width)
    base_rows, mod_table, joined_far = fence((base_rows, mod_table, joined_far))

    def expand(block, segment):
        table = mod_table[block * per_group : (block + 1) * per_group]
        result = table[per_group - 1][None, :]
        for k in range(per_group - 2, -1, -1):
            result = jnp.where(segment[:, None] == k, table[k][None, :], result)
        return result

    segment_own = segment_all[:rows]
    scale_attn, gate_attn, shift_ffn, scale_ffn, gate_ffn = [
        expand(i, segment_own) for i in range(1, 6)
    ]
    grad_out = out_grad.astype(F32)
    grad_result = (gate_ffn * grad_out).astype(BF)
    base_norm, base_scale = norm_parts(base_rows)
    normed = (base_norm * (1.0 + scale_attn) + expand(0, segment_own)).astype(BF)
    far_normed = xor_sp(normed, far)
    far_normed, output_blocks, my_qkv, grad_result = fence(
        (far_normed, output_blocks, my_qkv, grad_result)
    )
    grad_result_far = xor_sp(grad_result, far)
    two_normed = jnp.concatenate([normed, far_normed], axis=0)
    near_normed = xor_sp(two_normed, 1)
    joined_mine = exchange_near(joined_split, joined_far)
    near_normed, joined_mine = fence((near_normed, joined_mine))
    output_far = xor_sp(output_blocks, far)
    bias_all = jnp.stack(in_device_order(bias_blocks), axis=1).reshape(n_u, n_s, -1)
    offsets = [0]
    for size in bias_sizes:
        offsets.append(offsets[-1] + size)
    full_qkv_bias, full_output_bias, full_up_bias, full_down_bias = [
        bias_all[:, :, offsets[i] : offsets[i + 1]].reshape(-1) for i in range(4)
    ]
    my_qkv_bias = lax.dynamic_slice_in_dim(
        full_qkv_bias.reshape(3, width), s * part_width, part_width, 1
    ).reshape(-1)
    my_up_bias = lax.dynamic_index_in_dim(
        full_up_bias.reshape(n_u, n_s, -1), s, 1, keepdims=False
    ).reshape(-1)

    normed_all, query_rows, key_rows, value_rows, attended_heads, log_totals = attend(
        [two_normed, near_normed], my_qkv, my_qkv_bias, cosine, sine, segment_all
    )
    attended_heads, output_far, grad_result_far = fence(
        (attended_heads, output_far, grad_result_far)
    )
    arrived = exchange_sp([attended_heads[i * rows : (i + 1) * rows] for i in range(n_s)])
    output_near = xor_sp(jnp.concatenate([output_blocks, output_far], axis=0), 1)
    grad_result_near = xor_sp(jnp.concatenate([grad_result, grad_result_far], axis=0), 1)
    arrived, output_near, grad_result_near = fence((arrived, output_near, grad_result_near))
    output_pieces = whole_pieces(
        [
            (output_blocks, 0, range(n_u), 0, out_slot),
            (output_far, far, range(n_u), 0, out_slot),
        ],
        out_slot,
    )
    output_pieces.add(
        output_near,
        [(i * n_s + (s ^ 1)) * out_slot for i in range(n_u)]
        + [(i * n_s + (s ^ 1 ^ far)) * out_slot for i in range(n_u)],
        out_slot,
    )
    attended = jnp.concatenate(in_device_order(arrived), axis=1)
    full_output, branch = placed_product([attended], output_pieces, width)
    branch = branch + full_output_bias[None, :]
    middle = base_rows + gate_attn * branch
    middle_norm, middle_scale = norm_parts(middle)
    normed_ffn = (middle_norm * (1.0 + scale_ffn) + shift_ffn).astype(BF)

    half_rows = n_s * rows // 2
    far_ffn = xor_sp(normed_ffn, far)
    two_ffn = jnp.concatenate([normed_ffn, far_ffn], axis=0)
    near_ffn = xor_sp(two_ffn, 1)
    ffn_blocks = [two_ffn, near_ffn]
    grad_result_blocks = [grad_result, grad_result_far, grad_result_near]
    active, grad_hidden, grad_up_bias, kept, sent = feed_forward(
        ffn_blocks, grad_result_blocks, ff_lines, my_up_bias, n_s * cols
    )
    arrived = xor_sp(sent, 1)
    far_sent = (kept[rows:] + arrived[rows:].astype(F32)).astype(BF)
    far_sent, active, grad_hidden = fence((far_sent, active, grad_hidden))
    far_sum = xor_sp(far_sent, n_s // 2)

    ff_grads, result_kept, sent = feed_forward_weights(
        ffn_blocks, grad_hidden, active, grad_result_blocks, ff_lines, n_s * cols
    )
    far_sum, result_kept, sent, ff_grads = fence((far_sum, result_kept, sent, ff_grads))
    grad_normed_ffn = kept[:rows] + arrived[:rows].astype(F32) + far_sum.astype(F32)
    ff_mine = lax.psum_scatter(ff_grads, "utt", scatter_dimension=0, tiled=True)[0]
    grad_middle = grad_out + norm_back(
        middle_norm, middle_scale, grad_normed_ffn * (1.0 + scale_ffn)
    )
    grad_branch = (gate_attn * grad_middle).astype(BF)
    grad_attended = dot_nt(grad_branch, full_output).astype(BF)
    grad_heads = exchange_sp(
        [
            lax.dynamic_slice_in_dim(grad_attended, (s ^ d) * part_width, part_width, 1)
            for d in block_order(n_s)
        ]
    )
    result_arrived = xor_sp(after(sent, grad_attended), 1)
    grad_heads, result_arrived, grad_branch = fence((grad_heads, result_arrived, grad_branch))
    far_branch = xor_sp(grad_branch, far)
    result_sent = (result_kept[rows:] + result_arrived[rows:].astype(F32)).astype(BF)

    grad_projected = attend_back(
        query_rows, key_rows, value_rows, grad_heads, log_totals, cosine, sine, segment_all
    )
    grad_projected, far_branch = fence((grad_projected, far_branch))
    sent = product(grad_projected[half_rows:], my_qkv, 1, 1).astype(BF)
    kept = product(grad_projected[:half_rows], my_qkv, 1, 1)
    arrived = xor_sp(sent, 1)
    far_sent = (kept[rows:] + arrived[rows:].astype(F32)).astype(BF)
    far_sent, projected_late, far_branch, middle_late, nffn_late = fence(
        (far_sent, grad_projected, far_branch, grad_middle, grad_normed_ffn)
    )
    far_sum = xor_sp(far_sent, far)

    grad_qkv = dot_tn(normed_all, projected_late).astype(BF)
    my_qkv_bias_grad = jnp.sum(projected_late.astype(F32), axis=0)
    qkv_keep, qkv_send = split_pair(grad_qkv.reshape(-1, 2, n_s * cols, 3 * part_width), 1)
    qkv_arrived = swap_utt(qkv_send)
    branch_blocks, step = [grad_branch, far_branch], n_s // 4
    while step >= 1:
        branch_blocks = branch_blocks + [xor_sp(b, step) for b in branch_blocks]
        step //= 2
    grad_output = dot_tn(attended_heads, jnp.concatenate(branch_blocks, axis=0)).astype(BF)
    grad_output_bias = jnp.sum((gate_attn * middle_late).astype(BF).astype(F32), axis=0)
    early_tables = [
        segment_sums(v) for v in (middle_late * branch, nffn_late, nffn_late * middle_norm)
    ]
    far_sum, early_tables, qkv_keep, qkv_arrived, grad_output = fence(
        (far_sum, early_tables, qkv_keep, qkv_arrived, grad_output)
    )
    grad_normed = kept[:rows] + arrived[:rows].astype(F32) + far_sum.astype(F32)

    grad_base = (
        grad_middle + norm_back(base_norm, base_scale, grad_normed * (1.0 + scale_attn))
    ).astype(BF)
    far_base = xor_sp(grad_base, far)
    out_keep, out_send = split_pair(grad_output.reshape(-1, 2, out_slot, width), 1)
    out_arrived = swap_utt(out_send)
    far_base, normed_late, out_arrived = fence((far_base, grad_normed, out_arrived))
    out_half = (out_keep.astype(F32) + out_arrived.astype(F32)).astype(BF)
    two_base = jnp.concatenate([grad_base, far_base], axis=0)
    near_base = xor_sp(two_base, 1)
    grad_skip = dot_tn(
        jnp.concatenate(joined_mine, axis=0), jnp.concatenate([two_base, near_base], axis=0)
    ).astype(BF)
    skip_keep, skip_send = split_pair(grad_skip.reshape((-1, 2) + (slot, width)), 1)
    skip_send, out_half, base_late, normed_late, result_sent, late_grad = fence(
        (skip_send, out_half, grad_base, normed_late, result_sent, out_grad)
    )

    skip_arrived, far_result = swap_utt(skip_send), xor_sp(result_sent, far)
    frames_grad = dot_nt(base_late, full_skip[:width])
    skip_grad = dot_nt(base_late, full_skip[width:])
    late_tables = [segment_sums(v) for v in (normed_late, normed_late * base_norm)]
    skip_arrived, far_result, late_tables, frames_grad, skip_grad, qkv_keep, ff_mine = fence(
        (skip_arrived, far_result, late_tables, frames_grad, skip_grad, qkv_keep, ff_mine)
    )
    qkv_half = (qkv_keep.astype(F32) + qkv_arrived.astype(F32)).astype(BF)
    grad_out = late_grad.astype(F32)
    result = (
        result_kept[:rows]
        + result_arrived[:rows].astype(F32)
        + far_result.astype(F32)
        + full_down_bias[None, :]
    )
    skip_half = (skip_keep.astype(F32) + skip_arrived.astype(F32)).astype(BF)
    skip_half, qkv_half = fence((skip_half, qkv_half))

    skip_terms, qkv_terms = scatter_slow(skip_half), scatter_slow(qkv_half)
    mixed_out = (middle + gate_ffn * result).astype(BF)
    grad_down_bias = jnp.sum((gate_ffn * grad_out).astype(BF).astype(F32), axis=0)
    gate_table = segment_sums(grad_out * result)
    skip_sum = add_terms(skip_terms)
    qkv_mine = add_terms(qkv_terms).astype(BF)
    qkv_mine = qkv_mine.reshape(n_s, cols, 3 * part_width)
    out_sum = to_owner(add_terms(scatter_slow(out_half)))
    qkv_back = split_exchange_sp(qkv_mine)
    qkv_sum = (
        qkv_back.reshape(n_s, cols, 3, part_width).transpose(1, 2, 0, 3).reshape(cols, 3 * width)
    ).astype(F32)
    up_back = split_exchange_sp(ff_mine[: n_s * cols].reshape(n_s, cols, part_ff))
    up_sum = (
        up_back.reshape(n_s, cols, n_u, ff // n_all).transpose(1, 2, 0, 3).reshape(cols, ff)
    ).astype(F32)
    down_sum = ff_mine[n_s * cols :].astype(F32)

    grad_table = jnp.concatenate(late_tables + early_tables + [gate_table], axis=1)
    qkv_bias_slots = lax.dynamic_update_slice(
        jnp.zeros((3, width), F32), my_qkv_bias_grad.reshape(3, part_width), (0, s * part_width)
    ).reshape(-1)
    up_bias_slots = lax.dynamic_update_slice(
        jnp.zeros((n_u, n_s, ff // n_all), F32),
        grad_up_bias.reshape(n_u, 1, ff // n_all),
        (0, s, 0),
    ).reshape(-1)
    bias_vec = jnp.concatenate(
        [
            v.reshape(n_u, -1)
            for v in (qkv_bias_slots, grad_output_bias, up_bias_slots, grad_down_bias)
        ],
        axis=1,
    )
    vec_rows = -(-bias_vec.shape[1] // LANES)
    bias_vec = jnp.pad(bias_vec, ((0, 0), (0, vec_rows * LANES - bias_vec.shape[1])))
    table_rows = per_group * table_width // LANES
    tail = jnp.concatenate(
        [grad_table.reshape(table_rows, LANES), bias_vec.reshape(n_u * vec_rows, LANES)], axis=0
    )
    tail = sum_sp(tail)
    tail = jnp.concatenate(
        [
            jnp.broadcast_to(tail[None, :table_rows], (n_u, table_rows, LANES)),
            tail[table_rows:].reshape(n_u, vec_rows, LANES),
        ],
        axis=1,
    )
    tail = tail.astype(BF)
    tail = lax.all_to_all(tail, "utt", 0, 0, tiled=True).astype(F32)
    table_all = tail[:, :table_rows].reshape(n_u * per_group, table_width)
    adaln_sum = lax.dot_general(
        silu_own.astype(F32),
        table_all,
        (((0,), (0,)), ((), ())),
        precision=highest_precision,
        preferred_element_type=F32,
    )
    adaln_bias_sum = jnp.sum(owned(table_all), axis=0)
    vec = jnp.sum(tail[:, table_rows:], axis=0).reshape(-1)
    bias_sums, start = [], 0
    for size in bias_sizes:
        bias_sums.append(lax.dynamic_slice_in_dim(vec, start + s * size, size, 0))
        start += size * n_s

    return (
        mixed_out,
        frames_grad,
        skip_grad,
        skip_sum,
        adaln_sum,
        adaln_bias_sum,
        qkv_sum,
        bias_sums[0],
        out_sum,
        bias_sums[1],
        up_sum,
        bias_sums[2],
        down_sum,
        bias_sums[3],
    )


def solution(mesh):
    both = ("utt", "sp")
    matrix, vector, group = P(both, None), P(both), P("utt", None)
    return jax.shard_map(
        body,
        mesh=mesh,
        in_specs=(
            matrix,
            matrix,
            group,
            group,
            matrix,
            matrix,
            vector,
            matrix,
            vector,
            matrix,
            vector,
            matrix,
            vector,
            matrix,
            vector,
            matrix,
        ),
        out_specs=(
            matrix,
            matrix,
            matrix,
            matrix,
            matrix,
            vector,
            matrix,
            vector,
            matrix,
            vector,
            matrix,
            vector,
            matrix,
            vector,
        ),
        check_vma=False,
    )
```

```python
import math

import jax
import jax.numpy as jnp
from jax import lax
from jax.experimental import pallas as pl
from jax.experimental.pallas import tpu as pltpu
from jax.sharding import PartitionSpec as P

HD = 64
LANES = 128
BIAS_ROWS = 16
BF = jnp.bfloat16
F32 = jnp.float32
highest_precision = lax.Precision.HIGHEST
mask_value = -1e30


def product(left, right, left_dim, right_dim):
    return lax.dot_general(
        left, right, (((left_dim,), (right_dim,)), ((), ())), preferred_element_type=F32
    )


def dot32(left, right):
    return jnp.dot(left, right, preferred_element_type=F32)


def dot_nt(left, right):
    return lax.dot_general(left, right, (((1,), (1,)), ((), ())), preferred_element_type=F32)


def dot_tn(left, right):
    return lax.dot_general(left, right, (((0,), (0,)), ((), ())), preferred_element_type=F32)


fence = lax.optimization_barrier


def after(value, *others):
    return fence((value, others))[0]


def block_order(count):
    order, step = [0], count // 2
    while step >= 1:
        order = order + [d ^ step for d in order]
        step //= 2
    return order


def xor_sp(values, distance):
    size = lax.axis_size("sp")
    return lax.ppermute(values, "sp", [(i, i ^ distance) for i in range(size)])


def swap_utt(values):
    return lax.ppermute(values, "utt", [(i, i ^ 1) for i in range(lax.axis_size("utt"))])


def gather_sp(own):
    blocks, step = [own], lax.axis_size("sp") // 2
    while step >= 1:
        blocks = blocks + [xor_sp(b, step) for b in blocks]
        step //= 2
    return blocks


def exchange_sp(parts):
    order = block_order(len(parts))
    return [parts[0]] + [xor_sp(parts[i], order[i]) for i in range(1, len(parts))]


def in_device_order(blocks):
    order = block_order(len(blocks))
    stacked = jnp.stack([blocks[order.index(d)] for d in range(len(blocks))])
    me = lax.axis_index("sp")
    return [
        lax.dynamic_index_in_dim(stacked, me ^ a, 0, keepdims=False) for a in range(len(blocks))
    ]


def sum_sp(values):
    step = lax.axis_size("sp") // 2
    while step >= 1:
        values = values + xor_sp(values, step)
        step //= 2
    return values


def turn_utt(values, k):
    size = lax.axis_size("utt")
    high = size // 2
    routes = [(z * 2 + y, (z + k) % high * 2 + y) for z in range(high) for y in range(2)]
    return lax.ppermute(values, "utt", routes)


def line_blocks(own):
    return [own] + [turn_utt(own, k) for k in range(1, lax.axis_size("utt") // 2)]


def gather_line(own):
    return jnp.concatenate(line_blocks(own), axis=0)


def split_pair(parts, axis):
    low = lax.axis_index("utt") % 2
    keep = lax.dynamic_index_in_dim(parts, low, axis, keepdims=False)
    return keep, lax.dynamic_index_in_dim(parts, 1 - low, axis, keepdims=False)


def scatter_fast(parts):
    keep, send = split_pair(parts.reshape((-1, 2) + parts.shape[1:]), 1)
    return (keep.astype(F32) + swap_utt(send.astype(BF)).astype(F32)).astype(BF)


def scatter_slow(half):
    high = lax.axis_size("utt") // 2
    z = lax.axis_index("utt") // 2
    terms = [lax.dynamic_index_in_dim(half, z, 0, keepdims=False)]
    for k in range(1, high):
        piece = lax.dynamic_index_in_dim(half, (z + k) % high, 0, keepdims=False)
        terms.append(turn_utt(piece, k))
    return terms


def add_terms(terms):
    total = terms[0].astype(F32)
    for term in terms[1:]:
        total = total + term.astype(F32)
    return total


def entry(values, index):
    return lax.dynamic_index_in_dim(values, index, 0, keepdims=False)


def far_entries(values):
    me, far = lax.axis_index("sp"), lax.axis_size("sp") // 2
    return jnp.stack([entry(values, me ^ far), entry(values, me ^ far ^ 1)])


def exchange_far(values):
    return xor_sp(far_entries(values), lax.axis_size("sp") // 2)


def exchange_near(values, arrived):
    me = lax.axis_index("sp")
    last = xor_sp(jnp.stack([entry(values, me ^ 1), arrived[1]]), 1)
    return [entry(values, me), arrived[0], last[0], last[1]]


def split_exchange_sp(values):
    return jnp.stack(in_device_order(exchange_near(values, exchange_far(values))))


class Pieces:
    def __init__(self):
        self.arrays, self.starts, self.sizes = [], [], []

    def add(self, array, first_rows, size):
        self.arrays.append(array)
        self.starts.append(first_rows)
        self.sizes.append(size)

    def offsets(self):
        return jnp.stack([start for starts in self.starts for start in starts]).astype(jnp.int32)

    def count(self):
        return sum(len(starts) for starts in self.starts)

    def copies(self, offset_ref, refs, whole_ref, sems):
        made, n = [], 0
        for ref, starts, size in zip(refs, self.starts, self.sizes):
            for i in range(len(starts)):
                first = pl.multiple_of(offset_ref[n], size)
                made.append(
                    pltpu.make_async_copy(
                        ref.at[pl.ds(i * size, size)], whole_ref.at[pl.ds(first, size)], sems.at[n]
                    )
                )
                n += 1
        return made


def line_indices(flip):
    size = lax.axis_size("utt")
    high = size // 2
    u = lax.axis_index("utt")
    z, y = u // 2, u % 2
    return [(z - k + high) % high * 2 + (1 - y if flip else y) for k in range(high)]


def whole_pieces(arrays, rows):
    n_s, me = lax.axis_size("sp"), lax.axis_index("sp")
    pieces = Pieces()
    for array, d, owners, shift, size in arrays:
        pieces.add(array, [(i * n_s + (me ^ d)) * rows + shift for i in owners], size)
    return pieces


def to_owner(values):
    n_u, n_s = lax.axis_size("utt"), lax.axis_size("sp")
    routes = []
    for p in range(n_u):
        for s in range(n_s):
            routes.append((p * n_s + s, s * n_u + p))
    return lax.ppermute(values, ("utt", "sp"), routes)


def owned(values):
    n = lax.axis_size("utt") * lax.axis_size("sp")
    j = lax.axis_index("utt") * lax.axis_size("sp") + lax.axis_index("sp")
    size = values.shape[-1] // n
    return lax.dynamic_slice_in_dim(values, j * size, size, values.ndim - 1)


def norm_parts(values):
    mean_row = jnp.mean(values, axis=-1, keepdims=True)
    centered = values - mean_row
    variance = jnp.mean(centered * centered, axis=-1, keepdims=True)
    scale = lax.rsqrt(variance + 1e-06)
    return centered * scale, scale


def norm_back(normal, scale, grads):
    mean_grad = jnp.mean(grads, axis=-1, keepdims=True)
    mean_both = jnp.mean(grads * normal, axis=-1, keepdims=True)
    return (grads - mean_grad - normal * mean_both) * scale


def rotary_tables(position):
    half_head = HD // 2
    inverse = jnp.exp(jnp.arange(half_head, dtype=F32) * (-2.0 * math.log(10000.0) / HD))
    angle_arg = position.astype(F32)[:, None] * inverse[None, :]
    cosine, sine = jnp.cos(angle_arg), jnp.sin(angle_arg)
    return (
        jnp.concatenate([cosine] * 4, axis=1),
        jnp.concatenate([-sine, sine, -sine, sine], axis=1),
    )


def utterance_layout(lengths_row, frame_ids):
    ends_at = jnp.cumsum(lengths_row)
    starts_at = ends_at - lengths_row
    inside = (frame_ids[:, None] >= starts_at[None, :]) & (frame_ids[:, None] < ends_at[None, :])
    segment = jnp.sum(jnp.where(frame_ids[:, None] >= ends_at[None, :], 1, 0), axis=1).astype(
        jnp.int32
    )
    position = frame_ids - jnp.sum(jnp.where(inside, starts_at[None, :], 0), axis=1)
    return inside, segment, position


QUERY_ROWS = 512


def any_refs(count):
    return [pl.BlockSpec(memory_space=pltpu.HBM)] * count


def smem_ref():
    return pl.BlockSpec(memory_space=pltpu.SMEM)


def vmem_ref():
    return pl.BlockSpec(memory_space=pltpu.VMEM)


def placed_product(lefts, pieces, depth):
    n, count = len(pieces.arrays), pieces.count()
    rows = lefts[0].shape[0]
    width = pieces.arrays[0].shape[1]

    def kernel(offset_ref, *refs):
        piece_refs, left_refs = refs[:n], refs[n : n + len(lefts)]
        whole_ref, base_ref, sems = refs[n + len(lefts) :]
        copies = pieces.copies(offset_ref, piece_refs, whole_ref, sems)
        for copy in copies:
            copy.start()
        for copy in copies:
            copy.wait()
        total, first = None, 0
        for left_ref in left_refs:
            last = first + left_ref.shape[1]
            term = product(left_ref[...], whole_ref[first:last, :], 1, 0)
            total = term if total is None else total + term
            first = last
        base_ref[...] = total

    return pl.pallas_call(
        kernel,
        out_shape=(
            jax.ShapeDtypeStruct((depth, width), BF),
            jax.ShapeDtypeStruct((rows, width), F32),
        ),
        in_specs=[smem_ref()] + any_refs(n) + [vmem_ref()] * len(lefts),
        out_specs=(vmem_ref(),) * 2,
        scratch_shapes=[pltpu.SemaphoreType.DMA((count,))],

        cost_estimate=pl.CostEstimate(
            flops=2 * rows * depth * width,
            bytes_accessed=4 * depth * width + 2 * rows * (depth + 2 * width),
            transcendentals=0,
        ),
        name="placed_product",
    )(pieces.offsets(), *pieces.arrays, *lefts)


def turn_halves(values, cosine, sine):
    half, cols = HD // 2, values.shape[1]
    first = lax.broadcasted_iota(jnp.int32, values.shape, 1) % HD < half
    swapped = jnp.where(
        first, pltpu.roll(values, cols - half, 1), pltpu.roll(values, half, 1)
    )
    repeats = cols // cosine.shape[1]
    wide = lambda t: jnp.concatenate([t] * repeats, axis=1) if repeats > 1 else t
    return values * wide(cosine) + swapped * wide(sine)


def attend(normed_blocks, weight, bias, cosine, sine, segment):
    blocks, width = len(normed_blocks), normed_blocks[0].shape[1]
    rows = normed_blocks[0].shape[0]
    total = blocks * rows
    cols = weight.shape[1] // 3
    heads = cols // HD
    block = min(QUERY_ROWS, total)

    def kernel(*refs):
        block_refs = refs[:blocks]
        (
            weight_ref,
            cos_from,
            sin_from,
            b_ref,
            segc_ref,
            segr_ref,
            x_ref,
            q_ref,
            k_ref,
            v_ref,
            o_ref,
            lse_ref,
            vt_ref,
            bias_ref,
            w_ref,
            cos_ref,
            sin_ref,
            sems,
        ) = refs[blocks:]
        sources = [weight_ref, cos_from, sin_from, *block_refs]
        targets = [w_ref, cos_ref, sin_ref] + [
            x_ref.at[pl.ds(i * rows, rows)] for i in range(blocks)
        ]
        copies = [
            pltpu.make_async_copy(sources[i], targets[i], sems.at[i]) for i in range(3 + blocks)
        ]
        for copy in copies:
            copy.start()

        for copy in copies:
            copy.wait()

        def project(i, carried):
            at = pl.ds(pl.multiple_of(i * block, block), block)
            three = product(x_ref[at, :], w_ref[...], 1, 0) + b_ref[...]
            cosine, sine = cos_ref[at, :], sin_ref[at, :]
            q_ref[at, :] = turn_halves(three[:, :cols], cosine, sine).astype(BF)
            k_ref[at, :] = turn_halves(three[:, cols : 2 * cols], cosine, sine).astype(BF)
            v_ref[at, :] = three[:, 2 * cols :].astype(BF)
            return carried

        lax.fori_loop(0, total // block, project, 0)
        vt_ref[...] = v_ref[...].T

        def one(i, carried):
            row = pl.multiple_of(i * block, block)
            same = segc_ref[...] == segr_ref[:, pl.ds(row, block)]
            bias_ref[...] = jnp.where(same, 0.0, mask_value)
            outs = []
            for h in range(heads):
                c = slice(h * HD, (h + 1) * HD)
                scores = product(k_ref[:, c], q_ref[pl.ds(row, block), c], 1, 1)
                scores = scores * (HD**-0.5) + bias_ref[...]
                top = jnp.max(scores, axis=0, keepdims=True)
                exps = jnp.exp(scores - top)
                totals = jnp.sum(exps, axis=0, keepdims=True)
                outs.append(product(vt_ref[c, :], exps.astype(BF), 1, 0) * (1.0 / totals))
                lse_ref[h : h + 1, pl.ds(row, block)] = top + jnp.log(totals)
            o_ref[pl.ds(row, block), :] = jnp.concatenate(outs, axis=0).T.astype(BF)
            return carried

        lax.fori_loop(0, total // block, one, 0)

    return pl.pallas_call(
        kernel,
        out_shape=(
            jax.ShapeDtypeStruct((total, width), BF),
            jax.ShapeDtypeStruct((total, cols), BF),
            jax.ShapeDtypeStruct((total, cols), BF),
            jax.ShapeDtypeStruct((total, cols), BF),
            jax.ShapeDtypeStruct((total, cols), BF),
            jax.ShapeDtypeStruct((heads, total), F32),
        ),
        in_specs=any_refs(blocks + 3) + [vmem_ref()] * 3,
        out_specs=(vmem_ref(),) * 6,
        scratch_shapes=[
            pltpu.VMEM((cols, total), BF),
            pltpu.VMEM((total, block), F32),
            pltpu.VMEM(weight.shape, BF),
            pltpu.VMEM(cosine.shape, F32),
            pltpu.VMEM(cosine.shape, F32),
            pltpu.SemaphoreType.DMA((blocks + 3,)),
        ],

        cost_estimate=pl.CostEstimate(
            flops=4 * total * total * cols + 6 * total * width * cols,
            bytes_accessed=8 * total * cols + 2 * total * width + 6 * width * cols,
            transcendentals=heads * total * total,
        ),
        name="attend_forward",
    )(
        *normed_blocks,
        weight,
        cosine,
        sine,
        bias[None, :],
        segment[:, None],
        segment[None, :],
    )


def attend_back(queries, keys, values, grad_blocks, log_totals, cosine, sine, segment):
    total, cols = queries.shape
    heads = cols // HD
    block = min(QUERY_ROWS, total)
    blocks, rows = len(grad_blocks), grad_blocks[0].shape[0]

    def kernel(*refs):
        big_refs, block_refs = refs[:5], refs[5 : 5 + blocks]
        (
            lse_ref,
            segc_ref,
            segr_ref,
            d_ref,
            q_ref,
            k_ref,
            v_ref,
            cos_ref,
            sin_ref,
            g_ref,
            kt_ref,
            bias_ref,
            dk_sum,
            dv_sum,
            sems,
        ) = refs[5 + blocks :]
        held = (q_ref, k_ref, v_ref, cos_ref, sin_ref)
        copies = [pltpu.make_async_copy(big_refs[i], held[i], sems.at[i]) for i in range(5)] + [
            pltpu.make_async_copy(block_refs[i], g_ref.at[pl.ds(i * rows, rows)], sems.at[5 + i])
            for i in range(blocks)
        ]
        for copy in copies:
            copy.start()
        dk_sum[...] = jnp.zeros_like(dk_sum)
        dv_sum[...] = jnp.zeros_like(dv_sum)
        for copy in copies:
            copy.wait()
        kt_ref[...] = k_ref[...].T

        def one(i, carried):
            row = pl.multiple_of(i * block, block)
            at = pl.ds(row, block)
            same = segc_ref[...] == segr_ref[:, at]
            bias_ref[...] = jnp.where(same, 0.0, mask_value)
            outs = []
            for h in range(heads):
                c = slice(h * HD, (h + 1) * HD)
                query, grad = q_ref[at, c], g_ref[at, c]
                scores = product(k_ref[:, c], query, 1, 1) * (HD**-0.5) + bias_ref[...]
                probs = jnp.exp(scores - lse_ref[h : h + 1, at])
                both = probs * product(v_ref[:, c], grad, 1, 1)
                inner = jnp.sum(both, axis=0, keepdims=True)
                grad_scores = (both - probs * inner).astype(BF)
                dv_sum[:, c] += product(probs.astype(BF), grad, 1, 0)
                dk_sum[:, c] += product(grad_scores, query, 1, 0)
                outs.append(product(kt_ref[c, :], grad_scores, 1, 0))
            grad_query = (jnp.concatenate(outs, axis=0) * (HD**-0.5)).T.astype(BF).astype(F32)
            d_ref[at, :cols] = turn_halves(grad_query, cos_ref[at, :], -sin_ref[at, :]).astype(BF)
            return carried

        lax.fori_loop(0, total // block, one, 0)
        grad_key = (dk_sum[...] * (HD**-0.5)).astype(BF).astype(F32)
        d_ref[:, cols : 2 * cols] = turn_halves(grad_key, cos_ref[...], -sin_ref[...]).astype(BF)
        d_ref[:, 2 * cols :] = dv_sum[...].astype(BF)

    return pl.pallas_call(
        kernel,
        out_shape=jax.ShapeDtypeStruct((total, 3 * cols), BF),
        in_specs=any_refs(5 + blocks) + [vmem_ref()] * 3,
        out_specs=vmem_ref(),
        scratch_shapes=[pltpu.VMEM((total, cols), BF)] * 3
        + [pltpu.VMEM(cosine.shape, F32)] * 2
        + [
            pltpu.VMEM((total, cols), BF),
            pltpu.VMEM((cols, total), BF),
            pltpu.VMEM((total, block), F32),
            pltpu.VMEM((total, cols), F32),
            pltpu.VMEM((total, cols), F32),
            pltpu.SemaphoreType.DMA((5 + blocks,)),
        ],

        cost_estimate=pl.CostEstimate(
            flops=10 * total * total * cols,
            bytes_accessed=14 * total * cols,
            transcendentals=heads * total * total,
        ),
        name="attend_backward",
    )(
        queries,
        keys,
        values,
        cosine,
        sine,
        *grad_blocks,
        log_totals,
        segment[:, None],
        segment[None, :],
    )


def gelu_both(values):
    root = math.sqrt(2.0 / math.pi)
    square = values * values
    tanh = jnp.tanh(root * (values + 0.044715 * (values * square)))
    half = 0.5 * (1.0 + tanh)
    slope = root * (1.0 + 3 * 0.044715 * square)
    return values * half, half + 0.5 * values * (1.0 - tanh * tanh) * slope


def feed_forward(normed_blocks, grad_blocks, weights, up_bias, up_rows):
    sources = list(normed_blocks) + list(grad_blocks)
    count, width = len(sources), normed_blocks[0].shape[1]
    total = sum(block.shape[0] for block in normed_blocks)
    parts, both_rows, ff = weights.shape
    down_rows = both_rows - up_rows
    group = max(1, 256 // down_rows)
    block, half = group * down_rows, total // 2
    steps = ff // block

    def kernel(*refs):
        (
            weight_from,
            b_ref,
            act_ref,
            gh_ref,
            sum_ref,
            keep_ref,
            send_ref,
            x_ref,
            g_ref,
            acc_ref,
            w_ref,
            hidden_ref,
            active_ref,
            old_hidden_ref,
            old_active_ref,
            sems,
        ) = refs[count:]
        step = pl.program_id(0)
        copies, first = [], 0
        for i, ref in enumerate(refs[:count]):
            whole = x_ref if i < len(normed_blocks) else g_ref
            at = pl.ds(first % total, ref.shape[0])
            copies.append(pltpu.make_async_copy(ref, whole.at[at], sems.at[i]))
            first += ref.shape[0]
        copies.append(pltpu.make_async_copy(weight_from, w_ref, sems.at[count]))

        def up_of(i):
            at = pl.ds(pl.multiple_of(i * block, block), block)
            return w_ref[:, :up_rows, at].reshape(width, block)

        def products():
            hidden_ref[...] = product(x_ref[...], up_of(step), 1, 0) + b_ref[step]
            down = w_ref[pl.ds(step * group, group), up_rows:, :].reshape(block, width)
            active_ref[...] = product(g_ref[...], down, 1, 1)

        def shift():
            old_hidden_ref[...] = hidden_ref[...]
            old_active_ref[...] = active_ref[...]

        def rest():
            active, slope = gelu_both(old_hidden_ref[...])
            act_ref[...] = active.astype(BF)
            grad_hidden = (old_active_ref[...] * slope).astype(BF)
            gh_ref[...] = grad_hidden
            sum_ref[...] = jnp.sum(grad_hidden.astype(F32), axis=0, keepdims=True)
            acc_ref[...] += product(grad_hidden, up_of(step - 1), 1, 1)

        @pl.when(step == 0)
        def _():
            for copy in copies:
                copy.start()
            acc_ref[...] = jnp.zeros_like(acc_ref)
            for copy in copies:
                copy.wait()
            products()

        @pl.when((step > 0) & (step < steps))
        def _():
            shift()
            products()
            rest()

        @pl.when(step == steps)
        def _():
            shift()
            rest()

        @pl.when(step == steps)
        def _():
            keep_ref[...] = acc_ref[:half, :]
            send_ref[...] = acc_ref[half:, :].astype(BF)

    fixed = lambda i: (0, 0)
    behind = lambda i: (0, jnp.maximum(i - 1, 0))
    return pl.pallas_call(
        kernel,
        grid=(steps + 1,),
        out_shape=(
            jax.ShapeDtypeStruct((total, ff), BF),
            jax.ShapeDtypeStruct((total, ff), BF),
            jax.ShapeDtypeStruct((1, ff), F32),
            jax.ShapeDtypeStruct((half, width), F32),
            jax.ShapeDtypeStruct((half, width), BF),
        ),
        in_specs=any_refs(count + 1) + [pl.BlockSpec((steps, 1, block), lambda i: (0, 0, 0))],
        out_specs=(
            pl.BlockSpec((total, block), behind),
            pl.BlockSpec((total, block), behind),
            pl.BlockSpec((1, block), behind),
            pl.BlockSpec((half, width), fixed),
            pl.BlockSpec((half, width), fixed),
        ),
        scratch_shapes=[
            pltpu.VMEM((total, width), BF),
            pltpu.VMEM((total, width), BF),
            pltpu.VMEM((total, width), F32),
            pltpu.VMEM(weights.shape, BF),
            pltpu.VMEM((total, block), F32),
            pltpu.VMEM((total, block), F32),
            pltpu.VMEM((total, block), F32),
            pltpu.VMEM((total, block), F32),
            pltpu.SemaphoreType.DMA((count + 1,)),
        ],

        cost_estimate=pl.CostEstimate(
            flops=6 * total * width * ff,
            bytes_accessed=2 * (4 * total * width + 2 * total * ff + 2 * width * ff),
            transcendentals=total * ff,
        ),
        name="feed_forward",
    )(*sources, weights, up_bias.reshape(steps, 1, block))


def feed_forward_weights(normed_blocks, grad_hidden, active, grad_blocks, weights, up_rows):
    sources = list(normed_blocks) + list(grad_blocks)
    count, width = len(sources), normed_blocks[0].shape[1]
    total, ff = active.shape
    parts = weights.shape[0]
    down_rows = ff // parts
    group = max(1, min(parts, 256 // up_rows))
    steps = parts // group
    tall, near = total // steps, steps // 2

    def kernel(*refs):
        (
            gh_from,
            weight_from,
            a_ref,
            r_ref,
            o_ref,
            keep_ref,
            send_ref,
            x_ref,
            g_ref,
            gh_ref,
            down_ref,
            sems,
        ) = refs[count:]
        step = pl.program_id(0)
        copies, first = [], 0
        for i, ref in enumerate(refs[:count]):
            whole = x_ref if i < len(normed_blocks) else g_ref
            at = pl.ds(first % total, ref.shape[0])
            copies.append(pltpu.make_async_copy(ref, whole.at[at], sems.at[i]))
            first += ref.shape[0]
        copies.append(pltpu.make_async_copy(gh_from, gh_ref, sems.at[count]))
        copies.append(
            pltpu.make_async_copy(weight_from.at[:, up_rows:, :], down_ref, sems.at[count + 1])
        )

        left, right = len(normed_blocks), count
        order = copies[:left] + copies[right : right + 1] + copies[left:right] + copies[right + 1 :]

        @pl.when(step == 0)
        def _():
            for copy in order:
                copy.start()
            for copy in order[: left + 1]:
                copy.wait()

        at = pl.ds(pl.multiple_of(step * (group * up_rows), group * up_rows), group * up_rows)
        up = product(x_ref[:, at], gh_ref[...], 0, 0).astype(BF)
        for i in range(group):
            o_ref[i, :up_rows, :] = up[i * up_rows : (i + 1) * up_rows]

        @pl.when(step == 0)
        def _():
            for copy in order[left + 1 :]:
                copy.wait()

        down = product(a_ref[...], g_ref[...], 0, 0).astype(BF)
        for i in range(group):
            o_ref[i, up_rows:, :] = down[i * down_rows : (i + 1) * down_rows]
        result = product(r_ref[...], down_ref[...].reshape(ff, width), 1, 0)

        @pl.when(step < near)
        def _():
            keep_ref[...] = result

        @pl.when(step >= near)
        def _():
            send_ref[...] = result.astype(BF)

    return pl.pallas_call(
        kernel,
        grid=(steps,),
        out_shape=(
            jax.ShapeDtypeStruct((parts, up_rows + down_rows, width), BF),
            jax.ShapeDtypeStruct((total // 2, width), F32),
            jax.ShapeDtypeStruct((total // 2, width), BF),
        ),
        in_specs=any_refs(count + 2)
        + [
            pl.BlockSpec((total, group * down_rows), lambda i: (0, i)),
            pl.BlockSpec((tall, ff), lambda i: (i, 0)),
        ],
        out_specs=(
            pl.BlockSpec((group, up_rows + down_rows, width), lambda i: (i, 0, 0)),
            pl.BlockSpec((tall, width), lambda i: (jnp.minimum(i, near - 1), 0)),
            pl.BlockSpec((tall, width), lambda i: (jnp.maximum(i - near, 0), 0)),
        ),
        scratch_shapes=[
            pltpu.VMEM((total, width), BF),
            pltpu.VMEM((total, width), BF),
            pltpu.VMEM((total, ff), BF),
            pltpu.VMEM((parts, down_rows, width), BF),
            pltpu.SemaphoreType.DMA((count + 2,)),
        ],
        cost_estimate=pl.CostEstimate(
            flops=6 * total * width * ff,
            bytes_accessed=2 * (2 * total * (width + ff) + 2 * width * ff),
            transcendentals=0,
        ),
        name="feed_forward_weights",
    )(*sources, grad_hidden, weights, active, active)


def own_time_features(times, first_col, col_count, model_width):
    half_width = model_width // 2
    cols = first_col + jnp.arange(col_count, dtype=jnp.int32)
    is_sine = cols < half_width
    steps_row = jnp.where(is_sine, cols, cols - half_width).astype(F32)
    frequency = jnp.exp(steps_row * (-math.log(10000.0) / (half_width - 1)))
    phase_arg = 1000.0 * times[:, None] * frequency[None, :]
    features = jnp.where(is_sine[None, :], jnp.sin(phase_arg), jnp.cos(phase_arg))
    return jax.nn.silu(features).astype(BF)


def pad_rows(vector):
    rows = -(-vector.shape[-1] // LANES)
    return jnp.pad(vector, (0, rows * LANES - vector.shape[-1])).reshape(rows, LANES)


def body(
    frames,
    skip_frames,
    lengths,
    flow_time,
    skip_weight,
    adaln_weight,
    adaln_bias,
    qkv_weight,
    qkv_bias,
    output_weight,
    output_bias,
    up_weight,
    up_bias,
    down_weight,
    down_bias,
    out_grad,
):
    n_u, n_s = lax.axis_size("utt"), lax.axis_size("sp")
    u, s = lax.axis_index("utt"), lax.axis_index("sp")
    n_all = n_u * n_s
    me = u * n_s + s
    rows, width = frames.shape
    per_group = lengths.shape[1]
    ff = up_weight.shape[1]
    part_width = width // n_s
    part_ff = ff // n_s
    lengths_row = lengths[0]

    all_ids = jnp.concatenate(
        [(s ^ d) * rows + jnp.arange(rows, dtype=jnp.int32) for d in block_order(n_s)]
    )
    inside_all, segment_all, position_all = utterance_layout(lengths_row, all_ids)
    inside = inside_all[:rows]

    cols = qkv_weight.shape[0]
    slot, out_slot = skip_weight.shape[0], output_weight.shape[0]
    far = n_s // 2
    bias_sizes = [qkv_bias.shape[0], output_bias.shape[0], up_bias.shape[0], down_bias.shape[0]]
    bias_own = pad_rows(
        jnp.concatenate([qkv_bias, output_bias, up_bias, down_bias]).astype(F32)
    )
    qkv_split = qkv_weight.reshape(cols, 3, n_s, part_width).transpose(2, 0, 1, 3)
    up_split = up_weight.reshape(cols, n_u, n_s, ff // n_all).transpose(2, 0, 1, 3)
    both_split = jnp.concatenate(
        [qkv_split.reshape(n_s, cols, 3 * part_width), up_split.reshape(n_s, cols, part_ff)], axis=2
    )
    skip_blocks = line_blocks(skip_weight)
    flow_row = jnp.pad(flow_time, ((0, 0), (0, LANES - per_group)))
    first_rows = jnp.concatenate([flow_row, bias_own], axis=0)
    both_mine = lax.all_to_all(both_split, "sp", 0, 0, tiled=True)
    first_rows = lax.all_to_all(
        jnp.broadcast_to(after(first_rows, both_mine)[None], (n_u,) + first_rows.shape),
        "utt",
        0,
        0,
        tiled=True,
    )
    part = n_u * slot
    chosen = jnp.arange(2 * width, dtype=jnp.int32)
    chosen = chosen % part // slot * (slot * n_s) + chosen // part * slot + chosen % slot
    selection = (jnp.arange(2 * width, dtype=jnp.int32)[:, None] == chosen[None, :]).astype(BF)
    joined_split = dot32(jnp.concatenate([frames, skip_frames], axis=1), selection).astype(BF)
    joined_split = joined_split.reshape(rows, n_s, part).transpose(1, 0, 2)
    joined_sent = far_entries(joined_split)
    skip_blocks, both_mine, joined_split, joined_sent = fence(
        (skip_blocks, both_mine, joined_split, joined_sent)
    )
    skip_line = jnp.concatenate(skip_blocks, axis=0)
    both_mine = both_mine.reshape(n_s * cols, -1)
    my_qkv = lax.all_gather(both_mine[:, : 3 * part_width], "utt", axis=0, tiled=True)
    ff_lines = lax.all_gather(
        jnp.concatenate([both_mine[:, 3 * part_width :], down_weight], axis=0), "utt", axis=0
    )

    times = first_rows[:, 0, :per_group].reshape(n_u * per_group)
    feature_rows = adaln_weight.shape[0]
    silu_own = own_time_features(times, me * feature_rows, feature_rows, width)
    table_width = adaln_weight.shape[1]
    mod_terms = dot32(silu_own, adaln_weight)
    bias_cols = lax.dynamic_update_slice(
        jnp.zeros((table_width,), F32), adaln_bias.astype(F32), (me * adaln_bias.shape[0],)
    )
    mod_terms = (mod_terms + bias_cols[None, :]).reshape(n_u, per_group, 6, width)
    mod_terms = mod_terms.transpose(0, 2, 1, 3).reshape(n_u, 6 * per_group, width)

    high, half = skip_line.shape[0] // slot, slot // 2
    rows_of = lambda x: x.reshape(high, slot, width)
    over_sp, over_utt = xor_sp(skip_line, far), swap_utt(skip_line)
    near_line = xor_sp(skip_line, 1)
    mod_terms = lax.all_to_all(mod_terms, "utt", 0, 0, tiled=True)
    cosine, sine = rotary_tables(position_all)
    over_sp, over_utt, near_line, cosine, sine = fence(
        (over_sp, over_utt, near_line, cosine, sine)
    )
    top = xor_sp(rows_of(over_utt)[:, :half].reshape(high * half, width), far)
    bottom = swap_utt(rows_of(over_sp)[:, half:].reshape(high * half, width))
    near_sp, near_utt = xor_sp(over_sp, 1), xor_sp(over_utt, 1)
    table_rows = 6 * per_group
    bias_own = first_rows[:, 1:].reshape(-1, width)
    top, bottom, near_sp, near_utt, mod_terms = fence((top, bottom, near_sp, near_utt, mod_terms))
    corner = jnp.concatenate([top, bottom], axis=0)
    message = jnp.concatenate([jnp.sum(mod_terms, axis=0), bias_own], axis=0)
    corner, message, joined_sent = fence((corner, message, joined_sent))
    output_blocks = lax.all_to_all(
        jnp.broadcast_to(after(output_weight, corner)[None], (n_u, out_slot, width)),
        "utt",
        0,
        0,
        tiled=True,
    ).reshape(n_u * out_slot, width)
    near_corner, message_far = fence((xor_sp(corner, 1), xor_sp(message, far)))
    joined_far = xor_sp(joined_sent, far)
    message = jnp.concatenate(
        [message[:table_rows] + message_far[:table_rows], bias_own, message_far[table_rows:]], axis=0
    )
    message_near = xor_sp(message, 1)
    mod_table = message[:table_rows] + message_near[:table_rows]
    bias_blocks = [
        m.reshape(2, n_u, -1)[i]
        for m in (message[table_rows:], message_near[table_rows:])
        for i in range(2)
    ]
    here, there = line_indices(False), line_indices(True)
    skip_pieces = Pieces()
    whole_row = lambda i, distance: (i * n_s + (s ^ distance)) * slot
    for array, owners, distance in (
        (skip_line, here, 0),
        (over_sp, here, far),
        (over_utt, there, 0),
        (near_line, here, 1),
        (near_sp, here, far ^ 1),
        (near_utt, there, 1),
    ):
        skip_pieces.add(array, [whole_row(i, distance) for i in owners], slot)
    for array, distance in ((corner, far), (near_corner, far ^ 1)):
        skip_pieces.add(
            array,
            [whole_row(i, distance) for i in there]
            + [whole_row(i, distance) + half for i in there],
            half,
        )

    def segment_sums(values):
        return jnp.stack(
            [jnp.sum(jnp.where(inside[:, k][:, None], values, 0.0), axis=0) for k in range(per_group)]
        )

    full_skip, base_rows = placed_product([frames, skip_frames], skip_pieces, 2 * width)
    base_rows, mod_table, joined_far = fence((base_rows, mod_table, joined_far))

    def expand(block, segment):
        table = mod_table[block * per_group : (block + 1) * per_group]
        result = table[per_group - 1][None, :]
        for k in range(per_group - 2, -1, -1):
            result = jnp.where(segment[:, None] == k, table[k][None, :], result)
        return result

    segment_own = segment_all[:rows]
    scale_attn, gate_attn, shift_ffn, scale_ffn, gate_ffn = [
        expand(i, segment_own) for i in range(1, 6)
    ]
    grad_out = out_grad.astype(F32)
    grad_result = (gate_ffn * grad_out).astype(BF)
    base_norm, base_scale = norm_parts(base_rows)
    normed = (base_norm * (1.0 + scale_attn) + expand(0, segment_own)).astype(BF)
    far_normed = xor_sp(normed, far)
    far_normed, output_blocks, my_qkv, grad_result = fence(
        (far_normed, output_blocks, my_qkv, grad_result)
    )
    grad_result_far = xor_sp(grad_result, far)
    two_normed = jnp.concatenate([normed, far_normed], axis=0)
    near_normed = xor_sp(two_normed, 1)
    joined_mine = exchange_near(joined_split, joined_far)
    near_normed, joined_mine = fence((near_normed, joined_mine))
    output_far = xor_sp(output_blocks, far)
    bias_all = jnp.stack(in_device_order(bias_blocks), axis=1).reshape(n_u, n_s, -1)
    offsets = [0]
    for size in bias_sizes:
        offsets.append(offsets[-1] + size)
    full_qkv_bias, full_output_bias, full_up_bias, full_down_bias = [
        bias_all[:, :, offsets[i] : offsets[i + 1]].reshape(-1) for i in range(4)
    ]
    my_qkv_bias = lax.dynamic_slice_in_dim(
        full_qkv_bias.reshape(3, width), s * part_width, part_width, 1
    ).reshape(-1)
    my_up_bias = lax.dynamic_index_in_dim(
        full_up_bias.reshape(n_u, n_s, -1), s, 1, keepdims=False
    ).reshape(-1)

    normed_all, query_rows, key_rows, value_rows, attended_heads, log_totals = attend(
        [two_normed, near_normed], my_qkv, my_qkv_bias, cosine, sine, segment_all
    )
    attended_heads, output_far, grad_result_far = fence(
        (attended_heads, output_far, grad_result_far)
    )
    arrived = exchange_sp([attended_heads[i * rows : (i + 1) * rows] for i in range(n_s)])
    output_near = xor_sp(jnp.concatenate([output_blocks, output_far], axis=0), 1)
    grad_result_near = xor_sp(jnp.concatenate([grad_result, grad_result_far], axis=0), 1)
    arrived, output_near, grad_result_near = fence((arrived, output_near, grad_result_near))
    output_pieces = whole_pieces(
        [
            (output_blocks, 0, range(n_u), 0, out_slot),
            (output_far, far, range(n_u), 0, out_slot),
        ],
        out_slot,
    )
    output_pieces.add(
        output_near,
        [(i * n_s + (s ^ 1)) * out_slot for i in range(n_u)]
        + [(i * n_s + (s ^ 1 ^ far)) * out_slot for i in range(n_u)],
        out_slot,
    )
    attended = jnp.concatenate(in_device_order(arrived), axis=1)
    full_output, branch = placed_product([attended], output_pieces, width)
    branch = branch + full_output_bias[None, :]
    middle = base_rows + gate_attn * branch
    middle_norm, middle_scale = norm_parts(middle)
    normed_ffn = (middle_norm * (1.0 + scale_ffn) + shift_ffn).astype(BF)

    half_rows = n_s * rows // 2
    far_ffn = xor_sp(normed_ffn, far)
    two_ffn = jnp.concatenate([normed_ffn, far_ffn], axis=0)
    near_ffn = xor_sp(two_ffn, 1)
    ffn_blocks = [two_ffn, near_ffn]
    grad_result_blocks = [grad_result, grad_result_far, grad_result_near]
    active, grad_hidden, grad_up_bias, kept, sent = feed_forward(
        ffn_blocks, grad_result_blocks, ff_lines, my_up_bias, n_s * cols
    )
    arrived = xor_sp(sent, 1)
    far_sent = (kept[rows:] + arrived[rows:].astype(F32)).astype(BF)
    far_sent, active, grad_hidden = fence((far_sent, active, grad_hidden))
    far_sum = xor_sp(far_sent, n_s // 2)

    ff_grads, result_kept, sent = feed_forward_weights(
        ffn_blocks, grad_hidden, active, grad_result_blocks, ff_lines, n_s * cols
    )
    far_sum, result_kept, sent, ff_grads = fence((far_sum, result_kept, sent, ff_grads))
    grad_normed_ffn = kept[:rows] + arrived[:rows].astype(F32) + far_sum.astype(F32)
    ff_mine = lax.psum_scatter(ff_grads, "utt", scatter_dimension=0, tiled=True)[0]
    grad_middle = grad_out + norm_back(
        middle_norm, middle_scale, grad_normed_ffn * (1.0 + scale_ffn)
    )
    grad_branch = (gate_attn * grad_middle).astype(BF)
    grad_attended = dot_nt(grad_branch, full_output).astype(BF)
    grad_heads = exchange_sp(
        [
            lax.dynamic_slice_in_dim(grad_attended, (s ^ d) * part_width, part_width, 1)
            for d in block_order(n_s)
        ]
    )
    result_arrived = xor_sp(after(sent, grad_attended), 1)
    grad_heads, result_arrived, grad_branch = fence((grad_heads, result_arrived, grad_branch))
    far_branch = xor_sp(grad_branch, far)
    result_sent = (result_kept[rows:] + result_arrived[rows:].astype(F32)).astype(BF)

    grad_projected = attend_back(
        query_rows, key_rows, value_rows, grad_heads, log_totals, cosine, sine, segment_all
    )
    grad_projected, far_branch = fence((grad_projected, far_branch))
    sent = product(grad_projected[half_rows:], my_qkv, 1, 1).astype(BF)
    kept = product(grad_projected[:half_rows], my_qkv, 1, 1)
    arrived = xor_sp(sent, 1)
    far_sent = (kept[rows:] + arrived[rows:].astype(F32)).astype(BF)
    far_sent, projected_late, far_branch, middle_late, nffn_late = fence(
        (far_sent, grad_projected, far_branch, grad_middle, grad_normed_ffn)
    )
    far_sum = xor_sp(far_sent, far)

    grad_qkv = dot_tn(normed_all, projected_late).astype(BF)
    my_qkv_bias_grad = jnp.sum(projected_late.astype(F32), axis=0)
    qkv_keep, qkv_send = split_pair(grad_qkv.reshape(-1, 2, n_s * cols, 3 * part_width), 1)
    qkv_arrived = swap_utt(qkv_send)
    branch_blocks, step = [grad_branch, far_branch], n_s // 4
    while step >= 1:
        branch_blocks = branch_blocks + [xor_sp(b, step) for b in branch_blocks]
        step //= 2
    grad_output = dot_tn(attended_heads, jnp.concatenate(branch_blocks, axis=0)).astype(BF)
    grad_output_bias = jnp.sum((gate_attn * middle_late).astype(BF).astype(F32), axis=0)
    early_tables = [
        segment_sums(v) for v in (middle_late * branch, nffn_late, nffn_late * middle_norm)
    ]
    far_sum, early_tables, qkv_keep, qkv_arrived, grad_output = fence(
        (far_sum, early_tables, qkv_keep, qkv_arrived, grad_output)
    )
    grad_normed = kept[:rows] + arrived[:rows].astype(F32) + far_sum.astype(F32)

    grad_base = (
        grad_middle + norm_back(base_norm, base_scale, grad_normed * (1.0 + scale_attn))
    ).astype(BF)
    far_base = xor_sp(grad_base, far)
    out_keep, out_send = split_pair(grad_output.reshape(-1, 2, out_slot, width), 1)
    out_arrived = swap_utt(out_send)
    far_base, normed_late, out_arrived = fence((far_base, grad_normed, out_arrived))
    out_half = (out_keep.astype(F32) + out_arrived.astype(F32)).astype(BF)
    two_base = jnp.concatenate([grad_base, far_base], axis=0)
    near_base = xor_sp(two_base, 1)
    grad_skip = dot_tn(
        jnp.concatenate(joined_mine, axis=0), jnp.concatenate([two_base, near_base], axis=0)
    ).astype(BF)
    skip_keep, skip_send = split_pair(grad_skip.reshape((-1, 2) + (slot, width)), 1)
    skip_send, out_half, base_late, normed_late, result_sent, late_grad = fence(
        (skip_send, out_half, grad_base, normed_late, result_sent, out_grad)
    )

    skip_arrived, far_result = swap_utt(skip_send), xor_sp(result_sent, far)
    frames_grad = dot_nt(base_late, full_skip[:width])
    skip_grad = dot_nt(base_late, full_skip[width:])
    late_tables = [segment_sums(v) for v in (normed_late, normed_late * base_norm)]
    skip_arrived, far_result, late_tables, frames_grad, skip_grad, qkv_keep, ff_mine = fence(
        (skip_arrived, far_result, late_tables, frames_grad, skip_grad, qkv_keep, ff_mine)
    )
    qkv_half = (qkv_keep.astype(F32) + qkv_arrived.astype(F32)).astype(BF)
    grad_out = late_grad.astype(F32)
    result = (
        result_kept[:rows]
        + result_arrived[:rows].astype(F32)
        + far_result.astype(F32)
        + full_down_bias[None, :]
    )
    skip_half = (skip_keep.astype(F32) + skip_arrived.astype(F32)).astype(BF)
    skip_half, qkv_half = fence((skip_half, qkv_half))

    skip_terms, qkv_terms = scatter_slow(skip_half), scatter_slow(qkv_half)
    mixed_out = (middle + gate_ffn * result).astype(BF)
    grad_down_bias = jnp.sum((gate_ffn * grad_out).astype(BF).astype(F32), axis=0)
    gate_table = segment_sums(grad_out * result)
    skip_sum = add_terms(skip_terms)
    qkv_mine = add_terms(qkv_terms).astype(BF)
    qkv_mine = qkv_mine.reshape(n_s, cols, 3 * part_width)
    out_sum = to_owner(add_terms(scatter_slow(out_half)))
    qkv_back = split_exchange_sp(qkv_mine)
    qkv_sum = (
        qkv_back.reshape(n_s, cols, 3, part_width).transpose(1, 2, 0, 3).reshape(cols, 3 * width)
    ).astype(F32)
    up_back = split_exchange_sp(ff_mine[: n_s * cols].reshape(n_s, cols, part_ff))
    up_sum = (
        up_back.reshape(n_s, cols, n_u, ff // n_all).transpose(1, 2, 0, 3).reshape(cols, ff)
    ).astype(F32)
    down_sum = ff_mine[n_s * cols :].astype(F32)

    grad_table = jnp.concatenate(late_tables + early_tables + [gate_table], axis=1)
    qkv_bias_slots = lax.dynamic_update_slice(
        jnp.zeros((3, width), F32), my_qkv_bias_grad.reshape(3, part_width), (0, s * part_width)
    ).reshape(-1)
    up_bias_slots = lax.dynamic_update_slice(
        jnp.zeros((n_u, n_s, ff // n_all), F32),
        grad_up_bias.reshape(n_u, 1, ff // n_all),
        (0, s, 0),
    ).reshape(-1)
    bias_vec = jnp.concatenate(
        [
            v.reshape(n_u, -1)
            for v in (qkv_bias_slots, grad_output_bias, up_bias_slots, grad_down_bias)
        ],
        axis=1,
    )
    vec_rows = -(-bias_vec.shape[1] // LANES)
    bias_vec = jnp.pad(bias_vec, ((0, 0), (0, vec_rows * LANES - bias_vec.shape[1])))
    table_rows = per_group * table_width // LANES
    tail = jnp.concatenate(
        [grad_table.reshape(table_rows, LANES), bias_vec.reshape(n_u * vec_rows, LANES)], axis=0
    )
    tail = sum_sp(tail)
    tail = jnp.concatenate(
        [
            jnp.broadcast_to(tail[None, :table_rows], (n_u, table_rows, LANES)),
            tail[table_rows:].reshape(n_u, vec_rows, LANES),
        ],
        axis=1,
    )
    tail = tail.astype(BF)
    tail = lax.all_to_all(tail, "utt", 0, 0, tiled=True).astype(F32)
    table_all = tail[:, :table_rows].reshape(n_u * per_group, table_width)
    adaln_sum = lax.dot_general(
        silu_own.astype(F32),
        table_all,
        (((0,), (0,)), ((), ())),
        precision=highest_precision,
        preferred_element_type=F32,
    )
    adaln_bias_sum = jnp.sum(owned(table_all), axis=0)
    vec = jnp.sum(tail[:, table_rows:], axis=0).reshape(-1)
    bias_sums, start = [], 0
    for size in bias_sizes:
        bias_sums.append(lax.dynamic_slice_in_dim(vec, start + s * size, size, 0))
        start += size * n_s

    return (
        mixed_out,
        frames_grad,
        skip_grad,
        skip_sum,
        adaln_sum,
        adaln_bias_sum,
        qkv_sum,
        bias_sums[0],
        out_sum,
        bias_sums[1],
        up_sum,
        bias_sums[2],
        down_sum,
        bias_sums[3],
    )


def solution(mesh):
    both = ("utt", "sp")
    matrix, vector, group = P(both, None), P(both), P("utt", None)
    return jax.shard_map(
        body,
        mesh=mesh,
        in_specs=(
            matrix,
            matrix,
            group,
            group,
            matrix,
            matrix,
            vector,
            matrix,
            vector,
            matrix,
            vector,
            matrix,
            vector,
            matrix,
            vector,
            matrix,
        ),
        out_specs=(
            matrix,
            matrix,
            matrix,
            matrix,
            matrix,
            vector,
            matrix,
            vector,
            matrix,
            vector,
            matrix,
            vector,
            matrix,
            vector,
        ),
        check_vma=False,
    )
```

```python
import math

import jax
import jax.numpy as jnp
from jax import lax
from jax.experimental import pallas as pl
from jax.experimental.pallas import tpu as pltpu
from jax.sharding import PartitionSpec as P

HD = 64
LANES = 128
BIAS_ROWS = 16
BF = jnp.bfloat16
F32 = jnp.float32
highest_precision = lax.Precision.HIGHEST
mask_value = -1e30


def product(left, right, left_dim, right_dim):
    return lax.dot_general(
        left, right, (((left_dim,), (right_dim,)), ((), ())), preferred_element_type=F32
    )


def dot32(left, right):
    return jnp.dot(left, right, preferred_element_type=F32)


def dot_nt(left, right):
    return lax.dot_general(left, right, (((1,), (1,)), ((), ())), preferred_element_type=F32)


def dot_tn(left, right):
    return lax.dot_general(left, right, (((0,), (0,)), ((), ())), preferred_element_type=F32)


fence = lax.optimization_barrier


def after(value, *others):
    return fence((value, others))[0]


def block_order(count):
    order, step = [0], count // 2
    while step >= 1:
        order = order + [d ^ step for d in order]
        step //= 2
    return order


def xor_sp(values, distance):
    size = lax.axis_size("sp")
    return lax.ppermute(values, "sp", [(i, i ^ distance) for i in range(size)])


def swap_utt(values):
    return lax.ppermute(values, "utt", [(i, i ^ 1) for i in range(lax.axis_size("utt"))])


def gather_sp(own):
    blocks, step = [own], lax.axis_size("sp") // 2
    while step >= 1:
        blocks = blocks + [xor_sp(b, step) for b in blocks]
        step //= 2
    return blocks


def exchange_sp(parts):
    order = block_order(len(parts))
    return [parts[0]] + [xor_sp(parts[i], order[i]) for i in range(1, len(parts))]


def in_device_order(blocks):
    order = block_order(len(blocks))
    stacked = jnp.stack([blocks[order.index(d)] for d in range(len(blocks))])
    me = lax.axis_index("sp")
    return [
        lax.dynamic_index_in_dim(stacked, me ^ a, 0, keepdims=False) for a in range(len(blocks))
    ]


def sum_sp(values):
    step = lax.axis_size("sp") // 2
    while step >= 1:
        values = values + xor_sp(values, step)
        step //= 2
    return values


def turn_utt(values, k):
    size = lax.axis_size("utt")
    high = size // 2
    routes = [(z * 2 + y, (z + k) % high * 2 + y) for z in range(high) for y in range(2)]
    return lax.ppermute(values, "utt", routes)


def line_blocks(own):
    return [own] + [turn_utt(own, k) for k in range(1, lax.axis_size("utt") // 2)]


def gather_line(own):
    return jnp.concatenate(line_blocks(own), axis=0)


def split_pair(parts, axis):
    low = lax.axis_index("utt") % 2
    keep = lax.dynamic_index_in_dim(parts, low, axis, keepdims=False)
    return keep, lax.dynamic_index_in_dim(parts, 1 - low, axis, keepdims=False)


def scatter_fast(parts):
    keep, send = split_pair(parts.reshape((-1, 2) + parts.shape[1:]), 1)
    return (keep.astype(F32) + swap_utt(send.astype(BF)).astype(F32)).astype(BF)


def scatter_slow(half):
    high = lax.axis_size("utt") // 2
    z = lax.axis_index("utt") // 2
    terms = [lax.dynamic_index_in_dim(half, z, 0, keepdims=False)]
    for k in range(1, high):
        piece = lax.dynamic_index_in_dim(half, (z + k) % high, 0, keepdims=False)
        terms.append(turn_utt(piece, k))
    return terms


def add_terms(terms):
    total = terms[0].astype(F32)
    for term in terms[1:]:
        total = total + term.astype(F32)
    return total


def entry(values, index):
    return lax.dynamic_index_in_dim(values, index, 0, keepdims=False)


def far_entries(values):
    me, far = lax.axis_index("sp"), lax.axis_size("sp") // 2
    return jnp.stack([entry(values, me ^ far), entry(values, me ^ far ^ 1)])


def exchange_far(values):
    return xor_sp(far_entries(values), lax.axis_size("sp") // 2)


def exchange_near(values, arrived):
    me = lax.axis_index("sp")
    last = xor_sp(jnp.stack([entry(values, me ^ 1), arrived[1]]), 1)
    return [entry(values, me), arrived[0], last[0], last[1]]


def split_exchange_sp(values):
    return jnp.stack(in_device_order(exchange_near(values, exchange_far(values))))


class Pieces:
    def __init__(self):
        self.arrays, self.starts, self.sizes = [], [], []

    def add(self, array, first_rows, size):
        self.arrays.append(array)
        self.starts.append(first_rows)
        self.sizes.append(size)

    def offsets(self):
        return jnp.stack([start for starts in self.starts for start in starts]).astype(jnp.int32)

    def count(self):
        return sum(len(starts) for starts in self.starts)

    def copies(self, offset_ref, refs, whole_ref, sems):
        made, n = [], 0
        for ref, starts, size in zip(refs, self.starts, self.sizes):
            for i in range(len(starts)):
                first = pl.multiple_of(offset_ref[n], size)
                made.append(
                    pltpu.make_async_copy(
                        ref.at[pl.ds(i * size, size)], whole_ref.at[pl.ds(first, size)], sems.at[n]
                    )
                )
                n += 1
        return made


def line_indices(flip):
    size = lax.axis_size("utt")
    high = size // 2
    u = lax.axis_index("utt")
    z, y = u // 2, u % 2
    return [(z - k + high) % high * 2 + (1 - y if flip else y) for k in range(high)]


def whole_pieces(arrays, rows):
    n_s, me = lax.axis_size("sp"), lax.axis_index("sp")
    pieces = Pieces()
    for array, d, owners, shift, size in arrays:
        pieces.add(array, [(i * n_s + (me ^ d)) * rows + shift for i in owners], size)
    return pieces


def to_owner(values):
    n_u, n_s = lax.axis_size("utt"), lax.axis_size("sp")
    routes = []
    for p in range(n_u):
        for s in range(n_s):
            routes.append((p * n_s + s, s * n_u + p))
    return lax.ppermute(values, ("utt", "sp"), routes)


def owned(values):
    n = lax.axis_size("utt") * lax.axis_size("sp")
    j = lax.axis_index("utt") * lax.axis_size("sp") + lax.axis_index("sp")
    size = values.shape[-1] // n
    return lax.dynamic_slice_in_dim(values, j * size, size, values.ndim - 1)


def norm_parts(values):
    mean_row = jnp.mean(values, axis=-1, keepdims=True)
    centered = values - mean_row
    variance = jnp.mean(centered * centered, axis=-1, keepdims=True)
    scale = lax.rsqrt(variance + 1e-06)
    return centered * scale, scale


def norm_back(normal, scale, grads):
    mean_grad = jnp.mean(grads, axis=-1, keepdims=True)
    mean_both = jnp.mean(grads * normal, axis=-1, keepdims=True)
    return (grads - mean_grad - normal * mean_both) * scale


def rotary_tables(position):
    half_head = HD // 2
    inverse = jnp.exp(jnp.arange(half_head, dtype=F32) * (-2.0 * math.log(10000.0) / HD))
    angle_arg = position.astype(F32)[:, None] * inverse[None, :]
    cosine, sine = jnp.cos(angle_arg), jnp.sin(angle_arg)
    return (
        jnp.concatenate([cosine] * 4, axis=1),
        jnp.concatenate([-sine, sine, -sine, sine], axis=1),
    )


def utterance_layout(lengths_row, frame_ids):
    ends_at = jnp.cumsum(lengths_row)
    starts_at = ends_at - lengths_row
    inside = (frame_ids[:, None] >= starts_at[None, :]) & (frame_ids[:, None] < ends_at[None, :])
    segment = jnp.sum(jnp.where(frame_ids[:, None] >= ends_at[None, :], 1, 0), axis=1).astype(
        jnp.int32
    )
    position = frame_ids - jnp.sum(jnp.where(inside, starts_at[None, :], 0), axis=1)
    return inside, segment, position


QUERY_ROWS = 512


def any_refs(count):
    return [pl.BlockSpec(memory_space=pltpu.HBM)] * count


def smem_ref():
    return pl.BlockSpec(memory_space=pltpu.SMEM)


def vmem_ref():
    return pl.BlockSpec(memory_space=pltpu.VMEM)


def placed_product(lefts, pieces, depth):
    n, count = len(pieces.arrays), pieces.count()
    rows = lefts[0].shape[0]
    width = pieces.arrays[0].shape[1]

    def kernel(offset_ref, *refs):
        piece_refs, left_refs = refs[:n], refs[n : n + len(lefts)]
        whole_ref, base_ref, sems = refs[n + len(lefts) :]
        copies = pieces.copies(offset_ref, piece_refs, whole_ref, sems)
        for copy in copies:
            copy.start()
        for copy in copies:
            copy.wait()
        total, first = None, 0
        for left_ref in left_refs:
            last = first + left_ref.shape[1]
            term = product(left_ref[...], whole_ref[first:last, :], 1, 0)
            total = term if total is None else total + term
            first = last
        base_ref[...] = total

    return pl.pallas_call(
        kernel,
        out_shape=(
            jax.ShapeDtypeStruct((depth, width), BF),
            jax.ShapeDtypeStruct((rows, width), F32),
        ),
        in_specs=[smem_ref()] + any_refs(n) + [vmem_ref()] * len(lefts),
        out_specs=(vmem_ref(),) * 2,
        scratch_shapes=[pltpu.SemaphoreType.DMA((count,))],

        cost_estimate=pl.CostEstimate(
            flops=2 * rows * depth * width,
            bytes_accessed=4 * depth * width + 2 * rows * (depth + 2 * width),
            transcendentals=0,
        ),
        name="placed_product",
    )(pieces.offsets(), *pieces.arrays, *lefts)


def turn_halves(values, cosine, sine):
    half, cols = HD // 2, values.shape[1]
    first = lax.broadcasted_iota(jnp.int32, values.shape, 1) % HD < half
    swapped = jnp.where(
        first, pltpu.roll(values, cols - half, 1), pltpu.roll(values, half, 1)
    )
    repeats = cols // cosine.shape[1]
    wide = lambda t: jnp.concatenate([t] * repeats, axis=1) if repeats > 1 else t
    return values * wide(cosine) + swapped * wide(sine)


def attend(normed_blocks, weight, bias, cosine, sine, segment):
    blocks, width = len(normed_blocks), normed_blocks[0].shape[1]
    rows = normed_blocks[0].shape[0]
    total = blocks * rows
    cols = weight.shape[1] // 3
    heads = cols // HD
    block = min(QUERY_ROWS, total)

    def kernel(*refs):
        block_refs = refs[:blocks]
        (
            weight_ref,
            cos_from,
            sin_from,
            b_ref,
            segc_ref,
            segr_ref,
            x_out,
            q_out,
            k_out,
            v_out,
            o_ref,
            lse_ref,
            x_ref,
            q_ref,
            k_ref,
            v_ref,
            vt_ref,
            bias_ref,
            w_ref,
            cos_ref,
            sin_ref,
            sems,
        ) = refs[blocks:]
        sources = [weight_ref, cos_from, sin_from, *block_refs]
        targets = [w_ref, cos_ref, sin_ref] + [
            x_ref.at[pl.ds(i * rows, rows)] for i in range(blocks)
        ]
        copies = [
            pltpu.make_async_copy(sources[i], targets[i], sems.at[i]) for i in range(3 + blocks)
        ]
        for copy in copies:
            copy.start()

        for copy in copies:
            copy.wait()

        def project(i, carried):
            at = pl.ds(pl.multiple_of(i * block, block), block)
            three = product(x_ref[at, :], w_ref[...], 1, 0) + b_ref[...]
            cosine, sine = cos_ref[at, :], sin_ref[at, :]
            q_ref[at, :] = turn_halves(three[:, :cols], cosine, sine).astype(BF)
            k_ref[at, :] = turn_halves(three[:, cols : 2 * cols], cosine, sine).astype(BF)
            v_ref[at, :] = three[:, 2 * cols :].astype(BF)
            return carried

        lax.fori_loop(0, total // block, project, 0)
        moved = ((x_ref, x_out), (q_ref, q_out), (k_ref, k_out), (v_ref, v_out))
        outs_going = [
            pltpu.make_async_copy(moved[i][0], moved[i][1], sems.at[3 + blocks + i])
            for i in range(4)
        ]
        for copy in outs_going:
            copy.start()
        vt_ref[...] = v_ref[...].T

        def one(i, carried):
            row = pl.multiple_of(i * block, block)
            same = segc_ref[...] == segr_ref[:, pl.ds(row, block)]
            bias_ref[...] = jnp.where(same, 0.0, mask_value)
            outs = []
            for h in range(heads):
                c = slice(h * HD, (h + 1) * HD)
                scores = product(k_ref[:, c], q_ref[pl.ds(row, block), c], 1, 1)
                scores = scores * (HD**-0.5) + bias_ref[...]
                top = jnp.max(scores, axis=0, keepdims=True)
                exps = jnp.exp(scores - top)
                totals = jnp.sum(exps, axis=0, keepdims=True)
                outs.append(product(vt_ref[c, :], exps.astype(BF), 1, 0) * (1.0 / totals))
                lse_ref[h : h + 1, pl.ds(row, block)] = top + jnp.log(totals)
            o_ref[pl.ds(row, block), :] = jnp.concatenate(outs, axis=0).T.astype(BF)
            return carried

        lax.fori_loop(0, total // block, one, 0)
        for copy in outs_going:
            copy.wait()

    return pl.pallas_call(
        kernel,
        out_shape=(
            jax.ShapeDtypeStruct((total, width), BF),
            jax.ShapeDtypeStruct((total, cols), BF),
            jax.ShapeDtypeStruct((total, cols), BF),
            jax.ShapeDtypeStruct((total, cols), BF),
            jax.ShapeDtypeStruct((total, cols), BF),
            jax.ShapeDtypeStruct((heads, total), F32),
        ),
        in_specs=any_refs(blocks + 3) + [vmem_ref()] * 3,
        out_specs=(*any_refs(4), vmem_ref(), vmem_ref()),
        scratch_shapes=[
            pltpu.VMEM((total, width), BF),
            pltpu.VMEM((total, cols), BF),
            pltpu.VMEM((total, cols), BF),
            pltpu.VMEM((total, cols), BF),
            pltpu.VMEM((cols, total), BF),
            pltpu.VMEM((total, block), F32),
            pltpu.VMEM(weight.shape, BF),
            pltpu.VMEM(cosine.shape, F32),
            pltpu.VMEM(cosine.shape, F32),
            pltpu.SemaphoreType.DMA((blocks + 7,)),
        ],

        cost_estimate=pl.CostEstimate(
            flops=4 * total * total * cols + 6 * total * width * cols,
            bytes_accessed=8 * total * cols + 2 * total * width + 6 * width * cols,
            transcendentals=heads * total * total,
        ),
        name="attend_forward",
    )(
        *normed_blocks,
        weight,
        cosine,
        sine,
        bias[None, :],
        segment[:, None],
        segment[None, :],
    )


def attend_back(queries, keys, values, grad_blocks, log_totals, cosine, sine, segment):
    total, cols = queries.shape
    heads = cols // HD
    block = min(QUERY_ROWS, total)
    blocks, rows = len(grad_blocks), grad_blocks[0].shape[0]

    def kernel(*refs):
        big_refs, block_refs = refs[:5], refs[5 : 5 + blocks]
        (
            lse_ref,
            segc_ref,
            segr_ref,
            d_ref,
            q_ref,
            k_ref,
            v_ref,
            cos_ref,
            sin_ref,
            g_ref,
            kt_ref,
            bias_ref,
            dk_sum,
            dv_sum,
            sems,
        ) = refs[5 + blocks :]
        held = (q_ref, k_ref, v_ref, cos_ref, sin_ref)
        copies = [pltpu.make_async_copy(big_refs[i], held[i], sems.at[i]) for i in range(5)] + [
            pltpu.make_async_copy(block_refs[i], g_ref.at[pl.ds(i * rows, rows)], sems.at[5 + i])
            for i in range(blocks)
        ]
        early = copies[:3] + copies[5:]
        for copy in early + copies[3:5]:
            copy.start()
        dk_sum[...] = jnp.zeros_like(dk_sum)
        dv_sum[...] = jnp.zeros_like(dv_sum)
        for copy in early:
            copy.wait()
        kt_ref[...] = k_ref[...].T
        for copy in copies[3:5]:
            copy.wait()

        def one(i, carried):
            row = pl.multiple_of(i * block, block)
            at = pl.ds(row, block)
            same = segc_ref[...] == segr_ref[:, at]
            bias_ref[...] = jnp.where(same, 0.0, mask_value)
            outs = []
            for h in range(heads):
                c = slice(h * HD, (h + 1) * HD)
                query, grad = q_ref[at, c], g_ref[at, c]
                scores = product(k_ref[:, c], query, 1, 1) * (HD**-0.5) + bias_ref[...]
                probs = jnp.exp(scores - lse_ref[h : h + 1, at])
                both = probs * product(v_ref[:, c], grad, 1, 1)
                inner = jnp.sum(both, axis=0, keepdims=True)
                grad_scores = (both - probs * inner).astype(BF)
                dv_sum[:, c] += product(probs.astype(BF), grad, 1, 0)
                dk_sum[:, c] += product(grad_scores, query, 1, 0)
                outs.append(product(kt_ref[c, :], grad_scores, 1, 0))
            grad_query = (jnp.concatenate(outs, axis=0) * (HD**-0.5)).T.astype(BF).astype(F32)
            d_ref[at, :cols] = turn_halves(grad_query, cos_ref[at, :], -sin_ref[at, :]).astype(BF)
            return carried

        lax.fori_loop(0, total // block, one, 0)
        grad_key = (dk_sum[...] * (HD**-0.5)).astype(BF).astype(F32)
        d_ref[:, cols : 2 * cols] = turn_halves(grad_key, cos_ref[...], -sin_ref[...]).astype(BF)
        d_ref[:, 2 * cols :] = dv_sum[...].astype(BF)

    return pl.pallas_call(
        kernel,
        out_shape=jax.ShapeDtypeStruct((total, 3 * cols), BF),
        in_specs=any_refs(5 + blocks) + [vmem_ref()] * 3,
        out_specs=vmem_ref(),
        scratch_shapes=[pltpu.VMEM((total, cols), BF)] * 3
        + [pltpu.VMEM(cosine.shape, F32)] * 2
        + [
            pltpu.VMEM((total, cols), BF),
            pltpu.VMEM((cols, total), BF),
            pltpu.VMEM((total, block), F32),
            pltpu.VMEM((total, cols), F32),
            pltpu.VMEM((total, cols), F32),
            pltpu.SemaphoreType.DMA((5 + blocks,)),
        ],

        cost_estimate=pl.CostEstimate(
            flops=10 * total * total * cols,
            bytes_accessed=14 * total * cols,
            transcendentals=heads * total * total,
        ),
        name="attend_backward",
    )(
        queries,
        keys,
        values,
        cosine,
        sine,
        *grad_blocks,
        log_totals,
        segment[:, None],
        segment[None, :],
    )


def gelu_both(values):
    root = math.sqrt(2.0 / math.pi)
    square = values * values
    tanh = jnp.tanh(root * (values + 0.044715 * (values * square)))
    half = 0.5 * (1.0 + tanh)
    slope = root * (1.0 + 3 * 0.044715 * square)
    return values * half, half + 0.5 * values * (1.0 - tanh * tanh) * slope


def feed_forward(normed_blocks, grad_blocks, weights, up_bias, up_rows):
    sources = list(normed_blocks) + list(grad_blocks)
    count, width = len(sources), normed_blocks[0].shape[1]
    total = sum(block.shape[0] for block in normed_blocks)
    parts, both_rows, ff = weights.shape
    down_rows = both_rows - up_rows
    group = max(1, 256 // down_rows)
    block, half = group * down_rows, total // 2
    steps = ff // block

    def kernel(*refs):
        (
            weight_from,
            b_ref,
            act_ref,
            gh_ref,
            sum_ref,
            keep_ref,
            send_ref,
            x_ref,
            g_ref,
            acc_ref,
            w_ref,
            hidden_ref,
            active_ref,
            old_hidden_ref,
            old_active_ref,
            sems,
        ) = refs[count:]
        step = pl.program_id(0)
        copies, first = [], 0
        for i, ref in enumerate(refs[:count]):
            whole = x_ref if i < len(normed_blocks) else g_ref
            at = pl.ds(first % total, ref.shape[0])
            copies.append(pltpu.make_async_copy(ref, whole.at[at], sems.at[i]))
            first += ref.shape[0]
        copies.append(pltpu.make_async_copy(weight_from, w_ref, sems.at[count]))

        def up_of(i):
            at = pl.ds(pl.multiple_of(i * block, block), block)
            return w_ref[:, :up_rows, at].reshape(width, block)

        def products():
            hidden_ref[...] = product(x_ref[...], up_of(step), 1, 0) + b_ref[step]
            down = w_ref[pl.ds(step * group, group), up_rows:, :].reshape(block, width)
            active_ref[...] = product(g_ref[...], down, 1, 1)

        def shift():
            old_hidden_ref[...] = hidden_ref[...]
            old_active_ref[...] = active_ref[...]

        def rest():
            active, slope = gelu_both(old_hidden_ref[...])
            act_ref[...] = active.astype(BF)
            grad_hidden = (old_active_ref[...] * slope).astype(BF)
            gh_ref[...] = grad_hidden
            sum_ref[...] = jnp.sum(grad_hidden.astype(F32), axis=0, keepdims=True)
            acc_ref[...] += product(grad_hidden, up_of(step - 1), 1, 1)

        @pl.when(step == 0)
        def _():
            for copy in copies:
                copy.start()
            acc_ref[...] = jnp.zeros_like(acc_ref)
            for copy in copies:
                copy.wait()
            products()

        @pl.when((step > 0) & (step < steps))
        def _():
            shift()
            products()
            rest()

        @pl.when(step == steps)
        def _():
            shift()
            rest()

        @pl.when(step == steps)
        def _():
            keep_ref[...] = acc_ref[:half, :]
            send_ref[...] = acc_ref[half:, :].astype(BF)

    fixed = lambda i: (0, 0)
    behind = lambda i: (0, jnp.maximum(i - 1, 0))
    return pl.pallas_call(
        kernel,
        grid=(steps + 1,),
        out_shape=(
            jax.ShapeDtypeStruct((total, ff), BF),
            jax.ShapeDtypeStruct((total, ff), BF),
            jax.ShapeDtypeStruct((1, ff), F32),
            jax.ShapeDtypeStruct((half, width), F32),
            jax.ShapeDtypeStruct((half, width), BF),
        ),
        in_specs=any_refs(count + 1) + [pl.BlockSpec((steps, 1, block), lambda i: (0, 0, 0))],
        out_specs=(
            pl.BlockSpec((total, block), behind),
            pl.BlockSpec((total, block), behind),
            pl.BlockSpec((1, block), behind),
            pl.BlockSpec((half, width), fixed),
            pl.BlockSpec((half, width), fixed),
        ),
        scratch_shapes=[
            pltpu.VMEM((total, width), BF),
            pltpu.VMEM((total, width), BF),
            pltpu.VMEM((total, width), F32),
            pltpu.VMEM(weights.shape, BF),
            pltpu.VMEM((total, block), F32),
            pltpu.VMEM((total, block), F32),
            pltpu.VMEM((total, block), F32),
            pltpu.VMEM((total, block), F32),
            pltpu.SemaphoreType.DMA((count + 1,)),
        ],

        cost_estimate=pl.CostEstimate(
            flops=6 * total * width * ff,
            bytes_accessed=2 * (4 * total * width + 2 * total * ff + 2 * width * ff),
            transcendentals=total * ff,
        ),
        name="feed_forward",
    )(*sources, weights, up_bias.reshape(steps, 1, block))


def feed_forward_weights(normed_blocks, grad_hidden, active, grad_blocks, weights, up_rows):
    sources = list(normed_blocks) + list(grad_blocks)
    count, width = len(sources), normed_blocks[0].shape[1]
    total, ff = active.shape
    parts = weights.shape[0]
    down_rows = ff // parts
    group = max(1, min(parts, 256 // up_rows))
    steps = parts // group
    tall, near = total // steps, steps // 2

    def kernel(*refs):
        (
            gh_from,
            weight_from,
            a_ref,
            r_ref,
            o_ref,
            keep_ref,
            send_ref,
            x_ref,
            g_ref,
            gh_ref,
            down_ref,
            sems,
        ) = refs[count:]
        step = pl.program_id(0)
        copies, first = [], 0
        for i, ref in enumerate(refs[:count]):
            whole = x_ref if i < len(normed_blocks) else g_ref
            at = pl.ds(first % total, ref.shape[0])
            copies.append(pltpu.make_async_copy(ref, whole.at[at], sems.at[i]))
            first += ref.shape[0]
        copies.append(pltpu.make_async_copy(gh_from, gh_ref, sems.at[count]))
        copies.append(
            pltpu.make_async_copy(weight_from.at[:, up_rows:, :], down_ref, sems.at[count + 1])
        )

        left, right = len(normed_blocks), count
        order = copies[:left] + copies[right : right + 1] + copies[left:right] + copies[right + 1 :]

        @pl.when(step == 0)
        def _():
            for copy in order:
                copy.start()
            for copy in order[: left + 1]:
                copy.wait()

        at = pl.ds(pl.multiple_of(step * (group * up_rows), group * up_rows), group * up_rows)
        up = product(x_ref[:, at], gh_ref[...], 0, 0).astype(BF)
        for i in range(group):
            o_ref[i, :up_rows, :] = up[i * up_rows : (i + 1) * up_rows]

        @pl.when(step == 0)
        def _():
            for copy in order[left + 1 :]:
                copy.wait()

        down = product(a_ref[...], g_ref[...], 0, 0).astype(BF)
        for i in range(group):
            o_ref[i, up_rows:, :] = down[i * down_rows : (i + 1) * down_rows]
        result = product(r_ref[...], down_ref[...].reshape(ff, width), 1, 0)

        @pl.when(step < near)
        def _():
            keep_ref[...] = result

        @pl.when(step >= near)
        def _():
            send_ref[...] = result.astype(BF)

    return pl.pallas_call(
        kernel,
        grid=(steps,),
        out_shape=(
            jax.ShapeDtypeStruct((parts, up_rows + down_rows, width), BF),
            jax.ShapeDtypeStruct((total // 2, width), F32),
            jax.ShapeDtypeStruct((total // 2, width), BF),
        ),
        in_specs=any_refs(count + 2)
        + [
            pl.BlockSpec((total, group * down_rows), lambda i: (0, i)),
            pl.BlockSpec((tall, ff), lambda i: (i, 0)),
        ],
        out_specs=(
            pl.BlockSpec((group, up_rows + down_rows, width), lambda i: (i, 0, 0)),
            pl.BlockSpec((tall, width), lambda i: (jnp.minimum(i, near - 1), 0)),
            pl.BlockSpec((tall, width), lambda i: (jnp.maximum(i - near, 0), 0)),
        ),
        scratch_shapes=[
            pltpu.VMEM((total, width), BF),
            pltpu.VMEM((total, width), BF),
            pltpu.VMEM((total, ff), BF),
            pltpu.VMEM((parts, down_rows, width), BF),
            pltpu.SemaphoreType.DMA((count + 2,)),
        ],
        cost_estimate=pl.CostEstimate(
            flops=6 * total * width * ff,
            bytes_accessed=2 * (2 * total * (width + ff) + 2 * width * ff),
            transcendentals=0,
        ),
        name="feed_forward_weights",
    )(*sources, grad_hidden, weights, active, active)


def own_time_features(times, first_col, col_count, model_width):
    half_width = model_width // 2
    cols = first_col + jnp.arange(col_count, dtype=jnp.int32)
    is_sine = cols < half_width
    steps_row = jnp.where(is_sine, cols, cols - half_width).astype(F32)
    frequency = jnp.exp(steps_row * (-math.log(10000.0) / (half_width - 1)))
    phase_arg = 1000.0 * times[:, None] * frequency[None, :]
    features = jnp.where(is_sine[None, :], jnp.sin(phase_arg), jnp.cos(phase_arg))
    return jax.nn.silu(features).astype(BF)


def pad_rows(vector):
    rows = -(-vector.shape[-1] // LANES)
    return jnp.pad(vector, (0, rows * LANES - vector.shape[-1])).reshape(rows, LANES)


def body(
    frames,
    skip_frames,
    lengths,
    flow_time,
    skip_weight,
    adaln_weight,
    adaln_bias,
    qkv_weight,
    qkv_bias,
    output_weight,
    output_bias,
    up_weight,
    up_bias,
    down_weight,
    down_bias,
    out_grad,
):
    n_u, n_s = lax.axis_size("utt"), lax.axis_size("sp")
    u, s = lax.axis_index("utt"), lax.axis_index("sp")
    n_all = n_u * n_s
    me = u * n_s + s
    rows, width = frames.shape
    per_group = lengths.shape[1]
    ff = up_weight.shape[1]
    part_width = width // n_s
    part_ff = ff // n_s
    lengths_row = lengths[0]

    all_ids = jnp.concatenate(
        [(s ^ d) * rows + jnp.arange(rows, dtype=jnp.int32) for d in block_order(n_s)]
    )
    inside_all, segment_all, position_all = utterance_layout(lengths_row, all_ids)
    inside = inside_all[:rows]

    cols = qkv_weight.shape[0]
    slot, out_slot = skip_weight.shape[0], output_weight.shape[0]
    far = n_s // 2
    bias_sizes = [qkv_bias.shape[0], output_bias.shape[0], up_bias.shape[0], down_bias.shape[0]]
    bias_own = pad_rows(
        jnp.concatenate([qkv_bias, output_bias, up_bias, down_bias]).astype(F32)
    )
    qkv_split = qkv_weight.reshape(cols, 3, n_s, part_width).transpose(2, 0, 1, 3)
    up_split = up_weight.reshape(cols, n_u, n_s, ff // n_all).transpose(2, 0, 1, 3)
    both_split = jnp.concatenate(
        [qkv_split.reshape(n_s, cols, 3 * part_width), up_split.reshape(n_s, cols, part_ff)], axis=2
    )
    skip_blocks = line_blocks(skip_weight)
    flow_row = jnp.pad(flow_time, ((0, 0), (0, LANES - per_group)))
    first_rows = jnp.concatenate([flow_row, bias_own], axis=0)
    both_mine = lax.all_to_all(both_split, "sp", 0, 0, tiled=True)
    first_rows = lax.all_to_all(
        jnp.broadcast_to(after(first_rows, both_mine)[None], (n_u,) + first_rows.shape),
        "utt",
        0,
        0,
        tiled=True,
    )
    part = n_u * slot
    chosen = jnp.arange(2 * width, dtype=jnp.int32)
    chosen = chosen % part // slot * (slot * n_s) + chosen // part * slot + chosen % slot
    selection = (jnp.arange(2 * width, dtype=jnp.int32)[:, None] == chosen[None, :]).astype(BF)
    joined_split = dot32(jnp.concatenate([frames, skip_frames], axis=1), selection).astype(BF)
    joined_split = joined_split.reshape(rows, n_s, part).transpose(1, 0, 2)
    joined_sent = far_entries(joined_split)
    skip_blocks, both_mine, joined_split, joined_sent = fence(
        (skip_blocks, both_mine, joined_split, joined_sent)
    )
    skip_line = jnp.concatenate(skip_blocks, axis=0)
    both_mine = both_mine.reshape(n_s * cols, -1)
    my_qkv = lax.all_gather(both_mine[:, : 3 * part_width], "utt", axis=0, tiled=True)
    ff_lines = lax.all_gather(
        jnp.concatenate([both_mine[:, 3 * part_width :], down_weight], axis=0), "utt", axis=0
    )

    times = first_rows[:, 0, :per_group].reshape(n_u * per_group)
    feature_rows = adaln_weight.shape[0]
    silu_own = own_time_features(times, me * feature_rows, feature_rows, width)
    table_width = adaln_weight.shape[1]
    mod_terms = dot32(silu_own, adaln_weight)
    bias_cols = lax.dynamic_update_slice(
        jnp.zeros((table_width,), F32), adaln_bias.astype(F32), (me * adaln_bias.shape[0],)
    )
    mod_terms = (mod_terms + bias_cols[None, :]).reshape(n_u, per_group, 6, width)
    mod_terms = mod_terms.transpose(0, 2, 1, 3).reshape(n_u, 6 * per_group, width)

    high, half = skip_line.shape[0] // slot, slot // 2
    rows_of = lambda x: x.reshape(high, slot, width)
    over_sp, over_utt = xor_sp(skip_line, far), swap_utt(skip_line)
    near_line = xor_sp(skip_line, 1)
    mod_terms = lax.all_to_all(mod_terms, "utt", 0, 0, tiled=True)
    cosine, sine = rotary_tables(position_all)
    over_sp, over_utt, near_line, cosine, sine = fence(
        (over_sp, over_utt, near_line, cosine, sine)
    )
    top = xor_sp(rows_of(over_utt)[:, :half].reshape(high * half, width), far)
    bottom = swap_utt(rows_of(over_sp)[:, half:].reshape(high * half, width))
    near_sp, near_utt = xor_sp(over_sp, 1), xor_sp(over_utt, 1)
    table_rows = 6 * per_group
    bias_own = first_rows[:, 1:].reshape(-1, width)
    top, bottom, near_sp, near_utt, mod_terms = fence((top, bottom, near_sp, near_utt, mod_terms))
    corner = jnp.concatenate([top, bottom], axis=0)
    message = jnp.concatenate([jnp.sum(mod_terms, axis=0), bias_own], axis=0)
    corner, message, joined_sent = fence((corner, message, joined_sent))
    output_blocks = lax.all_to_all(
        jnp.broadcast_to(after(output_weight, corner)[None], (n_u, out_slot, width)),
        "utt",
        0,
        0,
        tiled=True,
    ).reshape(n_u * out_slot, width)
    near_corner, message_far = fence((xor_sp(corner, 1), xor_sp(message, far)))
    joined_far = xor_sp(joined_sent, far)
    message = jnp.concatenate(
        [message[:table_rows] + message_far[:table_rows], bias_own, message_far[table_rows:]], axis=0
    )
    message_near = xor_sp(message, 1)
    mod_table = message[:table_rows] + message_near[:table_rows]
    bias_blocks = [
        m.reshape(2, n_u, -1)[i]
        for m in (message[table_rows:], message_near[table_rows:])
        for i in range(2)
    ]
    here, there = line_indices(False), line_indices(True)
    skip_pieces = Pieces()
    whole_row = lambda i, distance: (i * n_s + (s ^ distance)) * slot
    for array, owners, distance in (
        (skip_line, here, 0),
        (over_sp, here, far),
        (over_utt, there, 0),
        (near_line, here, 1),
        (near_sp, here, far ^ 1),
        (near_utt, there, 1),
    ):
        skip_pieces.add(array, [whole_row(i, distance) for i in owners], slot)
    for array, distance in ((corner, far), (near_corner, far ^ 1)):
        skip_pieces.add(
            array,
            [whole_row(i, distance) for i in there]
            + [whole_row(i, distance) + half for i in there],
            half,
        )

    def segment_sums(values):
        return jnp.stack(
            [jnp.sum(jnp.where(inside[:, k][:, None], values, 0.0), axis=0) for k in range(per_group)]
        )

    full_skip, base_rows = placed_product([frames, skip_frames], skip_pieces, 2 * width)
    base_rows, mod_table, joined_far = fence((base_rows, mod_table, joined_far))

    def expand(block, segment):
        table = mod_table[block * per_group : (block + 1) * per_group]
        result = table[per_group - 1][None, :]
        for k in range(per_group - 2, -1, -1):
            result = jnp.where(segment[:, None] == k, table[k][None, :], result)
        return result

    segment_own = segment_all[:rows]
    scale_attn, gate_attn, shift_ffn, scale_ffn, gate_ffn = [
        expand(i, segment_own) for i in range(1, 6)
    ]
    grad_out = out_grad.astype(F32)
    grad_result = (gate_ffn * grad_out).astype(BF)
    base_norm, base_scale = norm_parts(base_rows)
    normed = (base_norm * (1.0 + scale_attn) + expand(0, segment_own)).astype(BF)
    far_normed = xor_sp(normed, far)
    far_normed, output_blocks, my_qkv, grad_result = fence(
        (far_normed, output_blocks, my_qkv, grad_result)
    )
    grad_result_far = xor_sp(grad_result, far)
    two_normed = jnp.concatenate([normed, far_normed], axis=0)
    near_normed = xor_sp(two_normed, 1)
    joined_mine = exchange_near(joined_split, joined_far)
    near_normed, joined_mine = fence((near_normed, joined_mine))
    output_far = xor_sp(output_blocks, far)
    bias_all = jnp.stack(in_device_order(bias_blocks), axis=1).reshape(n_u, n_s, -1)
    offsets = [0]
    for size in bias_sizes:
        offsets.append(offsets[-1] + size)
    full_qkv_bias, full_output_bias, full_up_bias, full_down_bias = [
        bias_all[:, :, offsets[i] : offsets[i + 1]].reshape(-1) for i in range(4)
    ]
    my_qkv_bias = lax.dynamic_slice_in_dim(
        full_qkv_bias.reshape(3, width), s * part_width, part_width, 1
    ).reshape(-1)
    my_up_bias = lax.dynamic_index_in_dim(
        full_up_bias.reshape(n_u, n_s, -1), s, 1, keepdims=False
    ).reshape(-1)

    normed_all, query_rows, key_rows, value_rows, attended_heads, log_totals = attend(
        [two_normed, near_normed], my_qkv, my_qkv_bias, cosine, sine, segment_all
    )
    attended_heads, output_far, grad_result_far = fence(
        (attended_heads, output_far, grad_result_far)
    )
    arrived = exchange_sp([attended_heads[i * rows : (i + 1) * rows] for i in range(n_s)])
    output_near = xor_sp(jnp.concatenate([output_blocks, output_far], axis=0), 1)
    grad_result_near = xor_sp(jnp.concatenate([grad_result, grad_result_far], axis=0), 1)
    arrived, output_near, grad_result_near = fence((arrived, output_near, grad_result_near))
    output_pieces = whole_pieces(
        [
            (output_blocks, 0, range(n_u), 0, out_slot),
            (output_far, far, range(n_u), 0, out_slot),
        ],
        out_slot,
    )
    output_pieces.add(
        output_near,
        [(i * n_s + (s ^ 1)) * out_slot for i in range(n_u)]
        + [(i * n_s + (s ^ 1 ^ far)) * out_slot for i in range(n_u)],
        out_slot,
    )
    attended = jnp.concatenate(in_device_order(arrived), axis=1)
    full_output, branch = placed_product([attended], output_pieces, width)
    branch = branch + full_output_bias[None, :]
    middle = base_rows + gate_attn * branch
    middle_norm, middle_scale = norm_parts(middle)
    normed_ffn = (middle_norm * (1.0 + scale_ffn) + shift_ffn).astype(BF)

    half_rows = n_s * rows // 2
    far_ffn = xor_sp(normed_ffn, far)
    two_ffn = jnp.concatenate([normed_ffn, far_ffn], axis=0)
    near_ffn = xor_sp(two_ffn, 1)
    ffn_blocks = [two_ffn, near_ffn]
    grad_result_blocks = [grad_result, grad_result_far, grad_result_near]
    active, grad_hidden, grad_up_bias, kept, sent = feed_forward(
        ffn_blocks, grad_result_blocks, ff_lines, my_up_bias, n_s * cols
    )
    arrived = xor_sp(sent, 1)
    far_sent = (kept[rows:] + arrived[rows:].astype(F32)).astype(BF)
    far_sent, active, grad_hidden = fence((far_sent, active, grad_hidden))
    far_sum = xor_sp(far_sent, n_s // 2)

    ff_grads, result_kept, sent = feed_forward_weights(
        ffn_blocks, grad_hidden, active, grad_result_blocks, ff_lines, n_s * cols
    )
    far_sum, result_kept, sent, ff_grads = fence((far_sum, result_kept, sent, ff_grads))
    grad_normed_ffn = kept[:rows] + arrived[:rows].astype(F32) + far_sum.astype(F32)
    ff_mine = lax.psum_scatter(ff_grads, "utt", scatter_dimension=0, tiled=True)[0]
    grad_middle = grad_out + norm_back(
        middle_norm, middle_scale, grad_normed_ffn * (1.0 + scale_ffn)
    )
    grad_branch = (gate_attn * grad_middle).astype(BF)
    grad_attended = dot_nt(grad_branch, full_output).astype(BF)
    grad_heads = exchange_sp(
        [
            lax.dynamic_slice_in_dim(grad_attended, (s ^ d) * part_width, part_width, 1)
            for d in block_order(n_s)
        ]
    )
    result_arrived = xor_sp(after(sent, grad_attended), 1)
    grad_heads, result_arrived, grad_branch = fence((grad_heads, result_arrived, grad_branch))
    far_branch = xor_sp(grad_branch, far)
    result_sent = (result_kept[rows:] + result_arrived[rows:].astype(F32)).astype(BF)

    grad_projected = attend_back(
        query_rows, key_rows, value_rows, grad_heads, log_totals, cosine, sine, segment_all
    )
    grad_projected, far_branch = fence((grad_projected, far_branch))
    sent = product(grad_projected[half_rows:], my_qkv, 1, 1).astype(BF)
    kept = product(grad_projected[:half_rows], my_qkv, 1, 1)
    arrived = xor_sp(sent, 1)
    far_sent = (kept[rows:] + arrived[rows:].astype(F32)).astype(BF)
    far_sent, projected_late, far_branch, middle_late, nffn_late = fence(
        (far_sent, grad_projected, far_branch, grad_middle, grad_normed_ffn)
    )
    far_sum = xor_sp(far_sent, far)

    grad_qkv = dot_tn(normed_all, projected_late).astype(BF)
    my_qkv_bias_grad = jnp.sum(projected_late.astype(F32), axis=0)
    qkv_keep, qkv_send = split_pair(grad_qkv.reshape(-1, 2, n_s * cols, 3 * part_width), 1)
    qkv_arrived = swap_utt(qkv_send)
    branch_blocks, step = [grad_branch, far_branch], n_s // 4
    while step >= 1:
        branch_blocks = branch_blocks + [xor_sp(b, step) for b in branch_blocks]
        step //= 2
    grad_output = dot_tn(attended_heads, jnp.concatenate(branch_blocks, axis=0)).astype(BF)
    grad_output_bias = jnp.sum((gate_attn * middle_late).astype(BF).astype(F32), axis=0)
    early_tables = [
        segment_sums(v) for v in (middle_late * branch, nffn_late, nffn_late * middle_norm)
    ]
    far_sum, early_tables, qkv_keep, qkv_arrived, grad_output = fence(
        (far_sum, early_tables, qkv_keep, qkv_arrived, grad_output)
    )
    grad_normed = kept[:rows] + arrived[:rows].astype(F32) + far_sum.astype(F32)

    grad_base = (
        grad_middle + norm_back(base_norm, base_scale, grad_normed * (1.0 + scale_attn))
    ).astype(BF)
    far_base = xor_sp(grad_base, far)
    out_keep, out_send = split_pair(grad_output.reshape(-1, 2, out_slot, width), 1)
    out_arrived = swap_utt(out_send)
    far_base, normed_late, out_arrived = fence((far_base, grad_normed, out_arrived))
    out_half = (out_keep.astype(F32) + out_arrived.astype(F32)).astype(BF)
    two_base = jnp.concatenate([grad_base, far_base], axis=0)
    near_base = xor_sp(two_base, 1)
    grad_skip = dot_tn(
        jnp.concatenate(joined_mine, axis=0), jnp.concatenate([two_base, near_base], axis=0)
    ).astype(BF)
    skip_keep, skip_send = split_pair(grad_skip.reshape((-1, 2) + (slot, width)), 1)
    skip_send, out_half, base_late, normed_late, result_sent, late_grad = fence(
        (skip_send, out_half, grad_base, normed_late, result_sent, out_grad)
    )

    skip_arrived, far_result = swap_utt(skip_send), xor_sp(result_sent, far)
    frames_grad = dot_nt(base_late, full_skip[:width])
    skip_grad = dot_nt(base_late, full_skip[width:])
    late_tables = [segment_sums(v) for v in (normed_late, normed_late * base_norm)]
    skip_arrived, far_result, late_tables, frames_grad, skip_grad, qkv_keep, ff_mine = fence(
        (skip_arrived, far_result, late_tables, frames_grad, skip_grad, qkv_keep, ff_mine)
    )
    qkv_half = (qkv_keep.astype(F32) + qkv_arrived.astype(F32)).astype(BF)
    grad_out = late_grad.astype(F32)
    result = (
        result_kept[:rows]
        + result_arrived[:rows].astype(F32)
        + far_result.astype(F32)
        + full_down_bias[None, :]
    )
    skip_half = (skip_keep.astype(F32) + skip_arrived.astype(F32)).astype(BF)
    skip_half, qkv_half = fence((skip_half, qkv_half))

    skip_terms, qkv_terms = scatter_slow(skip_half), scatter_slow(qkv_half)
    mixed_out = (middle + gate_ffn * result).astype(BF)
    grad_down_bias = jnp.sum((gate_ffn * grad_out).astype(BF).astype(F32), axis=0)
    gate_table = segment_sums(grad_out * result)
    skip_sum = add_terms(skip_terms)
    qkv_mine = add_terms(qkv_terms).astype(BF)
    qkv_mine = qkv_mine.reshape(n_s, cols, 3 * part_width)
    out_sum = to_owner(add_terms(scatter_slow(out_half)))
    qkv_back = split_exchange_sp(qkv_mine)
    qkv_sum = (
        qkv_back.reshape(n_s, cols, 3, part_width).transpose(1, 2, 0, 3).reshape(cols, 3 * width)
    ).astype(F32)
    up_back = split_exchange_sp(ff_mine[: n_s * cols].reshape(n_s, cols, part_ff))
    up_sum = (
        up_back.reshape(n_s, cols, n_u, ff // n_all).transpose(1, 2, 0, 3).reshape(cols, ff)
    ).astype(F32)
    down_sum = ff_mine[n_s * cols :].astype(F32)

    grad_table = jnp.concatenate(late_tables + early_tables + [gate_table], axis=1)
    qkv_bias_slots = lax.dynamic_update_slice(
        jnp.zeros((3, width), F32), my_qkv_bias_grad.reshape(3, part_width), (0, s * part_width)
    ).reshape(-1)
    up_bias_slots = lax.dynamic_update_slice(
        jnp.zeros((n_u, n_s, ff // n_all), F32),
        grad_up_bias.reshape(n_u, 1, ff // n_all),
        (0, s, 0),
    ).reshape(-1)
    bias_vec = jnp.concatenate(
        [
            v.reshape(n_u, -1)
            for v in (qkv_bias_slots, grad_output_bias, up_bias_slots, grad_down_bias)
        ],
        axis=1,
    )
    vec_rows = -(-bias_vec.shape[1] // LANES)
    bias_vec = jnp.pad(bias_vec, ((0, 0), (0, vec_rows * LANES - bias_vec.shape[1])))
    table_rows = per_group * table_width // LANES
    tail = jnp.concatenate(
        [grad_table.reshape(table_rows, LANES), bias_vec.reshape(n_u * vec_rows, LANES)], axis=0
    )
    tail = sum_sp(tail)
    tail = jnp.concatenate(
        [
            jnp.broadcast_to(tail[None, :table_rows], (n_u, table_rows, LANES)),
            tail[table_rows:].reshape(n_u, vec_rows, LANES),
        ],
        axis=1,
    )
    tail = tail.astype(BF)
    tail = lax.all_to_all(tail, "utt", 0, 0, tiled=True).astype(F32)
    table_all = tail[:, :table_rows].reshape(n_u * per_group, table_width)
    adaln_sum = lax.dot_general(
        silu_own.astype(F32),
        table_all,
        (((0,), (0,)), ((), ())),
        precision=highest_precision,
        preferred_element_type=F32,
    )
    adaln_bias_sum = jnp.sum(owned(table_all), axis=0)
    vec = jnp.sum(tail[:, table_rows:], axis=0).reshape(-1)
    bias_sums, start = [], 0
    for size in bias_sizes:
        bias_sums.append(lax.dynamic_slice_in_dim(vec, start + s * size, size, 0))
        start += size * n_s

    return (
        mixed_out,
        frames_grad,
        skip_grad,
        skip_sum,
        adaln_sum,
        adaln_bias_sum,
        qkv_sum,
        bias_sums[0],
        out_sum,
        bias_sums[1],
        up_sum,
        bias_sums[2],
        down_sum,
        bias_sums[3],
    )


def solution(mesh):
    both = ("utt", "sp")
    matrix, vector, group = P(both, None), P(both), P("utt", None)
    return jax.shard_map(
        body,
        mesh=mesh,
        in_specs=(
            matrix,
            matrix,
            group,
            group,
            matrix,
            matrix,
            vector,
            matrix,
            vector,
            matrix,
            vector,
            matrix,
            vector,
            matrix,
            vector,
            matrix,
        ),
        out_specs=(
            matrix,
            matrix,
            matrix,
            matrix,
            matrix,
            vector,
            matrix,
            vector,
            matrix,
            vector,
            matrix,
            vector,
            matrix,
            vector,
        ),
        check_vma=False,
    )
```
